32 devices in a mesh: dp: 16 (over z, y, x), head: 2 (over core).
Axes of the slice: x: 2, y: 2, z: 4, core: 2. Of those that a mesh axis runs over, the one named last changes fastest.
Arguments:
- tokens: bfloat16 [8192, 768], P(('dp', 'head')), may hold values from -6 to 6
- w_query: float32 [768, 768], P('dp', 'head'), may hold values from -0.3125 to 0.3125
- w_key: float32 [768, 768], P('dp', 'head'), may hold values from -0.3125 to 0.3125
- w_value: float32 [768, 768], P('dp', 'head'), may hold values from -0.21875 to 0.21875
- w_out: float32 [768, 768], P(('dp', 'head')), may hold values from -0.875 to 0.875
- gain_attn: float32 [768], P(('dp', 'head')), may hold values from 0.5 to 1.5
- bias_attn: float32 [768], P(('dp', 'head')), may hold values from -0.5 to 0.5
- w_up: float32 [768, 3072], P(None, ('dp', 'head')), may hold values from -0.21875 to 0.21875
- w_down: float32 [3072, 768], P(('dp', 'head')), may hold values from -0.109375 to 0.109375
- gain_ffn: float32 [768], P(('dp', 'head')), may hold values from 0.5 to 1.5
- bias_ffn: float32 [768], P(('dp', 'head')), may hold values from -0.5 to 0.5
- seq_lengths: int32 [16, 8], P('dp'), may hold values from 0 to 512, as said below
- seq_offsets: int32 [16, 8], P('dp'), may hold values from 0 to 512, as said below
- out_grad: bfloat16 [8192, 768], P(('dp', 'head')), may hold values from -6 to 6
Outputs:
- output: bfloat16 [8192, 768], P(('dp', 'head'))
- input_grad: bfloat16 [8192, 768], P(('dp', 'head'))
- grad_w_query: float32 [768, 768], P('dp', 'head')
- grad_w_key: float32 [768, 768], P('dp', 'head')
- grad_w_value: float32 [768, 768], P('dp', 'head')
- grad_w_out: float32 [768, 768], P(('dp', 'head'))
- grad_gain_attn: float32 [768], P(('dp', 'head'))
- grad_bias_attn: float32 [768], P(('dp', 'head'))
- grad_w_up: float32 [768, 3072], P(None, ('dp', 'head'))
- grad_w_down: float32 [3072, 768], P(('dp', 'head'))
- grad_gain_ffn: float32 [768], P(('dp', 'head'))
- grad_bias_ffn: float32 [768], P(('dp', 'head'))
The draws below stay inside these ranges and needn't reach their ends.
Inputs may be any that keep to these rules, and one draw needn't show every extreme that they name: Slot j of bin b holds a sequence of seq_lengths[b, j] rows, 0 marking an empty slot; the lengths of a bin sum to at most 512. The sequence in slot j of bin b takes rows seq_offsets[b, j] to seq_offsets[b, j] + seq_lengths[b, j] - 1 of that bin; the sequences of a bin do not intersect; rows that no sequence takes are padding.
All inputs are finite; a program needn't handle non-finite values.
Results may differ from the reference program's by a relative error of at most 0.017.
The reference program's roundings to bfloat16 on the way count: a program that leaves them out, or rounds other values in their place, can miss the bound.
Values may be sent and summed in bfloat16 or wider, within the bound.
A program may use at most 128 MiB of HBM per device.

```python
import math
import jax
import jax.numpy as jnp
from jax import lax

D = 768
HEADS = 12
FF = 3072
HD = 64
BIN = 512
SLOTS = 8
BINS = 16
TOKENS = 8192


def packing(key):
    mixed_key = jax.random.fold_in(key, 11)
    cut_key, keep_key, pad_key = jax.random.split(mixed_key, 3)
    cut_points = jax.random.randint(cut_key, (BINS, SLOTS - 1), 1, BIN)
    keep_flags = jax.random.randint(keep_key, (BINS, SLOTS - 1), 0, 2)
    padding = jax.random.randint(pad_key, (BINS, 1), 0, BIN // 32 + 1)
    single = (jnp.arange(BINS, dtype=jnp.int32) % 8 == 3)[:, None]
    filled = jnp.where(single, BIN, BIN - padding).astype(jnp.int32)
    bounds = jnp.where((keep_flags == 1) & jnp.logical_not(single), jnp.minimum(cut_points, filled), filled)
    bounds = jnp.sort(bounds, axis=1)
    starts = jnp.concatenate([jnp.zeros((BINS, 1), jnp.int32), bounds], axis=1)
    finish = jnp.concatenate([bounds, filled], axis=1)
    return ((finish - starts).astype(jnp.int32), starts.astype(jnp.int32))


def draw_seq_lengths(key, part):
    return packing(key)[0]


def draw_seq_offsets(key, part):
    return packing(key)[1]


def with_spikes(values, rng, source, target, blocks, factor):
    owner, partner = [(jnp.arange(values.shape[axis_at]) // (values.shape[axis_at] // blocks)).reshape([-1 if axis == axis_at else 1 for axis in range(values.ndim)]) for axis_at in (source, target)]
    chosen = jax.random.permutation(rng, blocks)[partner]
    strong = (owner == chosen) | (owner == (partner + blocks // 2) % blocks)
    return jnp.where(strong, factor * values, values)


def level_of(stream_key, extent, cuts, least, largest):
    gain, own = 1.0, jax.random.fold_in(stream_key, 6)
    for axis_at, parts in cuts:
        draws = jnp.exp(jax.random.uniform(jax.random.fold_in(own, axis_at), (parts,), jnp.float32, least / len(cuts), largest / len(cuts)))
        gain = gain * jnp.repeat(draws, extent[axis_at] // parts).reshape([-1 if axis == axis_at else 1 for axis in range(len(extent))])
    return gain


def scatter_about(stream_key, shape, scale, bound, cuts=(), kind=jnp.bfloat16):
    gain = level_of(stream_key, shape, cuts, -0.22, 0.18) if cuts else 1.0
    values = jax.random.normal(stream_key, shape, jnp.float32) * scale * gain
    return jnp.minimum(jnp.maximum(values, -bound), bound).astype(kind)


def noise_with(key, extent, width, reach, cuts, heavy, kind=jnp.bfloat16):
    drawn = width * jax.random.normal(key, extent, jnp.float32)
    if cuts:
        drawn = drawn * level_of(key, extent, cuts, -0.22, 0.18)
    return jnp.clip(with_spikes(drawn, jax.random.fold_in(key, 3), *heavy), -reach, reach).astype(kind)


def setup_inputs(seed: int = 0) -> dict:
    splits = jax.random.split(jax.random.key(seed), 15)
    return {
        "tokens": noise_with(splits[0], (TOKENS, D), 1.0, 6.0, ((0, 32),), (0, 1, 32, 2.75)),
        "w_query": scatter_about(splits[1], (D, D), (D // 2) ** -0.5, 0.3125, ((0, 16), (1, 2)), jnp.float32),
        "w_key": scatter_about(splits[2], (D, D), (D // 2) ** -0.5, 0.3125, ((0, 16), (1, 2)), jnp.float32),
        "w_value": scatter_about(splits[3], (D, D), D ** -0.5, 0.21875, ((0, 16), (1, 2)), jnp.float32),
        "w_out": scatter_about(splits[4], (D, D), (D // 16) ** -0.5, 0.875, ((0, 32),), jnp.float32),
        "gain_attn": jnp.clip(1.0 + 0.1 * jax.random.normal(splits[5], (D,), jnp.float32), 0.5, 1.5),
        "bias_attn": jnp.clip(jax.random.uniform(splits[6], (D,), jnp.float32, -0.5, 0.5) * level_of(splits[6], (D,), ((0, 32),), -0.4, 0.0), -0.5, 0.5),
        "w_up": scatter_about(splits[7], (D, FF), D ** -0.5, 0.21875, ((1, 32),), jnp.float32),
        "w_down": scatter_about(splits[8], (FF, D), FF ** -0.5, 0.109375, ((0, 32),), jnp.float32),
        "gain_ffn": jnp.clip(1.0 + 0.1 * jax.random.normal(splits[9], (D,), jnp.float32), 0.5, 1.5),
        "bias_ffn": jnp.clip(jax.random.uniform(splits[10], (D,), jnp.float32, -0.5, 0.5) * level_of(splits[10], (D,), ((0, 32),), -0.4, 0.0), -0.5, 0.5),
        "seq_lengths": draw_seq_lengths(jax.random.fold_in(splits[14], 71), 0),
        "seq_offsets": draw_seq_offsets(jax.random.fold_in(splits[14], 71), 0),
        "out_grad": scatter_about(splits[13], (TOKENS, D), 1.0, 6.0, ((0, 32),)),
    }


@jax.custom_vjp
def low(v):
    return lax.optimization_barrier(v.astype(jnp.bfloat16)).astype(jnp.float32)

@jax.custom_vjp
def low_back(v):
    return v

def low_keep(v):
    return (low(v), None)

def low_pass(kept, grad):
    return (grad,)

def back_keep(v):
    return (v, None)

def back_low(kept, grad):
    return (low(grad),)
low.defvjp(low_keep, low_pass)
low_back.defvjp(back_keep, back_low)

def labels_of(lengths, offsets):
    position = jnp.arange(BIN, dtype=jnp.int32)[:, None]
    starts = offsets[None, :].astype(jnp.int32)
    inside = (position >= starts) & (position < starts + lengths[None, :].astype(jnp.int32))
    slot_order = jnp.arange(1, SLOTS + 1, dtype=jnp.int32)[None, :]
    return lax.optimization_barrier(jnp.sum(jnp.where(inside, slot_order, 0), axis=1)).astype(jnp.int32)

def layer_norm(operand, gain_vec, bias_vec):
    row_mean = lax.optimization_barrier(jnp.mean(operand, axis=-1, keepdims=True))
    centered = operand - row_mean
    variance = lax.optimization_barrier(jnp.mean(centered * centered, axis=-1, keepdims=True))
    return centered * lax.rsqrt(variance + 1e-12) * gain_vec + bias_vec

def attend_bin(pieces):
    queries, key_rows, value_rows, labels_bin = pieces
    highest = lax.Precision.HIGHEST
    scores = jnp.einsum('qhd,khd->hqk', queries, key_rows, precision=highest) * (1.0 / math.sqrt(HD))
    scores = low_back(scores)
    allowed = ((labels_bin[:, None] == labels_bin[None, :]) & (labels_bin[:, None] > 0))[None]
    live_rows = (labels_bin > 0)[None, :, None]
    row_top = lax.optimization_barrier(jnp.max(jnp.where(allowed, scores, -1e+30), axis=2, keepdims=True))
    row_top = jnp.where(live_rows, row_top, 0.0)
    weights = jnp.where(allowed, jnp.exp(jnp.where(allowed, scores - row_top, 0.0)), 0.0)
    denominator = lax.optimization_barrier(jnp.sum(weights, axis=2, keepdims=True)) + jnp.where(live_rows, 0.0, 1.0)
    probability = low(weights / denominator)
    return jnp.einsum('hqk,khd->qhd', probability, value_rows, precision=highest)

def layer(tokens, params, labels):
    w_query, w_key, w_value, w_out, gain_attn, bias_attn, w_up, w_down, gain_ffn, bias_ffn = [low(param) for param in params]
    row_count = tokens.shape[0]
    bin_count = row_count // BIN
    highest = lax.Precision.HIGHEST

    def project(weight):
        projected = jnp.dot(tokens, weight, precision=highest, preferred_element_type=jnp.float32)
        return low(low_back(projected)).reshape(bin_count, BIN, HEADS, HD)
    queries = project(w_query)
    key_rows = project(w_key)
    value_rows = project(w_value)
    attended = lax.map(jax.checkpoint(attend_bin), (queries, key_rows, value_rows, labels))
    attended = low(low_back(attended.reshape(row_count, D)))
    branch = low_back(jnp.dot(attended, w_out, precision=highest, preferred_element_type=jnp.float32))
    normed = layer_norm(tokens + branch, gain_attn, bias_attn)
    pre_act = low_back(jnp.dot(low(normed), w_up, precision=highest, preferred_element_type=jnp.float32))
    hidden = low(jax.nn.gelu(pre_act, approximate=False))
    second = normed + low_back(jnp.dot(hidden, w_down, precision=highest, preferred_element_type=jnp.float32))
    return layer_norm(second, gain_ffn, bias_ffn)

def reference(tokens, w_query, w_key, w_value, w_out, gain_attn, bias_attn, w_up, w_down, gain_ffn, bias_ffn, seq_lengths, seq_offsets, out_grad):
    params = (w_query, w_key, w_value, w_out, gain_attn, bias_attn, w_up, w_down, gain_ffn, bias_ffn)
    per_step = 8 if BINS % 8 == 0 else 1
    step_count = BINS // per_step
    step_rows = per_step * BIN
    inputs_all = tokens.astype(jnp.float32).reshape(step_count, step_rows, D)
    cotangents = out_grad.astype(jnp.float32).reshape(step_count, step_rows, D)
    lengths_all = seq_lengths.reshape(step_count, per_step, SLOTS)
    offsets_all = seq_offsets.reshape(step_count, per_step, SLOTS)

    def scan_step(grad_sums, pieces):
        block_in, block_grad, block_lengths, block_offsets = pieces
        labels = jax.vmap(labels_of)(block_lengths, block_offsets)

        def forward(operand, weights):
            return layer(operand, weights, labels)
        result, pullback = jax.vjp(forward, block_in, params)
        grad_in, grad_params = pullback(block_grad)
        grad_sums = tuple((running + increment for running, increment in zip(grad_sums, grad_params)))
        return (grad_sums, (result.astype(jnp.bfloat16), grad_in.astype(jnp.bfloat16)))
    zero_sums = tuple((jnp.zeros_like(param) for param in params))
    grad_sums, (results, grads_in) = lax.scan(scan_step, zero_sums, (inputs_all, cotangents, lengths_all, offsets_all))
    return (results.reshape(TOKENS, D), grads_in.reshape(TOKENS, D), grad_sums[0], grad_sums[1], grad_sums[2], grad_sums[3], grad_sums[4], grad_sums[5], grad_sums[6], grad_sums[7], grad_sums[8], grad_sums[9])
```

```python
import functools
import math
import types

import jax
import jax.numpy as jnp
from jax import lax
from jax.experimental import pallas as pl
from jax.experimental.pallas import tpu as pltpu
from jax.sharding import PartitionSpec as P

HD = 64
BIN = 512
EPS = 1e-12
F32 = jnp.float32
BF = jnp.bfloat16
MESH = pl.DeviceIdType.MESH

MU, MV = 2, 1
ROWS = {"Q": 48, "O": 48, "U": 96, "D": 96}
COLS = {"Q": 1152, "O": 384, "U": 768, "D": 768}
APART = {"Q": 32, "O": 32, "U": 64, "D": 64}
PIECES = ("Q", "O", "U", "D")
PER_PIECE = ("G", "S1", "R1", "S2A", "R2A", "S3A", "R3A", "S2C", "R2C", "S3C", "R3C")
DP, HEAD = "dp", "head"
BOTH = (DP, HEAD)


def mm(a, b, ca=1, cb=0):
    return lax.dot_general(a, b, (((ca,), (cb,)), ((), ())), preferred_element_type=F32)


def scratch_list():
    items = []

    def add(name, shape, dtype):
        items.append((name, pltpu.VMEM(shape, dtype)))

    add("X", (512, 768), BF)
    add("WQ", (768, 1152), BF)
    add("WOP", (2, 768, 384), BF)
    add("WO", (768, 768), BF)
    add("WU", (1536, 768), BF)
    add("WD", (1536, 768), BF)
    for n in ("Q3", "K3", "V3", "ATT", "GA", "DQ", "DK", "DV"):
        add(n, (3, 512, 128), BF)
    add("ATTR", (3, 256, 128), BF)
    add("GAS", (3, 256, 128), BF)
    add("BIAS", (512, 512), F32)
    add("LIVE", (512, 128), F32)
    add("P32", (6, 512, 512), F32)
    add("PB", (512, 512), BF)
    add("DSB", (512, 512), BF)
    add("U1", (256, 768), F32)
    add("N1", (256, 768), F32)
    add("INV1", (256, 128), F32)
    add("FIN", (512, 768), BF)
    add("HID", (4, 512, 384), BF)
    add("GEL", (4, 512, 384), F32)
    add("SEC", (512, 768), F32)
    add("SECR", (256, 768), F32)
    add("GS", (256, 768), F32)
    add("GFB", (512, 768), BF)
    add("GB", (256, 768), BF)
    add("IGS", (256, 768), BF)
    add("IGR", (256, 768), BF)
    add("T", (768, 1152), F32)
    add("S0", (768, 384), BF)
    add("R0", (768, 384), BF)
    for p in PIECES:
        r, c, a = ROWS[p], COLS[p], APART[p]
        b = r - a
        sizes = (8 * r, 8 * r, 8 * r, 4 * a, 4 * a, 3 * a, 3 * a, 6 * b, 6 * b, b, b)
        for key, size in zip(PER_PIECE, sizes):
            add(key + p, (size, c), F32 if key == "G" else BF)
    add("VS", (96, 768), F32)
    add("VR", (80, 768), F32)
    add("UT", (128, 768), F32)
    items.append(("ss", pltpu.SemaphoreType.DMA((320,))))
    items.append(("rs", pltpu.SemaphoreType.DMA((320,))))
    items.append(("ls", pltpu.SemaphoreType.DMA((4,))))
    return items


IN_NAMES = ("tok", "wq", "wk", "wv", "wo", "ga", "ba", "wu", "wd", "gf", "bf", "len", "off", "og")
OUT_NAMES = ("out", "ig", "dwq", "dwk", "dwv", "dwo", "dga", "dba", "dwu", "dwd", "dgf", "dbf")


def layer_kernel(*refs):
    names = IN_NAMES + OUT_NAMES + tuple(n for n, _ in scratch_list())
    named = dict(zip(names, refs))
    r = types.SimpleNamespace(**named)
    for key in PER_PIECE:
        setattr(r, key, {p: named[key + p] for p in PIECES})
    me = lax.axis_index(DP)
    c = lax.axis_index(HEAD)
    x = lax.rem(me, 2)
    y = lax.rem(lax.div(me, 2), 2)
    z = lax.div(me, 4)
    u = x + c * (y - x)
    v = y + c * (x - y)
    ub = 1 + c
    vb = 2 - c
    zs = (z, z + 1 - 2 * lax.rem(z, 2), lax.rem(z + 2, 4), 3 - z)

    def chip(m):
        zm, du, dv = m // 4, (m // 2) % 2, m % 2
        uu = 1 - u if du else u
        vv = 1 - v if dv else v
        return 4 * zs[zm] + ub * uu + vb * vv

    ids = [chip(m) for m in range(16)]
    partner = (me, 1 - c)
    base256, base24, other24 = 256 * c, 24 * c, 24 * (1 - c)
    own_rows = pl.ds(pl.multiple_of(256 * c, 256), 256)
    oth_rows = pl.ds(pl.multiple_of(256 * (1 - c), 256), 256)

    peers = [partner] + [(ids[m], c) for m in (MU, MV, 4, 8, 12)]
    barrier = pltpu.get_barrier_semaphore()
    for dev in peers:
        pl.semaphore_signal(barrier, inc=1, device_id=dev, device_id_type=MESH)
    pl.semaphore_wait(barrier, len(peers))

    sends = []
    recv_ids = {}

    def recv_sem(key):
        if key not in recv_ids:
            recv_ids[key] = len(recv_ids)
        return r.rs.at[recv_ids[key]]

    def send(key, src, dst, dev):
        cp = pltpu.make_async_remote_copy(
            src_ref=src,
            dst_ref=dst,
            send_sem=r.ss.at[len(sends)],
            recv_sem=recv_sem(key),
            device_id=dev,
            device_id_type=MESH,
        )
        cp.start()
        sends.append((src, dst, len(sends), key, dev))

    def wait_send(entry):
        src, dst, k, key, dev = entry
        pltpu.make_async_remote_copy(
            src_ref=src,
            dst_ref=dst,
            send_sem=r.ss.at[k],
            recv_sem=recv_sem(key),
            device_id=dev,
            device_id_type=MESH,
        ).wait_send()

    waited = set()

    def wait_sent(key):
        for entry in sends:
            if entry[3] == key:
                wait_send(entry)
                waited.add(key)

    def wait_recv(key, ref):
        pltpu.make_async_remote_copy(
            src_ref=ref,
            dst_ref=ref,
            send_sem=r.ss.at[0],
            recv_sem=recv_sem(key),
            device_id=partner,
            device_id_type=MESH,
        ).wait_recv()

    def wbuf(p):
        return {"Q": r.WQ, "O": r.WOP.at[c], "U": r.WU, "D": r.WD}[p]

    starts = {}
    for n_rows in (48, 96):
        for m in range(16):
            first = pl.multiple_of(ids[m] * n_rows, 16)
            third = pl.multiple_of(ids[m] * n_rows + 2 * n_rows // 3, 16)
            starts[n_rows, m] = (first, third)

    def wslice(p, part, m):
        a, rows = APART[p], ROWS[p]
        first, third = starts[rows, m]
        if part == "A":
            return wbuf(p).at[pl.ds(first, a), :]
        return wbuf(p).at[pl.ds(third, rows - a), :]

    def forward(p, part, m, f):
        ref = wslice(p, part, m)
        send(("ag", p, part, m ^ f), ref, ref, (ids[f], c))

    def got(p, part, m):
        wait_recv(("ag", p, part, m), wslice(p, part, m))

    def ag_own(p):
        for f in (4, 8, 12):
            forward(p, "A", 0, f)
        forward(p, "C", 0, MU)
        forward(p, "A", 0, MU)
        forward(p, "A", 0, MV)
        for f in (4, 8, 12):
            forward(p, "C", 0, f)
        forward(p, "C", 0, MV)

    def ag_steps(p):
        steps = []

        def step(part, m, flips):
            def run():
                got(p, part, m)
                for f in flips:
                    forward(p, part, m, f)

            steps.append(run)

        step("C", MU, (4, 8, 12, MV))
        step("A", MU, (MV,))
        for zz in (4, 8, 12):
            step("A", zz, (MU, MV))
        for zz in (4, 8, 12):
            step("C", zz, (MV,))
            step("C", zz + MU, (MV,))
        for zz in (4, 8, 12):
            step("A", zz + MU, (MV,))
        return steps

    def ag_plane(p, zm):
        for m in (4 * zm + MV, 4 * zm + MU + MV):
            got(p, "A", m)
            got(p, "C", m)

    def run(steps):
        for s in steps:
            s()

    vec_peer = (partner, (ids[MU], c), (ids[MV], c), (ids[4], c), (ids[8], c))

    def vec_send(k, s):
        send(("v", k, s), r.VS.at[pl.ds(48 * k + 8 * s, 8), :], r.VR.at[pl.ds(40 * k + 8 * s, 8), :], vec_peer[s])

    def vec_step(k, s):
        src, got_row = pl.ds(48 * k + 8 * s, 8), pl.ds(40 * k + 8 * s, 8)
        wait_recv(("v", k, s), r.VR.at[got_row, :])
        r.VS[pl.ds(48 * k + 8 * s + 8, 8), :] = r.VS[src, :] + r.VR[got_row, :]
        if s < 4:
            vec_send(k, s + 1)

    def rs1_send(p, zm):
        rows = 2 * ROWS[p]
        s = pl.ds(zm * rows, rows)
        send(("r1", p, zm), r.S1[p].at[s, :], r.R1[p].at[s, :], (ids[MV], c))

    def rs_sum1(p, zm):
        rows, a = ROWS[p], APART[p]
        b = rows - a
        g, r1 = r.G[p], r.R1[p]
        s = pl.ds(zm * 2 * rows, 2 * rows)
        wait_recv(("r1", p, zm), r1.at[s, :])
        for du in (1, 0):
            o = (2 * zm + du) * rows
            top = g[o : o + a, :] + r1[o : o + a, :].astype(F32)
            low = g[o + a : o + rows, :] + r1[o + a : o + rows, :].astype(F32)
            if du == 1:
                q = pl.ds(zm * a, a)
                r.S2A[p][q, :] = top.astype(BF)
                send(("r2a", p, zm), r.S2A[p].at[q, :], r.R2A[p].at[q, :], (ids[MU], c))
            else:
                g[o : o + a, :] = top
            if zm:
                q = pl.ds(((zm - 1) * 2 + du) * b, b)
                r.S2C[p][q, :] = low.astype(BF)
            else:
                g[o + a : o + rows, :] = low
        if zm:
            q = pl.ds((zm - 1) * 2 * b, 2 * b)
            send(("r2c", p, zm), r.S2C[p].at[q, :], r.R2C[p].at[q, :], (ids[4 * zm], c))

    def rs_sum2a(p, zm):
        rows, a = ROWS[p], APART[p]
        g, r2 = r.G[p], r.R2A[p]
        q = pl.ds(zm * a, a)
        wait_recv(("r2a", p, zm), r2.at[q, :])
        o = 2 * zm * rows
        val = g[o : o + a, :] + r2[q, :].astype(F32)
        if zm:
            k = pl.ds((zm - 1) * a, a)
            r.S3A[p][k, :] = val.astype(BF)
            send(("r3a", p, zm), r.S3A[p].at[k, :], r.R3A[p].at[k, :], (ids[4 * zm], c))
        else:
            g[o : o + a, :] = val

    def rs_sum2c(p):
        rows, a = ROWS[p], APART[p]
        b = rows - a
        g, r2 = r.G[p], r.R2C[p]
        for zm in (1, 2, 3):
            wait_recv(("r2c", p, zm), r2.at[pl.ds((zm - 1) * 2 * b, 2 * b), :])
        for du in (1, 0):
            o = du * rows + a
            val = g[o : o + b, :]
            for zm in (1, 2, 3):
                k = ((zm - 1) * 2 + du) * b
                val = val + r2[k : k + b, :].astype(F32)
            if du == 1:
                r.S3C[p][...] = val.astype(BF)
                send(("r3c", p), r.S3C[p], r.R3C[p], (ids[MU], c))
            else:
                g[o : o + b, :] = val

    def rs_final(p):
        rows, a = ROWS[p], APART[p]
        g = r.G[p]
        r3a, r3c = r.R3A[p], r.R3C[p]
        for zm in (1, 2, 3):
            wait_recv(("r3a", p, zm), r3a.at[pl.ds((zm - 1) * a, a), :])
        val = g[0:a, :]
        for zm in (1, 2, 3):
            val = val + r3a[(zm - 1) * a : zm * a, :].astype(F32)
        g[0:a, :] = val
        wait_recv(("r3c", p), r3c)
        g[a:rows, :] = g[a:rows, :] + r3c[...].astype(F32)

    def block_row(zm, du, dv):
        uu = 1 - u if du else u
        vv = 1 - v if dv else v
        return ub * uu + vb * vv

    def stage(p, zm, src, base):
        rows, cols = ROWS[p], COLS[p]
        for du in (1, 0):
            k = (2 * zm + du) * rows
            far = pl.ds(pl.multiple_of(base + block_row(zm, du, 1) * rows, 8), rows)
            near = pl.ds(pl.multiple_of(base + block_row(zm, du, 0) * rows, 8), rows)
            r.S1[p][k : k + rows, :] = src[far, 0:cols].astype(BF)
            r.G[p][k : k + rows, :] = src[near, 0:cols]
        rs1_send(p, zm)

    r.WQ[pl.ds(pl.multiple_of(me * 48, 16), 48), 0:384] = r.wq[...].astype(BF)
    r.WQ[pl.ds(pl.multiple_of(me * 48, 16), 48), 384:768] = r.wk[...].astype(BF)
    r.WQ[pl.ds(pl.multiple_of(me * 48, 16), 48), 768:1152] = r.wv[...].astype(BF)
    ag_own("Q")
    send("tok", r.tok, r.X.at[own_rows, :], partner)
    local = pltpu.make_async_copy(r.tok, r.X.at[own_rows, :], r.ls.at[0])
    local.start()
    flat = 2 * me + c
    r.VS[0:8, :] = jnp.zeros((8, 768), F32)
    for k, n in enumerate(("ga", "ba", "gf", "bf")):
        r.VS[k : k + 1, 0:24] = getattr(r, n)[...].reshape(1, 24).astype(BF).astype(F32)
    r.VS[0:8, :] = pltpu.roll(r.VS[0:8, :], 24 * flat, 1)
    vec_send(0, 0)
    wo = r.wo[...]
    r.WOP[c, pl.ds(pl.multiple_of(me * 48, 16), 48), :] = jnp.concatenate(
        [wo[:, 0:384], wo[:, 384:768]], axis=0
    ).astype(BF)
    ag_own("O")
    wut = jnp.transpose(jnp.concatenate([r.wu[...], jnp.zeros((768, 32), F32)], axis=1))
    r.WU[pl.ds(pl.multiple_of(me * 96, 16), 96), :] = wut[0:96, :].astype(BF)
    r.WD[pl.ds(pl.multiple_of(me * 96, 16), 96), :] = r.wd[...].astype(BF)

    col_pos = lax.broadcasted_iota(jnp.int32, (512, 128), 0)
    row_pos = lax.broadcasted_iota(jnp.int32, (8, 512), 1)
    col_lab = jnp.zeros((512, 128), jnp.int32)
    row_lab = jnp.zeros((8, 512), jnp.int32)
    for j in range(8):
        lo = r.off[0, j]
        hi = lo + r.len[0, j]
        col_lab = jnp.where((col_pos >= lo) & (col_pos < hi), j + 1, col_lab)
        row_lab = jnp.where((row_pos >= lo) & (row_pos < hi), j + 1, row_lab)
    r.LIVE[...] = jnp.where(col_lab > 0, 1.0, 0.0).astype(F32)
    row_lab = jnp.where(row_lab > 0, row_lab, -1)
    for t in range(4):
        q = slice(128 * t, 128 * t + 128)
        lab = jnp.concatenate([col_lab[q]] * 4, axis=1)
        same = lab == jnp.broadcast_to(row_lab[0:1], (128, 512))
        r.BIAS[q, :] = jnp.where(same, 0.0, -1e30).astype(F32)

    run(ag_steps("Q")[:7])
    ag_own("U")
    run(ag_steps("Q")[7:])
    o_steps, u_steps, d_steps = ag_steps("O"), ag_steps("U"), ag_steps("D")
    vec_step(0, 0)
    wait_recv("tok", r.X.at[own_rows, :])
    local.wait()
    run(o_steps[:4])
    for zm in range(4):
        ag_plane("Q", zm)

    for k, n in enumerate(("Q3", "K3", "V3")):
        full = mm(r.X[...], r.WQ[:, 384 * k : 384 * k + 384])
        full = full.astype(BF)
        if k == 0:
            full = full * BF(0.125)
        for i in range(3):
            getattr(r, n)[i] = full[:, 128 * i : 128 * i + 128]
    ag_own("D")
    vec_step(0, 1)

    for i in range(3):
        r.ATT[i] = jnp.zeros((512, 128), BF)
    fw_hooks = [
        o_steps[4:9],
        o_steps[9:] + u_steps[:1],
        [functools.partial(vec_step, 0, 2)] + u_steps[1:4],
        u_steps[4:7],
        [functools.partial(vec_step, 0, 3)] + u_steps[7:10],
        u_steps[10:],
    ]
    lane = lax.broadcasted_iota(jnp.int32, (1, 128), 1)

    def half(val, a):
        keep = (lane >= 64 * a) & (lane < 64 * a + 64)
        return jnp.where(keep, val, jnp.zeros_like(val))

    def at_index(h, hooks):
        for k, steps in enumerate(hooks):

            def go(steps=steps):
                run(steps)

            pl.when(h == k)(go)

    def fwd_head(h, carry):
        at_index(h, fw_hooks)
        i = lax.div(h, 2)
        a = lax.rem(h, 2)
        vals = half(r.V3[i], a)
        keys = half(r.K3[i], a)
        for t in range(4):
            q = slice(128 * t, 128 * t + 128)
            s = mm(r.Q3[i, q, :], keys, 1, 1) + r.BIAS[q, :]
            live = r.LIVE[q, 0:1]
            top = jnp.where(live > 0, jnp.max(s, axis=1, keepdims=True), 0.0)
            w = jnp.exp(s - top)
            total = jnp.sum(w, axis=1, keepdims=True) + (1.0 - live)
            prob = w * (1.0 / total)
            r.P32[h, q, :] = prob
            o = mm(prob.astype(BF), vals)
            r.ATT[i, q, :] = r.ATT[i, q, :] + o.astype(BF)
        return carry

    lax.fori_loop(0, 6, fwd_head, 0)

    send("att", r.ATT.at[:, oth_rows, :], r.ATTR, partner)
    for zm in range(4):
        ag_plane("O", zm)
    send("wop", r.WOP.at[c], r.WOP.at[c], partner)
    run(d_steps[:4])
    vec_step(0, 4)
    wait_recv("wop", r.WOP.at[1 - c])

    def build_out(i, carry):
        for k in range(2):
            blk = r.WOP[k, pl.ds(pl.multiple_of(48 * i, 16), 48), :].astype(F32)
            rows = jnp.concatenate([blk[0:24], blk[24:48]], axis=1)
            r.T[pl.ds(pl.multiple_of(48 * i + 24 * k, 8), 24), 0:768] = rows
        return carry

    lax.fori_loop(0, 16, build_out, 0)
    r.WO[...] = r.T[:, 0:768].astype(BF)
    wait_recv("att", r.ATTR)
    own_heads = pl.ds(pl.multiple_of(384 * c, 128), 384)
    oth_heads = pl.ds(pl.multiple_of(384 * (1 - c), 128), 384)

    def joined(ref, rows):
        return jnp.concatenate([ref[i, rows, :] for i in range(3)], axis=1)

    all256 = pl.ds(0, 256)
    branch = mm(joined(r.ATT, own_rows), r.WO[own_heads, :])
    branch = branch + mm(joined(r.ATTR, all256), r.WO[oth_heads, :])
    r.GS[...] = branch
    run(d_steps[4:6])

    def norm(val):
        mean = jnp.mean(val, axis=1, keepdims=True)
        cen = val - mean
        inv = lax.rsqrt(jnp.mean(cen * cen, axis=1, keepdims=True) + EPS)
        return cen * inv, inv

    def ln1(t, carry):
        q = pl.ds(pl.multiple_of(64 * t, 64), 64)
        unit, inv = norm(r.tok[q, :].astype(F32) + r.GS[q, :])
        r.U1[q, :] = unit
        r.INV1[q, :] = jnp.broadcast_to(inv, (64, 128))
        one = unit * r.VS[40:41, :] + r.VS[41:42, :]
        r.N1[q, :] = one
        r.FIN[pl.ds(pl.multiple_of(base256 + 64 * t, 64), 64), :] = one.astype(BF)
        return carry

    lax.fori_loop(0, 4, ln1, 0)
    send("fin", r.FIN.at[own_rows, :], r.FIN.at[own_rows, :], partner)
    run(d_steps[6:8])
    wait_recv("fin", r.FIN.at[oth_rows, :])

    def plane_rows(zm):
        return pl.ds(pl.multiple_of(384 * zs[zm], 128), 384)

    def ffn_up(zm):
        for t in range(2):
            q = slice(256 * t, 256 * t + 256)
            pre = mm(r.FIN[q, :], r.WU[plane_rows(zm), :], 1, 1)
            r.GEL[zm, q, :] = pre

        def act(t, carry):
            q = pl.ds(pl.multiple_of(64 * t, 64), 64)
            pre = r.GEL[zm, q, :]
            cdf = 0.5 * (1.0 + lax.erf(pre * (2.0**-0.5)))
            pdf = jnp.exp(-0.5 * pre * pre) * (1.0 / math.sqrt(2.0 * math.pi))
            r.HID[zm, q, :] = (pre * cdf).astype(BF)
            r.GEL[zm, q, :] = cdf + pre * pdf
            return carry

        lax.fori_loop(0, 8, act, 0)

    d_groups = (d_steps[8:10], d_steps[10:12], d_steps[12:], [])
    for zm in range(4):
        ag_plane("U", zm)
        ffn_up(zm)
        run(d_groups[zm])
    for zm in range(4):
        ag_plane("D", zm)
        for rows in (oth_rows, own_rows):
            part = mm(r.HID[zm, rows, :], r.WD[plane_rows(zm), :])
            if zm:
                part = part + r.SEC[rows, :]
            r.SEC[rows, :] = part
            if zm == 3 and rows is oth_rows:
                send("sec", r.SEC.at[oth_rows, :], r.SECR, partner)
    wait_recv("sec", r.SECR)

    def ln2(t, sums):
        dg, db = sums
        q = pl.ds(pl.multiple_of(64 * t, 64), 64)
        qq = pl.ds(pl.multiple_of(base256 + 64 * t, 64), 64)
        unit, inv = norm(r.N1[q, :] + (r.SEC[qq, :] + r.SECR[q, :]))
        gain = r.VS[42:43, :]
        r.out[q, :] = (unit * gain + r.VS[43:44, :]).astype(BF)
        e = r.og[q, :].astype(F32)
        dg = dg + jnp.sum(e * unit, axis=0, keepdims=True)
        db = db + jnp.sum(e, axis=0, keepdims=True)
        eg = e * gain
        inner = jnp.mean(eg * unit, axis=1, keepdims=True)
        gs = inv * (eg - jnp.mean(eg, axis=1, keepdims=True) - unit * inner)
        r.GS[q, :] = gs
        r.GFB[qq, :] = gs.astype(BF)
        return dg, db

    zero = jnp.zeros((1, 768), F32)
    dg2, db2 = lax.fori_loop(0, 4, ln2, (zero, zero))
    send("gfb", r.GFB.at[own_rows, :], r.GFB.at[own_rows, :], partner)
    wait_recv("gfb", r.GFB.at[oth_rows, :])
    wait_sent("sec")

    for n_done, zm in enumerate((3, 2, 1, 0)):
        r.T[0:384, 0:768] = mm(r.HID[zm], r.GFB[...], 0, 0)
        stage("D", zm, r.T, 0)
        for t in range(2):
            q = slice(256 * t, 256 * t + 256)
            gh = mm(r.GFB[q, :], r.WD[plane_rows(zm), :], 1, 1)
            r.HID[zm, q, :] = (gh * r.GEL[zm, q, :]).astype(BF)
        r.T[384:768, 0:768] = mm(r.HID[zm], r.FIN[...], 0, 0)
        stage("U", zm, r.T, 384)
        for rows in (oth_rows, own_rows):
            part = mm(r.HID[zm, rows, :], r.WU[plane_rows(zm), :])
            if n_done:
                part = part + r.SEC[rows, :]
            r.SEC[rows, :] = part
            if n_done == 3 and rows is oth_rows:
                send("gn", r.SEC.at[oth_rows, :], r.SECR, partner)
        if n_done:
            rs_sum1("D", zm + 1)
    wait_recv("gn", r.SECR)

    def ln1_back(t, sums):
        dg, db = sums
        q = pl.ds(pl.multiple_of(64 * t, 64), 64)
        qq = pl.ds(pl.multiple_of(base256 + 64 * t, 64), 64)
        e = r.GS[q, :] + (r.SEC[qq, :] + r.SECR[q, :])
        unit = r.U1[q, :]
        inv = r.INV1[q, 0:1]
        dg = dg + jnp.sum(e * unit, axis=0, keepdims=True)
        db = db + jnp.sum(e, axis=0, keepdims=True)
        eg = e * r.VS[40:41, :]
        inner = jnp.mean(eg * unit, axis=1, keepdims=True)
        first = inv * (eg - jnp.mean(eg, axis=1, keepdims=True) - unit * inner)
        r.GS[q, :] = first
        r.GB[q, :] = first.astype(BF)
        return dg, db

    dg1, db1 = lax.fori_loop(0, 4, ln1_back, (zero, zero))
    r.VS[48:56, :] = jnp.zeros((8, 768), F32)
    for k, val in enumerate((dg1, db1, dg2, db2)):
        r.VS[48 + k : 49 + k, :] = val
    vec_send(1, 0)

    gview = mm(r.GB[...], r.WO[oth_heads, :], 1, 1).astype(BF)
    for i in range(3):
        r.GAS[i] = gview[:, 128 * i : 128 * i + 128]
    send("gas", r.GAS, r.GA.at[:, own_rows, :], partner)
    gview = mm(r.GB[...], r.WO[own_heads, :], 1, 1).astype(BF)
    for i in range(3):
        r.GA[i, own_rows, :] = gview[:, 128 * i : 128 * i + 128]
    rs_sum1("D", 0)
    r.T[own_heads, 0:768] = mm(joined(r.ATT, own_rows), r.GB[...], 0, 0)
    r.T[oth_heads, 0:768] = mm(joined(r.ATTR, all256), r.GB[...], 0, 0)

    def pair_out(i, carry):
        q = pl.ds(pl.multiple_of(48 * i, 16), 48)
        blk = r.T[pl.ds(pl.multiple_of(48 * i + other24, 8), 24), 0:768]
        r.S0[q, :] = jnp.concatenate([blk[:, 0:384], blk[:, 384:768]], axis=0).astype(BF)
        return carry

    lax.fori_loop(0, 16, pair_out, 0)
    send("s0", r.S0, r.R0, partner)
    rs_sum1("U", 3)
    rs_sum1("U", 2)
    wait_recv("s0", r.R0)

    def out_block(m):
        i = ids[m]
        blk = r.T[pl.ds(pl.multiple_of(48 * i + base24, 8), 24), 0:768]
        blk = jnp.concatenate([blk[:, 0:384], blk[:, 384:768]], axis=0)
        return blk + r.R0[pl.ds(pl.multiple_of(48 * i, 16), 48), :].astype(F32)

    for zm in (3, 2, 1, 0):
        for du in (1, 0):
            k = (2 * zm + du) * 48
            r.S1["O"][k : k + 48, :] = out_block(4 * zm + 2 * du + 1).astype(BF)
            r.G["O"][k : k + 48, :] = out_block(4 * zm + 2 * du)
        rs1_send("O", zm)

    wait_recv("gas", r.GA.at[:, oth_rows, :])
    for n in ("DQ", "DK", "DV"):
        for i in range(3):
            getattr(r, n)[i] = jnp.zeros((512, 128), BF)

    def s1(p, zm):
        return functools.partial(rs_sum1, p, zm)

    def s2a(p, zm):
        return functools.partial(rs_sum2a, p, zm)

    def s2c(p):
        return functools.partial(rs_sum2c, p)

    def vs(s):
        return functools.partial(vec_step, 1, s)

    bw_hooks = [
        [s1("U", 1), s2a("D", 3), s2a("D", 2), vs(0)],
        [s1("U", 0), s2a("D", 1), s2a("D", 0), s2c("D")],
        [s2a("U", 3), s2a("U", 2), vs(1), s1("O", 3), s1("O", 2)],
        [s2a("U", 1), s2a("U", 0), s2c("U"), s1("O", 1), s1("O", 0)],
        [functools.partial(rs_final, "D"), vs(2)],
        [s2a("O", 3), s2a("O", 2), s2a("O", 1), s2a("O", 0), s2c("O"), vs(3)],
    ]

    def bwd_head(h, carry):
        at_index(h, bw_hooks)
        i = lax.div(h, 2)
        a = lax.rem(h, 2)
        go = half(r.GA[i], a)
        for t in range(4):
            q = slice(128 * t, 128 * t + 128)
            prob = r.P32[h, q, :]
            dp = mm(go[q], r.V3[i], 1, 1)
            delta = jnp.sum(prob * dp, axis=1, keepdims=True)
            r.DSB[q, :] = (prob * (dp - delta)).astype(BF)
            r.PB[q, :] = prob.astype(BF)
        r.DV[i] = r.DV[i] + mm(r.PB[...], go, 0, 0).astype(BF)
        dq = mm(r.DSB[...], half(r.K3[i], a)) * 0.125
        r.DQ[i] = r.DQ[i] + dq.astype(BF)
        dk = mm(r.DSB[...], half(r.Q3[i], a), 0, 0)
        r.DK[i] = r.DK[i] + dk.astype(BF)
        return carry

    lax.fori_loop(0, 6, bwd_head, 0)

    all512 = pl.ds(0, 512)
    for k, n in enumerate(("DQ", "DK", "DV")):
        r.T[:, 384 * k : 384 * k + 384] = mm(r.X[...], joined(getattr(r, n), all512), 0, 0)
    for zm in (3, 2, 1, 0):
        stage("Q", zm, r.T, 192 * zs[zm])
    run([functools.partial(rs_final, "U"), vs(4)])

    for rows in (oth_rows, own_rows):
        acc = mm(joined(r.DQ, rows), r.WQ[:, 0:384], 1, 1)
        acc = acc + mm(joined(r.DK, rows), r.WQ[:, 384:768], 1, 1)
        acc = acc + mm(joined(r.DV, rows), r.WQ[:, 768:1152], 1, 1)
        if rows is oth_rows:
            r.IGS[...] = acc.astype(BF)
            send("ig", r.IGS, r.IGR, partner)
        else:
            r.GS[...] = r.GS[...] + acc
    wait_recv("ig", r.IGR)
    r.ig[...] = (r.GS[...] + r.IGR[...].astype(F32)).astype(BF)

    for zm in (3, 2, 1, 0):
        rs_sum1("Q", zm)
    rs_final("O")
    for zm in (3, 2, 1, 0):
        rs_sum2a("Q", zm)
    rs_sum2c("Q")
    r.dwd[...] = r.G["D"][0:96, :]
    r.UT[0:96, :] = r.G["U"][0:96, :]
    r.UT[96:128, :] = jnp.zeros((32, 768), F32)
    r.dwu[...] = jnp.transpose(r.UT[...])[:, 0:96]
    go = r.G["O"][0:48, :]
    r.dwo[...] = jnp.concatenate([go[0:24], go[24:48]], axis=1)
    back = pltpu.roll(r.VS[88:96, :], lax.rem(768 - 24 * flat, 768), 1)
    for k, n in enumerate(("dga", "dba", "dgf", "dbf")):
        getattr(r, n)[...] = back[k, 0:24]
    rs_final("Q")
    r.dwq[...] = r.G["Q"][0:48, 0:384]
    r.dwk[...] = r.G["Q"][0:48, 384:768]
    r.dwv[...] = r.G["Q"][0:48, 768:1152]

    for entry in sends:
        if entry[3] not in waited:
            wait_send(entry)


def layer_small(*args):
    shapes = (
        ((256, 768), BF),
        ((256, 768), BF),
        ((48, 384), F32),
        ((48, 384), F32),
        ((48, 384), F32),
        ((24, 768), F32),
        ((24,), F32),
        ((24,), F32),
        ((768, 96), F32),
        ((96, 768), F32),
        ((24,), F32),
        ((24,), F32),
    )
    vmem = pl.BlockSpec(memory_space=pltpu.VMEM)
    smem = pl.BlockSpec(memory_space=pltpu.SMEM)
    return pl.pallas_call(
        layer_kernel,
        out_shape=tuple(jax.ShapeDtypeStruct(s, d) for s, d in shapes),
        in_specs=[smem if n in ("len", "off") else vmem for n in IN_NAMES],
        out_specs=tuple(vmem for _ in shapes),
        scratch_shapes=[s for _, s in scratch_list()],
        compiler_params=pltpu.CompilerParams(
            collective_id=0, has_side_effects=True, vmem_limit_bytes=67043328
        ),
    )(*args)


def labels_of(lengths, offsets):
    position = jnp.arange(BIN, dtype=jnp.int32)[:, None]
    starts = offsets[None, :]
    inside = (position >= starts) & (position < starts + lengths[None, :])
    slot_order = jnp.arange(1, lengths.shape[0] + 1, dtype=jnp.int32)[None, :]
    return jnp.sum(jnp.where(inside, slot_order, 0), axis=1)


def layer_norm(operand, gain_vec, bias_vec):
    row_mean = jnp.mean(operand, axis=-1, keepdims=True)
    centered = operand - row_mean
    inverse = lax.rsqrt(jnp.mean(centered * centered, axis=-1, keepdims=True) + EPS)
    normed = centered * inverse
    return (normed * gain_vec + bias_vec, normed, inverse)


def norm_back(grad_rows, normed, inverse, gain_vec):
    scaled = grad_rows * gain_vec
    inner = jnp.mean(scaled * normed, axis=-1, keepdims=True)
    return inverse * (scaled - jnp.mean(scaled, axis=-1, keepdims=True) - normed * inner)


def gelu_exact(operand):
    return jax.nn.gelu(operand, approximate=False)


def contract_rows(left, right):
    return lax.dot_general(
        left, right, (((0,), (0,)), ((), ())), preferred_element_type=F32
    )


def contract_cols(left, right):
    return lax.dot_general(
        left, right, (((1,), (1,)), ((), ())), preferred_element_type=F32
    )


def score_block(queries, key_rows, labels_bin, factor):
    scores = (
        jnp.einsum("qhd,khd->hqk", queries, key_rows, preferred_element_type=F32) * factor
    )
    allowed = ((labels_bin[:, None] == labels_bin[None, :]) & (labels_bin[:, None] > 0))[None]
    live_rows = (labels_bin > 0)[None, :, None]
    return (scores, allowed, live_rows)


def masked_exp(scores, allowed, row_top):
    return jnp.where(allowed, jnp.exp(jnp.where(allowed, scores - row_top, 0.0)), 0.0)


def attend_bin(pieces, factor):
    queries, key_rows, value_rows, labels_bin = pieces
    scores, allowed, live_rows = score_block(queries, key_rows, labels_bin, factor)
    row_top = jnp.max(jnp.where(allowed, scores, -1e30), axis=2, keepdims=True)
    row_top = jnp.where(live_rows, row_top, 0.0)
    weights = masked_exp(scores, allowed, row_top)
    denominator = jnp.sum(weights, axis=2, keepdims=True) + jnp.where(live_rows, 0.0, 1.0)
    probability = (weights / denominator).astype(jnp.bfloat16)
    mixed_rows = jnp.einsum(
        "hqk,khd->qhd", probability, value_rows, preferred_element_type=F32
    )
    return (mixed_rows.astype(jnp.bfloat16), row_top, denominator)


def attend_back(pieces, factor):
    queries, key_rows, value_rows, labels_bin, row_top, denominator, grad_mixed = pieces
    scores, allowed, live_rows = score_block(queries, key_rows, labels_bin, factor)
    probability = masked_exp(scores, allowed, row_top) / denominator
    grad_values = jnp.einsum(
        "hqk,qhd->khd",
        probability.astype(jnp.bfloat16),
        grad_mixed,
        preferred_element_type=F32,
    )
    grad_probs = jnp.einsum(
        "qhd,khd->hqk", grad_mixed, value_rows, preferred_element_type=F32
    )
    row_delta = jnp.sum(probability * grad_probs, axis=2, keepdims=True)
    grad_scores = (probability * (grad_probs - row_delta)).astype(jnp.bfloat16)
    grad_queries = (
        jnp.einsum("hqk,khd->qhd", grad_scores, key_rows, preferred_element_type=F32)
        * factor
    )
    grad_keys = (
        jnp.einsum("hqk,qhd->khd", grad_scores, queries, preferred_element_type=F32)
        * factor
    )
    return (
        grad_queries.astype(jnp.bfloat16),
        grad_keys.astype(jnp.bfloat16),
        grad_values.astype(jnp.bfloat16),
    )


def per_device(
    tokens,
    w_query,
    w_key,
    w_value,
    w_out,
    gain_attn,
    bias_attn,
    w_up,
    w_down,
    gain_ffn,
    bias_ffn,
    seq_lengths,
    seq_offsets,
    out_grad,
):
    low_type = jnp.bfloat16
    bin_count = seq_lengths.shape[0]
    group_rows = bin_count * BIN
    head_width = w_query.shape[1]
    local_heads = head_width // HD
    factor = 1.0 / math.sqrt(HD)
    labels = jax.vmap(labels_of)(seq_lengths, seq_offsets)
    full_query, full_key, full_value = (
        lax.all_gather(w_query.astype(low_type), DP, axis=0, tiled=True),
        lax.all_gather(w_key.astype(low_type), DP, axis=0, tiled=True),
        lax.all_gather(w_value.astype(low_type), DP, axis=0, tiled=True),
    )
    projection = jnp.concatenate([full_query, full_key, full_value], axis=1)
    whole_rows = lax.all_gather(tokens, HEAD, axis=0, tiled=True)
    projected = jnp.dot(whole_rows, projection, preferred_element_type=F32).astype(low_type)
    shape_bins = (bin_count, BIN, local_heads, HD)
    queries = projected[:, :head_width].reshape(shape_bins)
    key_rows = projected[:, head_width : 2 * head_width].reshape(shape_bins)
    value_rows = projected[:, 2 * head_width :].reshape(shape_bins)
    mixed_bins, row_tops, denominators = lax.map(
        lambda pieces: attend_bin(pieces, factor), (queries, key_rows, value_rows, labels)
    )
    attended = mixed_bins.reshape(group_rows, head_width)
    out_full, up_part, down_part, gain_one, bias_one, gain_two, bias_two = (
        lax.all_gather(w_out.astype(low_type), BOTH, axis=0, tiled=True),
        lax.all_gather(w_up.astype(low_type), BOTH, axis=1, tiled=True),
        lax.all_gather(w_down.astype(low_type), BOTH, axis=0, tiled=True),
        lax.all_gather(gain_attn.astype(low_type), BOTH, axis=0, tiled=True),
        lax.all_gather(bias_attn.astype(low_type), BOTH, axis=0, tiled=True),
        lax.all_gather(gain_ffn.astype(low_type), BOTH, axis=0, tiled=True),
        lax.all_gather(bias_ffn.astype(low_type), BOTH, axis=0, tiled=True),
    )
    gain_first = gain_one.astype(F32)
    gain_second = gain_two.astype(F32)
    token_view = lax.all_to_all(attended, HEAD, split_axis=0, concat_axis=1, tiled=True)
    first_sum = tokens.astype(F32) + jnp.dot(
        token_view, out_full, preferred_element_type=F32
    )
    normed_one, unit_one, inverse_one = layer_norm(
        first_sum, gain_first, bias_one.astype(F32)
    )
    ffn_input = normed_one.astype(low_type)
    pre_act = jnp.dot(ffn_input, up_part, preferred_element_type=F32)
    activated, gelu_pull = jax.vjp(gelu_exact, pre_act)
    hidden = activated.astype(low_type)
    second_sum = normed_one + jnp.dot(hidden, down_part, preferred_element_type=F32)
    result, unit_two, inverse_two = layer_norm(
        second_sum, gain_second, bias_two.astype(F32)
    )
    output = result.astype(low_type)
    grad_result = out_grad.astype(F32)
    grad_gain_two = jnp.sum(grad_result * unit_two, axis=0)
    grad_bias_two = jnp.sum(grad_result, axis=0)
    grad_second = norm_back(grad_result, unit_two, inverse_two, gain_second)
    grad_ffn = grad_second.astype(low_type)
    grad_down_part = contract_rows(hidden, grad_ffn)
    grad_pre = gelu_pull(contract_cols(grad_ffn, down_part))[0].astype(low_type)
    grad_up_part = contract_rows(ffn_input, grad_pre)
    grad_normed = grad_second + contract_cols(grad_pre, up_part)
    grad_gain_one = jnp.sum(grad_normed * unit_one, axis=0)
    grad_bias_one = jnp.sum(grad_normed, axis=0)
    grad_first = norm_back(grad_normed, unit_one, inverse_one, gain_first)
    grad_branch = grad_first.astype(low_type)
    grad_out_full = contract_rows(token_view, grad_branch)
    part_out, part_up, part_down, part_gain_one, part_bias_one, part_gain_two, part_bias_two = (
        lax.psum_scatter(grad_out_full, BOTH, scatter_dimension=0, tiled=True),
        lax.psum_scatter(grad_up_part, BOTH, scatter_dimension=1, tiled=True),
        lax.psum_scatter(grad_down_part, BOTH, scatter_dimension=0, tiled=True),
        lax.psum_scatter(grad_gain_one, BOTH, scatter_dimension=0, tiled=True),
        lax.psum_scatter(grad_bias_one, BOTH, scatter_dimension=0, tiled=True),
        lax.psum_scatter(grad_gain_two, BOTH, scatter_dimension=0, tiled=True),
        lax.psum_scatter(grad_bias_two, BOTH, scatter_dimension=0, tiled=True),
    )
    grad_token_view = contract_cols(grad_branch, out_full).astype(low_type)
    grad_attended = lax.all_to_all(grad_token_view, HEAD, split_axis=1, concat_axis=0, tiled=True)
    grad_bins = grad_attended.reshape(shape_bins)
    grad_queries, grad_keys, grad_values = lax.map(
        lambda pieces: attend_back(pieces, factor),
        (queries, key_rows, value_rows, labels, row_tops, denominators, grad_bins),
    )
    grad_projected = jnp.concatenate(
        [
            grad_queries.reshape(group_rows, head_width),
            grad_keys.reshape(group_rows, head_width),
            grad_values.reshape(group_rows, head_width),
        ],
        axis=1,
    )
    grad_projection = contract_rows(whole_rows, grad_projected)
    part_query, part_key, part_value = (
        lax.psum_scatter(grad_projection[:, :head_width], DP, scatter_dimension=0, tiled=True),
        lax.psum_scatter(
            grad_projection[:, head_width : 2 * head_width], DP, scatter_dimension=0, tiled=True
        ),
        lax.psum_scatter(
            grad_projection[:, 2 * head_width :], DP, scatter_dimension=0, tiled=True
        ),
    )
    input_grad = (
        grad_first
        + lax.psum_scatter(
            contract_cols(grad_projected, projection).astype(jnp.bfloat16),
            HEAD,
            scatter_dimension=0,
            tiled=True,
        ).astype(F32)
    ).astype(low_type)
    return (
        output,
        input_grad,
        part_query,
        part_key,
        part_value,
        part_out,
        part_gain_one,
        part_bias_one,
        part_up,
        part_down,
        part_gain_two,
        part_bias_two,
    )


def solution(mesh):
    small = mesh.shape[DP] == 16 and mesh.shape[HEAD] == 2
    return jax.shard_map(
        layer_small if small else per_device,
        mesh=mesh,
        in_specs=(
            P(BOTH, None),
            P(DP, HEAD),
            P(DP, HEAD),
            P(DP, HEAD),
            P(BOTH, None),
            P(BOTH),
            P(BOTH),
            P(None, BOTH),
            P(BOTH, None),
            P(BOTH),
            P(BOTH),
            P(DP, None),
            P(DP, None),
            P(BOTH, None),
        ),
        out_specs=(
            P(BOTH, None),
            P(BOTH, None),
            P(DP, HEAD),
            P(DP, HEAD),
            P(DP, HEAD),
            P(BOTH, None),
            P(BOTH),
            P(BOTH),
            P(None, BOTH),
            P(BOTH, None),
            P(BOTH),
            P(BOTH),
        ),
        check_vma=False,
    )
```

```python
import functools
import math
import types

import jax
import jax.numpy as jnp
from jax import lax
from jax.experimental import pallas as pl
from jax.experimental.pallas import tpu as pltpu
from jax.sharding import PartitionSpec as P

HD = 64
BIN = 512
EPS = 1e-12
F32 = jnp.float32
BF = jnp.bfloat16
MESH = pl.DeviceIdType.MESH

MU, MV = 2, 1
ROWS = {"Q": 48, "O": 48, "U": 96, "D": 96}
COLS = {"Q": 1152, "O": 384, "U": 768, "D": 768}
APART = {"Q": 32, "O": 32, "U": 64, "D": 64}
PIECES = ("Q", "O", "U", "D")
PER_PIECE = ("G", "S1", "R1", "S2A", "R2A", "S3A", "R3A", "S2C", "R2C", "S3C", "R3C")
DP, HEAD = "dp", "head"
BOTH = (DP, HEAD)


def mm(a, b, ca=1, cb=0):
    return lax.dot_general(a, b, (((ca,), (cb,)), ((), ())), preferred_element_type=F32)


def scratch_list():
    items = []

    def add(name, shape, dtype):
        items.append((name, pltpu.VMEM(shape, dtype)))

    add("X", (512, 768), BF)
    add("WQ", (768, 1152), BF)
    add("WOP", (2, 768, 384), BF)
    add("WO", (768, 768), BF)
    add("WU", (1536, 768), BF)
    add("WD", (1536, 768), BF)
    for n in ("Q3", "K3", "V3", "ATT", "GA", "DQ", "DK", "DV"):
        add(n, (3, 512, 128), BF)
    add("ATTR", (3, 256, 128), BF)
    add("GAS", (3, 256, 128), BF)
    add("BIAS", (512, 512), F32)
    add("LIVE", (512, 128), F32)
    add("P32", (6, 512, 512), F32)
    add("PB", (512, 512), BF)
    add("DSB", (512, 512), BF)
    add("U1", (256, 768), F32)
    add("N1", (256, 768), F32)
    add("INV1", (256, 128), F32)
    add("FIN", (512, 768), BF)
    add("HID", (4, 512, 384), BF)
    add("GEL", (4, 512, 384), F32)
    add("SEC", (512, 768), F32)
    add("SECR", (256, 768), F32)
    add("GS", (256, 768), F32)
    add("GFB", (512, 768), BF)
    add("GB", (256, 768), BF)
    add("IGS", (256, 768), BF)
    add("IGR", (256, 768), BF)
    add("T", (768, 1152), F32)
    add("S0", (768, 384), BF)
    add("R0", (768, 384), BF)
    for p in PIECES:
        r, c, a = ROWS[p], COLS[p], APART[p]
        b = r - a
        sizes = (8 * r, 8 * r, 8 * r, 4 * a, 4 * a, 3 * a, 3 * a, 6 * b, 6 * b, b, b)
        for key, size in zip(PER_PIECE, sizes):
            add(key + p, (size, c), F32 if key == "G" else BF)
    add("VS", (96, 768), F32)
    add("VR", (80, 768), F32)
    items.append(("ss", pltpu.SemaphoreType.DMA((320,))))
    items.append(("rs", pltpu.SemaphoreType.DMA((320,))))
    items.append(("ls", pltpu.SemaphoreType.DMA((4,))))
    return items


IN_NAMES = ("tok", "wq", "wk", "wv", "wo", "ga", "ba", "wu", "wd", "gf", "bf", "len", "off", "og")
OUT_NAMES = ("out", "ig", "dwq", "dwk", "dwv", "dwo", "dga", "dba", "dwu", "dwd", "dgf", "dbf")


def layer_kernel(*refs):
    names = IN_NAMES + OUT_NAMES + tuple(n for n, _ in scratch_list())
    named = dict(zip(names, refs))
    r = types.SimpleNamespace(**named)
    for key in PER_PIECE:
        setattr(r, key, {p: named[key + p] for p in PIECES})
    me = lax.axis_index(DP)
    c = lax.axis_index(HEAD)
    x = lax.rem(me, 2)
    y = lax.rem(lax.div(me, 2), 2)
    z = lax.div(me, 4)
    u = x + c * (y - x)
    v = y + c * (x - y)
    ub = 1 + c
    vb = 2 - c
    zs = (z, z + 1 - 2 * lax.rem(z, 2), lax.rem(z + 2, 4), 3 - z)

    def chip(m):
        zm, du, dv = m // 4, (m // 2) % 2, m % 2
        uu = 1 - u if du else u
        vv = 1 - v if dv else v
        return 4 * zs[zm] + ub * uu + vb * vv

    ids = [chip(m) for m in range(16)]
    partner = (me, 1 - c)
    base256, base24, other24 = 256 * c, 24 * c, 24 * (1 - c)
    own_rows = pl.ds(pl.multiple_of(256 * c, 256), 256)
    oth_rows = pl.ds(pl.multiple_of(256 * (1 - c), 256), 256)

    peers = [partner] + [(ids[m], c) for m in (MU, MV, 4, 8, 12)]
    barrier = pltpu.get_barrier_semaphore()
    for dev in peers:
        pl.semaphore_signal(barrier, inc=1, device_id=dev, device_id_type=MESH)
    pl.semaphore_wait(barrier, len(peers))

    sends = []
    recv_ids = {}

    def recv_sem(key):
        if key not in recv_ids:
            recv_ids[key] = len(recv_ids)
        return r.rs.at[recv_ids[key]]

    def send(key, src, dst, dev):
        cp = pltpu.make_async_remote_copy(
            src_ref=src,
            dst_ref=dst,
            send_sem=r.ss.at[len(sends)],
            recv_sem=recv_sem(key),
            device_id=dev,
            device_id_type=MESH,
        )
        cp.start()
        sends.append((src, dst, len(sends), key, dev))

    def wait_send(entry):
        src, dst, k, key, dev = entry
        pltpu.make_async_remote_copy(
            src_ref=src,
            dst_ref=dst,
            send_sem=r.ss.at[k],
            recv_sem=recv_sem(key),
            device_id=dev,
            device_id_type=MESH,
        ).wait_send()

    waited = set()

    def wait_sent(key):
        for entry in sends:
            if entry[3] == key:
                wait_send(entry)
                waited.add(key)

    def wait_recv(key, ref):
        pltpu.make_async_remote_copy(
            src_ref=ref,
            dst_ref=ref,
            send_sem=r.ss.at[0],
            recv_sem=recv_sem(key),
            device_id=partner,
            device_id_type=MESH,
        ).wait_recv()

    def wbuf(p):
        return {"Q": r.WQ, "O": r.WOP.at[c], "U": r.WU, "D": r.WD}[p]

    starts = {}
    for n_rows in (48, 96):
        for m in range(16):
            first = pl.multiple_of(ids[m] * n_rows, 16)
            third = pl.multiple_of(ids[m] * n_rows + 2 * n_rows // 3, 16)
            starts[n_rows, m] = (first, third)

    def wslice(p, part, m):
        a, rows = APART[p], ROWS[p]
        first, third = starts[rows, m]
        if part == "A":
            return wbuf(p).at[pl.ds(first, a), :]
        return wbuf(p).at[pl.ds(third, rows - a), :]

    def forward(p, part, m, f):
        ref = wslice(p, part, m)
        send(("ag", p, part, m ^ f), ref, ref, (ids[f], c))

    def got(p, part, m):
        wait_recv(("ag", p, part, m), wslice(p, part, m))

    def ag_own(p):
        for f in (4, 8, 12):
            forward(p, "A", 0, f)
        forward(p, "C", 0, MU)
        forward(p, "A", 0, MU)
        forward(p, "A", 0, MV)
        for f in (4, 8, 12):
            forward(p, "C", 0, f)
        forward(p, "C", 0, MV)

    def ag_steps(p):
        steps = []

        def step(part, m, flips):
            def run():
                got(p, part, m)
                for f in flips:
                    forward(p, part, m, f)

            steps.append(run)

        step("C", MU, (4, 8, 12, MV))
        step("A", MU, (MV,))
        for zz in (4, 8, 12):
            step("A", zz, (MU, MV))
        for zz in (4, 8, 12):
            step("C", zz, (MV,))
            step("C", zz + MU, (MV,))
        for zz in (4, 8, 12):
            step("A", zz + MU, (MV,))
        return steps

    def ag_plane(p, zm):
        for m in (4 * zm + MV, 4 * zm + MU + MV):
            got(p, "A", m)
            got(p, "C", m)

    def run(steps):
        for s in steps:
            s()

    vec_peer = (partner, (ids[MU], c), (ids[MV], c), (ids[4], c), (ids[8], c))

    def vec_send(k, s):
        send(("v", k, s), r.VS.at[pl.ds(48 * k + 8 * s, 8), :], r.VR.at[pl.ds(40 * k + 8 * s, 8), :], vec_peer[s])

    def vec_step(k, s):
        src, got_row = pl.ds(48 * k + 8 * s, 8), pl.ds(40 * k + 8 * s, 8)
        wait_recv(("v", k, s), r.VR.at[got_row, :])
        r.VS[pl.ds(48 * k + 8 * s + 8, 8), :] = r.VS[src, :] + r.VR[got_row, :]
        if s < 4:
            vec_send(k, s + 1)

    def rs1_send(p, zm):
        rows = 2 * ROWS[p]
        s = pl.ds(zm * rows, rows)
        send(("r1", p, zm), r.S1[p].at[s, :], r.R1[p].at[s, :], (ids[MV], c))

    def rs_sum1(p, zm):
        rows, a = ROWS[p], APART[p]
        b = rows - a
        g, r1 = r.G[p], r.R1[p]
        s = pl.ds(zm * 2 * rows, 2 * rows)
        wait_recv(("r1", p, zm), r1.at[s, :])
        for du in (1, 0):
            o = (2 * zm + du) * rows
            top = g[o : o + a, :] + r1[o : o + a, :].astype(F32)
            low = g[o + a : o + rows, :] + r1[o + a : o + rows, :].astype(F32)
            if du == 1:
                q = pl.ds(zm * a, a)
                r.S2A[p][q, :] = top.astype(BF)
                send(("r2a", p, zm), r.S2A[p].at[q, :], r.R2A[p].at[q, :], (ids[MU], c))
            else:
                g[o : o + a, :] = top
            if zm:
                q = pl.ds(((zm - 1) * 2 + du) * b, b)
                r.S2C[p][q, :] = low.astype(BF)
            else:
                g[o + a : o + rows, :] = low
        if zm:
            q = pl.ds((zm - 1) * 2 * b, 2 * b)
            send(("r2c", p, zm), r.S2C[p].at[q, :], r.R2C[p].at[q, :], (ids[4 * zm], c))

    def rs_sum2a(p, zm):
        rows, a = ROWS[p], APART[p]
        g, r2 = r.G[p], r.R2A[p]
        q = pl.ds(zm * a, a)
        wait_recv(("r2a", p, zm), r2.at[q, :])
        o = 2 * zm * rows
        val = g[o : o + a, :] + r2[q, :].astype(F32)
        if zm:
            k = pl.ds((zm - 1) * a, a)
            r.S3A[p][k, :] = val.astype(BF)
            send(("r3a", p, zm), r.S3A[p].at[k, :], r.R3A[p].at[k, :], (ids[4 * zm], c))
        else:
            g[o : o + a, :] = val

    def rs_sum2c(p):
        rows, a = ROWS[p], APART[p]
        b = rows - a
        g, r2 = r.G[p], r.R2C[p]
        for zm in (1, 2, 3):
            wait_recv(("r2c", p, zm), r2.at[pl.ds((zm - 1) * 2 * b, 2 * b), :])
        for du in (1, 0):
            o = du * rows + a
            val = g[o : o + b, :]
            for zm in (1, 2, 3):
                k = ((zm - 1) * 2 + du) * b
                val = val + r2[k : k + b, :].astype(F32)
            if du == 1:
                r.S3C[p][...] = val.astype(BF)
                send(("r3c", p), r.S3C[p], r.R3C[p], (ids[MU], c))
            else:
                g[o : o + b, :] = val

    def rs_final(p):
        rows, a = ROWS[p], APART[p]
        g = r.G[p]
        r3a, r3c = r.R3A[p], r.R3C[p]
        for zm in (1, 2, 3):
            wait_recv(("r3a", p, zm), r3a.at[pl.ds((zm - 1) * a, a), :])
        val = g[0:a, :]
        for zm in (1, 2, 3):
            val = val + r3a[(zm - 1) * a : zm * a, :].astype(F32)
        g[0:a, :] = val
        wait_recv(("r3c", p), r3c)
        g[a:rows, :] = g[a:rows, :] + r3c[...].astype(F32)

    def block_row(zm, du, dv):
        uu = 1 - u if du else u
        vv = 1 - v if dv else v
        return ub * uu + vb * vv

    def stage(p, zm, src, base):
        rows, cols = ROWS[p], COLS[p]
        for du in (1, 0):
            k = (2 * zm + du) * rows
            far = pl.ds(pl.multiple_of(base + block_row(zm, du, 1) * rows, 8), rows)
            near = pl.ds(pl.multiple_of(base + block_row(zm, du, 0) * rows, 8), rows)
            r.S1[p][k : k + rows, :] = src[far, 0:cols].astype(BF)
            r.G[p][k : k + rows, :] = src[near, 0:cols]
        rs1_send(p, zm)

    r.WQ[pl.ds(pl.multiple_of(me * 48, 16), 48), 0:384] = r.wq[...].astype(BF)
    r.WQ[pl.ds(pl.multiple_of(me * 48, 16), 48), 384:768] = r.wk[...].astype(BF)
    r.WQ[pl.ds(pl.multiple_of(me * 48, 16), 48), 768:1152] = r.wv[...].astype(BF)
    ag_own("Q")
    send("tok", r.tok, r.X.at[own_rows, :], partner)
    local = pltpu.make_async_copy(r.tok, r.X.at[own_rows, :], r.ls.at[0])
    local.start()
    flat = 2 * me + c
    r.VS[0:8, :] = jnp.zeros((8, 768), F32)
    for k, n in enumerate(("ga", "ba", "gf", "bf")):
        r.VS[k : k + 1, 0:24] = getattr(r, n)[...].reshape(1, 24).astype(BF).astype(F32)
    r.VS[0:8, :] = pltpu.roll(r.VS[0:8, :], 24 * flat, 1)
    vec_send(0, 0)
    wo = r.wo[...]
    r.WOP[c, pl.ds(pl.multiple_of(me * 48, 16), 48), :] = jnp.concatenate(
        [wo[:, 0:384], wo[:, 384:768]], axis=0
    ).astype(BF)
    ag_own("O")
    r.WU[pl.ds(pl.multiple_of(me * 96, 16), 96), :] = r.wu[...].astype(BF)
    r.WD[pl.ds(pl.multiple_of(me * 96, 16), 96), :] = r.wd[...].astype(BF)

    col_pos = lax.broadcasted_iota(jnp.int32, (512, 128), 0)
    row_pos = lax.broadcasted_iota(jnp.int32, (8, 512), 1)
    col_lab = jnp.zeros((512, 128), jnp.int32)
    row_lab = jnp.zeros((8, 512), jnp.int32)
    for j in range(8):
        lo = r.off[0, j]
        hi = lo + r.len[0, j]
        col_lab = jnp.where((col_pos >= lo) & (col_pos < hi), j + 1, col_lab)
        row_lab = jnp.where((row_pos >= lo) & (row_pos < hi), j + 1, row_lab)
    r.LIVE[...] = jnp.where(col_lab > 0, 1.0, 0.0).astype(F32)
    row_lab = jnp.where(row_lab > 0, row_lab, -1)
    for t in range(4):
        q = slice(128 * t, 128 * t + 128)
        lab = jnp.concatenate([col_lab[q]] * 4, axis=1)
        same = lab == jnp.broadcast_to(row_lab[0:1], (128, 512))
        r.BIAS[q, :] = jnp.where(same, 0.0, -1e30).astype(F32)

    run(ag_steps("Q")[:7])
    ag_own("U")
    run(ag_steps("Q")[7:])
    o_steps, u_steps, d_steps = ag_steps("O"), ag_steps("U"), ag_steps("D")
    vec_step(0, 0)
    wait_recv("tok", r.X.at[own_rows, :])
    local.wait()
    run(o_steps[:4])
    for zm in range(4):
        ag_plane("Q", zm)

    for k, n in enumerate(("Q3", "K3", "V3")):
        full = mm(r.X[...], r.WQ[:, 384 * k : 384 * k + 384])
        full = full.astype(BF)
        if k == 0:
            full = full * BF(0.125)
        for i in range(3):
            getattr(r, n)[i] = full[:, 128 * i : 128 * i + 128]
    ag_own("D")
    vec_step(0, 1)

    for i in range(3):
        r.ATT[i] = jnp.zeros((512, 128), BF)
    fw_hooks = [
        o_steps[4:9],
        o_steps[9:] + u_steps[:1],
        [functools.partial(vec_step, 0, 2)] + u_steps[1:4],
        u_steps[4:7],
        [functools.partial(vec_step, 0, 3)] + u_steps[7:10],
        u_steps[10:],
    ]
    lane = lax.broadcasted_iota(jnp.int32, (1, 128), 1)

    def half(val, a):
        keep = (lane >= 64 * a) & (lane < 64 * a + 64)
        return jnp.where(keep, val, jnp.zeros_like(val))

    def at_index(h, hooks):
        for k, steps in enumerate(hooks):

            def go(steps=steps):
                run(steps)

            pl.when(h == k)(go)

    def fwd_head(h, carry):
        at_index(h, fw_hooks)
        i = lax.div(h, 2)
        a = lax.rem(h, 2)
        vals = half(r.V3[i], a)
        keys = half(r.K3[i], a)
        for t in range(4):
            q = slice(128 * t, 128 * t + 128)
            s = mm(r.Q3[i, q, :], keys, 1, 1) + r.BIAS[q, :]
            live = r.LIVE[q, 0:1]
            top = jnp.where(live > 0, jnp.max(s, axis=1, keepdims=True), 0.0)
            w = jnp.exp(s - top)
            total = jnp.sum(w, axis=1, keepdims=True) + (1.0 - live)
            prob = w * (1.0 / total)
            r.P32[h, q, :] = prob
            o = mm(prob.astype(BF), vals)
            r.ATT[i, q, :] = r.ATT[i, q, :] + o.astype(BF)
        return carry

    lax.fori_loop(0, 6, fwd_head, 0)

    send("att", r.ATT.at[:, oth_rows, :], r.ATTR, partner)
    for zm in range(4):
        ag_plane("O", zm)
    send("wop", r.WOP.at[c], r.WOP.at[c], partner)
    run(d_steps[:4])
    vec_step(0, 4)
    wait_recv("wop", r.WOP.at[1 - c])

    def build_out(i, carry):
        for k in range(2):
            blk = r.WOP[k, pl.ds(pl.multiple_of(48 * i, 16), 48), :].astype(F32)
            rows = jnp.concatenate([blk[0:24], blk[24:48]], axis=1)
            r.T[pl.ds(pl.multiple_of(48 * i + 24 * k, 8), 24), 0:768] = rows
        return carry

    lax.fori_loop(0, 16, build_out, 0)
    r.WO[...] = r.T[:, 0:768].astype(BF)
    wait_recv("att", r.ATTR)
    own_heads = pl.ds(pl.multiple_of(384 * c, 128), 384)
    oth_heads = pl.ds(pl.multiple_of(384 * (1 - c), 128), 384)

    def joined(ref, rows):
        return jnp.concatenate([ref[i, rows, :] for i in range(3)], axis=1)

    all256 = pl.ds(0, 256)
    branch = mm(joined(r.ATT, own_rows), r.WO[own_heads, :])
    branch = branch + mm(joined(r.ATTR, all256), r.WO[oth_heads, :])
    r.GS[...] = branch
    run(d_steps[4:6])

    def norm(val):
        mean = jnp.mean(val, axis=1, keepdims=True)
        cen = val - mean
        inv = lax.rsqrt(jnp.mean(cen * cen, axis=1, keepdims=True) + EPS)
        return cen * inv, inv

    def ln1(t, carry):
        q = pl.ds(pl.multiple_of(64 * t, 64), 64)
        unit, inv = norm(r.tok[q, :].astype(F32) + r.GS[q, :])
        r.U1[q, :] = unit
        r.INV1[q, :] = jnp.broadcast_to(inv, (64, 128))
        one = unit * r.VS[40:41, :] + r.VS[41:42, :]
        r.N1[q, :] = one
        r.FIN[pl.ds(pl.multiple_of(base256 + 64 * t, 64), 64), :] = one.astype(BF)
        return carry

    lax.fori_loop(0, 4, ln1, 0)
    send("fin", r.FIN.at[own_rows, :], r.FIN.at[own_rows, :], partner)
    run(d_steps[6:8])
    wait_recv("fin", r.FIN.at[oth_rows, :])

    def plane_rows(zm):
        return pl.ds(pl.multiple_of(384 * zs[zm], 128), 384)

    def ffn_up(zm):
        for t in range(2):
            q = slice(256 * t, 256 * t + 256)
            pre = mm(r.FIN[q, :], r.WU[plane_rows(zm), :], 1, 1)
            r.GEL[zm, q, :] = pre

        def act(t, carry):
            q = pl.ds(pl.multiple_of(64 * t, 64), 64)
            pre = r.GEL[zm, q, :]
            cdf = 0.5 * (1.0 + lax.erf(pre * (2.0**-0.5)))
            pdf = jnp.exp(-0.5 * pre * pre) * (1.0 / math.sqrt(2.0 * math.pi))
            r.HID[zm, q, :] = (pre * cdf).astype(BF)
            r.GEL[zm, q, :] = cdf + pre * pdf
            return carry

        lax.fori_loop(0, 8, act, 0)

    d_groups = (d_steps[8:10], d_steps[10:12], d_steps[12:], [])
    for zm in range(4):
        ag_plane("U", zm)
        ffn_up(zm)
        run(d_groups[zm])
    for zm in range(4):
        ag_plane("D", zm)
        for rows in (oth_rows, own_rows):
            part = mm(r.HID[zm, rows, :], r.WD[plane_rows(zm), :])
            if zm:
                part = part + r.SEC[rows, :]
            r.SEC[rows, :] = part
            if zm == 3 and rows is oth_rows:
                send("sec", r.SEC.at[oth_rows, :], r.SECR, partner)
    wait_recv("sec", r.SECR)

    def ln2(t, sums):
        dg, db = sums
        q = pl.ds(pl.multiple_of(64 * t, 64), 64)
        qq = pl.ds(pl.multiple_of(base256 + 64 * t, 64), 64)
        unit, inv = norm(r.N1[q, :] + (r.SEC[qq, :] + r.SECR[q, :]))
        gain = r.VS[42:43, :]
        r.out[q, :] = (unit * gain + r.VS[43:44, :]).astype(BF)
        e = r.og[q, :].astype(F32)
        dg = dg + jnp.sum(e * unit, axis=0, keepdims=True)
        db = db + jnp.sum(e, axis=0, keepdims=True)
        eg = e * gain
        inner = jnp.mean(eg * unit, axis=1, keepdims=True)
        gs = inv * (eg - jnp.mean(eg, axis=1, keepdims=True) - unit * inner)
        r.GS[q, :] = gs
        r.GFB[qq, :] = gs.astype(BF)
        return dg, db

    zero = jnp.zeros((1, 768), F32)
    dg2, db2 = lax.fori_loop(0, 4, ln2, (zero, zero))
    send("gfb", r.GFB.at[own_rows, :], r.GFB.at[own_rows, :], partner)
    wait_recv("gfb", r.GFB.at[oth_rows, :])
    wait_sent("sec")

    for n_done, zm in enumerate((3, 2, 1, 0)):
        r.T[0:384, 0:768] = mm(r.HID[zm], r.GFB[...], 0, 0)
        stage("D", zm, r.T, 0)
        for t in range(2):
            q = slice(256 * t, 256 * t + 256)
            gh = mm(r.GFB[q, :], r.WD[plane_rows(zm), :], 1, 1)
            r.HID[zm, q, :] = (gh * r.GEL[zm, q, :]).astype(BF)
        r.T[384:768, 0:768] = mm(r.HID[zm], r.FIN[...], 0, 0)
        stage("U", zm, r.T, 384)
        for rows in (oth_rows, own_rows):
            part = mm(r.HID[zm, rows, :], r.WU[plane_rows(zm), :])
            if n_done:
                part = part + r.SEC[rows, :]
            r.SEC[rows, :] = part
            if n_done == 3 and rows is oth_rows:
                send("gn", r.SEC.at[oth_rows, :], r.SECR, partner)
        if n_done:
            rs_sum1("D", zm + 1)
    wait_recv("gn", r.SECR)

    def ln1_back(t, sums):
        dg, db = sums
        q = pl.ds(pl.multiple_of(64 * t, 64), 64)
        qq = pl.ds(pl.multiple_of(base256 + 64 * t, 64), 64)
        e = r.GS[q, :] + (r.SEC[qq, :] + r.SECR[q, :])
        unit = r.U1[q, :]
        inv = r.INV1[q, 0:1]
        dg = dg + jnp.sum(e * unit, axis=0, keepdims=True)
        db = db + jnp.sum(e, axis=0, keepdims=True)
        eg = e * r.VS[40:41, :]
        inner = jnp.mean(eg * unit, axis=1, keepdims=True)
        first = inv * (eg - jnp.mean(eg, axis=1, keepdims=True) - unit * inner)
        r.GS[q, :] = first
        r.GB[q, :] = first.astype(BF)
        return dg, db

    dg1, db1 = lax.fori_loop(0, 4, ln1_back, (zero, zero))
    r.VS[48:56, :] = jnp.zeros((8, 768), F32)
    for k, val in enumerate((dg1, db1, dg2, db2)):
        r.VS[48 + k : 49 + k, :] = val
    vec_send(1, 0)

    gview = mm(r.GB[...], r.WO[oth_heads, :], 1, 1).astype(BF)
    for i in range(3):
        r.GAS[i] = gview[:, 128 * i : 128 * i + 128]
    send("gas", r.GAS, r.GA.at[:, own_rows, :], partner)
    gview = mm(r.GB[...], r.WO[own_heads, :], 1, 1).astype(BF)
    for i in range(3):
        r.GA[i, own_rows, :] = gview[:, 128 * i : 128 * i + 128]
    rs_sum1("D", 0)
    r.T[own_heads, 0:768] = mm(joined(r.ATT, own_rows), r.GB[...], 0, 0)
    r.T[oth_heads, 0:768] = mm(joined(r.ATTR, all256), r.GB[...], 0, 0)

    def pair_out(i, carry):
        q = pl.ds(pl.multiple_of(48 * i, 16), 48)
        blk = r.T[pl.ds(pl.multiple_of(48 * i + other24, 8), 24), 0:768]
        r.S0[q, :] = jnp.concatenate([blk[:, 0:384], blk[:, 384:768]], axis=0).astype(BF)
        return carry

    lax.fori_loop(0, 16, pair_out, 0)
    send("s0", r.S0, r.R0, partner)
    rs_sum1("U", 3)
    rs_sum1("U", 2)
    wait_recv("s0", r.R0)

    def out_block(m):
        i = ids[m]
        blk = r.T[pl.ds(pl.multiple_of(48 * i + base24, 8), 24), 0:768]
        blk = jnp.concatenate([blk[:, 0:384], blk[:, 384:768]], axis=0)
        return blk + r.R0[pl.ds(pl.multiple_of(48 * i, 16), 48), :].astype(F32)

    for zm in (3, 2, 1, 0):
        for du in (1, 0):
            k = (2 * zm + du) * 48
            r.S1["O"][k : k + 48, :] = out_block(4 * zm + 2 * du + 1).astype(BF)
            r.G["O"][k : k + 48, :] = out_block(4 * zm + 2 * du)
        rs1_send("O", zm)

    wait_recv("gas", r.GA.at[:, oth_rows, :])
    for n in ("DQ", "DK", "DV"):
        for i in range(3):
            getattr(r, n)[i] = jnp.zeros((512, 128), BF)

    def s1(p, zm):
        return functools.partial(rs_sum1, p, zm)

    def s2a(p, zm):
        return functools.partial(rs_sum2a, p, zm)

    def s2c(p):
        return functools.partial(rs_sum2c, p)

    def vs(s):
        return functools.partial(vec_step, 1, s)

    bw_hooks = [
        [s1("U", 1), s2a("D", 3), s2a("D", 2), vs(0)],
        [s1("U", 0), s2a("D", 1), s2a("D", 0), s2c("D")],
        [s2a("U", 3), s2a("U", 2), vs(1), s1("O", 3), s1("O", 2)],
        [s2a("U", 1), s2a("U", 0), s2c("U"), s1("O", 1), s1("O", 0)],
        [functools.partial(rs_final, "D"), vs(2)],
        [s2a("O", 3), s2a("O", 2), s2a("O", 1), s2a("O", 0), s2c("O"), vs(3)],
    ]

    def bwd_head(h, carry):
        at_index(h, bw_hooks)
        i = lax.div(h, 2)
        a = lax.rem(h, 2)
        go = half(r.GA[i], a)
        for t in range(4):
            q = slice(128 * t, 128 * t + 128)
            prob = r.P32[h, q, :]
            dp = mm(go[q], r.V3[i], 1, 1)
            delta = jnp.sum(prob * dp, axis=1, keepdims=True)
            r.DSB[q, :] = (prob * (dp - delta)).astype(BF)
            r.PB[q, :] = prob.astype(BF)
        r.DV[i] = r.DV[i] + mm(r.PB[...], go, 0, 0).astype(BF)
        dq = mm(r.DSB[...], half(r.K3[i], a)) * 0.125
        r.DQ[i] = r.DQ[i] + dq.astype(BF)
        dk = mm(r.DSB[...], half(r.Q3[i], a), 0, 0)
        r.DK[i] = r.DK[i] + dk.astype(BF)
        return carry

    lax.fori_loop(0, 6, bwd_head, 0)

    all512 = pl.ds(0, 512)
    for k, n in enumerate(("DQ", "DK", "DV")):
        r.T[:, 384 * k : 384 * k + 384] = mm(r.X[...], joined(getattr(r, n), all512), 0, 0)
    for zm in (3, 2, 1, 0):
        stage("Q", zm, r.T, 192 * zs[zm])
    run([functools.partial(rs_final, "U"), vs(4)])

    for rows in (oth_rows, own_rows):
        acc = mm(joined(r.DQ, rows), r.WQ[:, 0:384], 1, 1)
        acc = acc + mm(joined(r.DK, rows), r.WQ[:, 384:768], 1, 1)
        acc = acc + mm(joined(r.DV, rows), r.WQ[:, 768:1152], 1, 1)
        if rows is oth_rows:
            r.IGS[...] = acc.astype(BF)
            send("ig", r.IGS, r.IGR, partner)
        else:
            r.GS[...] = r.GS[...] + acc
    wait_recv("ig", r.IGR)
    r.ig[...] = (r.GS[...] + r.IGR[...].astype(F32)).astype(BF)

    for zm in (3, 2, 1, 0):
        rs_sum1("Q", zm)
    rs_final("O")
    for zm in (3, 2, 1, 0):
        rs_sum2a("Q", zm)
    rs_sum2c("Q")
    r.dwd[...] = r.G["D"][0:96, :]
    r.dwu[...] = r.G["U"][0:96, :]
    go = r.G["O"][0:48, :]
    r.dwo[...] = jnp.concatenate([go[0:24], go[24:48]], axis=1)
    back = pltpu.roll(r.VS[88:96, :], lax.rem(768 - 24 * flat, 768), 1)
    for k, n in enumerate(("dga", "dba", "dgf", "dbf")):
        getattr(r, n)[...] = back[k, 0:24]
    rs_final("Q")
    r.dwq[...] = r.G["Q"][0:48, 0:384]
    r.dwk[...] = r.G["Q"][0:48, 384:768]
    r.dwv[...] = r.G["Q"][0:48, 768:1152]

    for entry in sends:
        if entry[3] not in waited:
            wait_send(entry)


def hand_over(*refs):
    half = len(refs) // 2
    for src, dst in zip(refs[:half], refs[half:]):
        dst[...] = src[...]


def layer_small(*args):
    shapes = (
        ((256, 768), BF),
        ((256, 768), BF),
        ((48, 384), F32),
        ((48, 384), F32),
        ((48, 384), F32),
        ((24, 768), F32),
        ((24,), F32),
        ((24,), F32),
        ((96, 768), F32),
        ((96, 768), F32),
        ((24,), F32),
        ((24,), F32),
    )
    vmem = pl.BlockSpec(memory_space=pltpu.VMEM)
    smem = pl.BlockSpec(memory_space=pltpu.SMEM)
    out_shape = tuple(jax.ShapeDtypeStruct(s, d) for s, d in shapes)
    up = IN_NAMES.index("wu")
    args = args[:up] + (args[up].T,) + args[up + 1 :]
    outs = pl.pallas_call(
        layer_kernel,
        out_shape=out_shape,
        in_specs=[smem if n in ("len", "off") else vmem for n in IN_NAMES],
        out_specs=tuple(vmem for _ in shapes),
        scratch_shapes=[s for _, s in scratch_list()],
        compiler_params=pltpu.CompilerParams(
            collective_id=0, has_side_effects=True, vmem_limit_bytes=67043328
        ),
    )(*args)
    outs = pl.pallas_call(
        hand_over,
        out_shape=out_shape,
        in_specs=[vmem for _ in shapes],
        out_specs=tuple(vmem for _ in shapes),
    )(*outs)
    up = OUT_NAMES.index("dwu")
    return outs[:up] + (outs[up].T,) + outs[up + 1 :]


def labels_of(lengths, offsets):
    position = jnp.arange(BIN, dtype=jnp.int32)[:, None]
    starts = offsets[None, :]
    inside = (position >= starts) & (position < starts + lengths[None, :])
    slot_order = jnp.arange(1, lengths.shape[0] + 1, dtype=jnp.int32)[None, :]
    return jnp.sum(jnp.where(inside, slot_order, 0), axis=1)


def layer_norm(operand, gain_vec, bias_vec):
    row_mean = jnp.mean(operand, axis=-1, keepdims=True)
    centered = operand - row_mean
    inverse = lax.rsqrt(jnp.mean(centered * centered, axis=-1, keepdims=True) + EPS)
    normed = centered * inverse
    return (normed * gain_vec + bias_vec, normed, inverse)


def norm_back(grad_rows, normed, inverse, gain_vec):
    scaled = grad_rows * gain_vec
    inner = jnp.mean(scaled * normed, axis=-1, keepdims=True)
    return inverse * (scaled - jnp.mean(scaled, axis=-1, keepdims=True) - normed * inner)


def gelu_exact(operand):
    return jax.nn.gelu(operand, approximate=False)


def contract_rows(left, right):
    return lax.dot_general(
        left, right, (((0,), (0,)), ((), ())), preferred_element_type=F32
    )


def contract_cols(left, right):
    return lax.dot_general(
        left, right, (((1,), (1,)), ((), ())), preferred_element_type=F32
    )


def score_block(queries, key_rows, labels_bin, factor):
    scores = (
        jnp.einsum("qhd,khd->hqk", queries, key_rows, preferred_element_type=F32) * factor
    )
    allowed = ((labels_bin[:, None] == labels_bin[None, :]) & (labels_bin[:, None] > 0))[None]
    live_rows = (labels_bin > 0)[None, :, None]
    return (scores, allowed, live_rows)


def masked_exp(scores, allowed, row_top):
    return jnp.where(allowed, jnp.exp(jnp.where(allowed, scores - row_top, 0.0)), 0.0)


def attend_bin(pieces, factor):
    queries, key_rows, value_rows, labels_bin = pieces
    scores, allowed, live_rows = score_block(queries, key_rows, labels_bin, factor)
    row_top = jnp.max(jnp.where(allowed, scores, -1e30), axis=2, keepdims=True)
    row_top = jnp.where(live_rows, row_top, 0.0)
    weights = masked_exp(scores, allowed, row_top)
    denominator = jnp.sum(weights, axis=2, keepdims=True) + jnp.where(live_rows, 0.0, 1.0)
    probability = (weights / denominator).astype(jnp.bfloat16)
    mixed_rows = jnp.einsum(
        "hqk,khd->qhd", probability, value_rows, preferred_element_type=F32
    )
    return (mixed_rows.astype(jnp.bfloat16), row_top, denominator)


def attend_back(pieces, factor):
    queries, key_rows, value_rows, labels_bin, row_top, denominator, grad_mixed = pieces
    scores, allowed, live_rows = score_block(queries, key_rows, labels_bin, factor)
    probability = masked_exp(scores, allowed, row_top) / denominator
    grad_values = jnp.einsum(
        "hqk,qhd->khd",
        probability.astype(jnp.bfloat16),
        grad_mixed,
        preferred_element_type=F32,
    )
    grad_probs = jnp.einsum(
        "qhd,khd->hqk", grad_mixed, value_rows, preferred_element_type=F32
    )
    row_delta = jnp.sum(probability * grad_probs, axis=2, keepdims=True)
    grad_scores = (probability * (grad_probs - row_delta)).astype(jnp.bfloat16)
    grad_queries = (
        jnp.einsum("hqk,khd->qhd", grad_scores, key_rows, preferred_element_type=F32)
        * factor
    )
    grad_keys = (
        jnp.einsum("hqk,qhd->khd", grad_scores, queries, preferred_element_type=F32)
        * factor
    )
    return (
        grad_queries.astype(jnp.bfloat16),
        grad_keys.astype(jnp.bfloat16),
        grad_values.astype(jnp.bfloat16),
    )


def per_device(
    tokens,
    w_query,
    w_key,
    w_value,
    w_out,
    gain_attn,
    bias_attn,
    w_up,
    w_down,
    gain_ffn,
    bias_ffn,
    seq_lengths,
    seq_offsets,
    out_grad,
):
    low_type = jnp.bfloat16
    bin_count = seq_lengths.shape[0]
    group_rows = bin_count * BIN
    head_width = w_query.shape[1]
    local_heads = head_width // HD
    factor = 1.0 / math.sqrt(HD)
    labels = jax.vmap(labels_of)(seq_lengths, seq_offsets)
    full_query, full_key, full_value = (
        lax.all_gather(w_query.astype(low_type), DP, axis=0, tiled=True),
        lax.all_gather(w_key.astype(low_type), DP, axis=0, tiled=True),
        lax.all_gather(w_value.astype(low_type), DP, axis=0, tiled=True),
    )
    projection = jnp.concatenate([full_query, full_key, full_value], axis=1)
    whole_rows = lax.all_gather(tokens, HEAD, axis=0, tiled=True)
    projected = jnp.dot(whole_rows, projection, preferred_element_type=F32).astype(low_type)
    shape_bins = (bin_count, BIN, local_heads, HD)
    queries = projected[:, :head_width].reshape(shape_bins)
    key_rows = projected[:, head_width : 2 * head_width].reshape(shape_bins)
    value_rows = projected[:, 2 * head_width :].reshape(shape_bins)
    mixed_bins, row_tops, denominators = lax.map(
        lambda pieces: attend_bin(pieces, factor), (queries, key_rows, value_rows, labels)
    )
    attended = mixed_bins.reshape(group_rows, head_width)
    out_full, up_part, down_part, gain_one, bias_one, gain_two, bias_two = (
        lax.all_gather(w_out.astype(low_type), BOTH, axis=0, tiled=True),
        lax.all_gather(w_up.astype(low_type), BOTH, axis=1, tiled=True),
        lax.all_gather(w_down.astype(low_type), BOTH, axis=0, tiled=True),
        lax.all_gather(gain_attn.astype(low_type), BOTH, axis=0, tiled=True),
        lax.all_gather(bias_attn.astype(low_type), BOTH, axis=0, tiled=True),
        lax.all_gather(gain_ffn.astype(low_type), BOTH, axis=0, tiled=True),
        lax.all_gather(bias_ffn.astype(low_type), BOTH, axis=0, tiled=True),
    )
    gain_first = gain_one.astype(F32)
    gain_second = gain_two.astype(F32)
    token_view = lax.all_to_all(attended, HEAD, split_axis=0, concat_axis=1, tiled=True)
    first_sum = tokens.astype(F32) + jnp.dot(
        token_view, out_full, preferred_element_type=F32
    )
    normed_one, unit_one, inverse_one = layer_norm(
        first_sum, gain_first, bias_one.astype(F32)
    )
    ffn_input = normed_one.astype(low_type)
    pre_act = jnp.dot(ffn_input, up_part, preferred_element_type=F32)
    activated, gelu_pull = jax.vjp(gelu_exact, pre_act)
    hidden = activated.astype(low_type)
    second_sum = normed_one + jnp.dot(hidden, down_part, preferred_element_type=F32)
    result, unit_two, inverse_two = layer_norm(
        second_sum, gain_second, bias_two.astype(F32)
    )
    output = result.astype(low_type)
    grad_result = out_grad.astype(F32)
    grad_gain_two = jnp.sum(grad_result * unit_two, axis=0)
    grad_bias_two = jnp.sum(grad_result, axis=0)
    grad_second = norm_back(grad_result, unit_two, inverse_two, gain_second)
    grad_ffn = grad_second.astype(low_type)
    grad_down_part = contract_rows(hidden, grad_ffn)
    grad_pre = gelu_pull(contract_cols(grad_ffn, down_part))[0].astype(low_type)
    grad_up_part = contract_rows(ffn_input, grad_pre)
    grad_normed = grad_second + contract_cols(grad_pre, up_part)
    grad_gain_one = jnp.sum(grad_normed * unit_one, axis=0)
    grad_bias_one = jnp.sum(grad_normed, axis=0)
    grad_first = norm_back(grad_normed, unit_one, inverse_one, gain_first)
    grad_branch = grad_first.astype(low_type)
    grad_out_full = contract_rows(token_view, grad_branch)
    part_out, part_up, part_down, part_gain_one, part_bias_one, part_gain_two, part_bias_two = (
        lax.psum_scatter(grad_out_full, BOTH, scatter_dimension=0, tiled=True),
        lax.psum_scatter(grad_up_part, BOTH, scatter_dimension=1, tiled=True),
        lax.psum_scatter(grad_down_part, BOTH, scatter_dimension=0, tiled=True),
        lax.psum_scatter(grad_gain_one, BOTH, scatter_dimension=0, tiled=True),
        lax.psum_scatter(grad_bias_one, BOTH, scatter_dimension=0, tiled=True),
        lax.psum_scatter(grad_gain_two, BOTH, scatter_dimension=0, tiled=True),
        lax.psum_scatter(grad_bias_two, BOTH, scatter_dimension=0, tiled=True),
    )
    grad_token_view = contract_cols(grad_branch, out_full).astype(low_type)
    grad_attended = lax.all_to_all(grad_token_view, HEAD, split_axis=1, concat_axis=0, tiled=True)
    grad_bins = grad_attended.reshape(shape_bins)
    grad_queries, grad_keys, grad_values = lax.map(
        lambda pieces: attend_back(pieces, factor),
        (queries, key_rows, value_rows, labels, row_tops, denominators, grad_bins),
    )
    grad_projected = jnp.concatenate(
        [
            grad_queries.reshape(group_rows, head_width),
            grad_keys.reshape(group_rows, head_width),
            grad_values.reshape(group_rows, head_width),
        ],
        axis=1,
    )
    grad_projection = contract_rows(whole_rows, grad_projected)
    part_query, part_key, part_value = (
        lax.psum_scatter(grad_projection[:, :head_width], DP, scatter_dimension=0, tiled=True),
        lax.psum_scatter(
            grad_projection[:, head_width : 2 * head_width], DP, scatter_dimension=0, tiled=True
        ),
        lax.psum_scatter(
            grad_projection[:, 2 * head_width :], DP, scatter_dimension=0, tiled=True
        ),
    )
    input_grad = (
        grad_first
        + lax.psum_scatter(
            contract_cols(grad_projected, projection).astype(jnp.bfloat16),
            HEAD,
            scatter_dimension=0,
            tiled=True,
        ).astype(F32)
    ).astype(low_type)
    return (
        output,
        input_grad,
        part_query,
        part_key,
        part_value,
        part_out,
        part_gain_one,
        part_bias_one,
        part_up,
        part_down,
        part_gain_two,
        part_bias_two,
    )


def solution(mesh):
    small = mesh.shape[DP] == 16 and mesh.shape[HEAD] == 2
    return jax.shard_map(
        layer_small if small else per_device,
        mesh=mesh,
        in_specs=(
            P(BOTH, None),
            P(DP, HEAD),
            P(DP, HEAD),
            P(DP, HEAD),
            P(BOTH, None),
            P(BOTH),
            P(BOTH),
            P(None, BOTH),
            P(BOTH, None),
            P(BOTH),
            P(BOTH),
            P(DP, None),
            P(DP, None),
            P(BOTH, None),
        ),
        out_specs=(
            P(BOTH, None),
            P(BOTH, None),
            P(DP, HEAD),
            P(DP, HEAD),
            P(DP, HEAD),
            P(BOTH, None),
            P(BOTH),
            P(BOTH),
            P(None, BOTH),
            P(BOTH, None),
            P(BOTH),
            P(BOTH),
        ),
        check_vma=False,
    )
```

```python
import functools
import math
import types

import jax
import jax.numpy as jnp
from jax import lax
from jax.experimental import pallas as pl
from jax.experimental.pallas import tpu as pltpu
from jax.sharding import PartitionSpec as P

HD = 64
BIN = 512
EPS = 1e-12
F32 = jnp.float32
BF = jnp.bfloat16
MESH = pl.DeviceIdType.MESH

MU, MV = 2, 1
ROWS = {"Q": 48, "O": 48, "U": 96, "D": 96}
COLS = {"Q": 1152, "O": 384, "U": 768, "D": 768}
APART = {"Q": 32, "O": 32, "U": 64, "D": 64}
PIECES = ("Q", "O", "U", "D")
PER_PIECE = ("G", "S1", "R1", "S2A", "R2A", "S3A", "R3A", "S2C", "R2C", "S3C", "R3C")
DP, HEAD = "dp", "head"
BOTH = (DP, HEAD)
COPIES = 200


def mm(a, b, ca=1, cb=0):
    return lax.dot_general(a, b, (((ca,), (cb,)), ((), ())), preferred_element_type=F32)


def scratch_list():
    items = []

    def add(name, shape, dtype):
        items.append((name, pltpu.VMEM(shape, dtype)))

    add("X", (512, 768), BF)
    add("WQ", (768, 1152), BF)
    add("WOP", (2, 768, 384), BF)
    add("WO", (768, 768), BF)
    add("WU", (1536, 768), BF)
    add("WD", (1536, 768), BF)
    for n in ("Q3", "K3", "V3", "ATT", "GA", "DQ", "DK", "DV"):
        add(n, (3, 512, 128), BF)
    add("ATTR", (3, 256, 128), BF)
    add("GAS", (3, 256, 128), BF)
    add("BIAS", (512, 512), F32)
    add("LIVE", (512, 128), F32)
    add("P32", (6, 512, 512), F32)
    add("PB", (512, 512), BF)
    add("DSB", (512, 512), BF)
    add("U1", (256, 768), F32)
    add("N1", (256, 768), F32)
    add("INV1", (256, 128), F32)
    add("FIN", (512, 768), BF)
    add("HID", (4, 512, 384), BF)
    add("GEL", (4, 512, 384), F32)
    add("SEC", (512, 768), F32)
    add("SECR", (256, 768), F32)
    add("GS", (256, 768), F32)
    add("GFB", (512, 768), BF)
    add("GB", (256, 768), BF)
    add("IGS", (256, 768), BF)
    add("IGR", (256, 768), BF)
    add("T", (768, 1152), F32)
    add("S0", (768, 384), BF)
    add("R0", (768, 384), BF)
    for p in PIECES:
        r, c, a = ROWS[p], COLS[p], APART[p]
        b = r - a
        sizes = (8 * r, 8 * r, 8 * r, 4 * a, 4 * a, 3 * a, 3 * a, 6 * b, 6 * b, b, b)
        for key, size in zip(PER_PIECE, sizes):
            add(key + p, (size, c), F32 if key == "G" else BF)
    add("VS", (96, 768), F32)
    add("VR", (80, 768), F32)
    items.append(("ss", pltpu.SemaphoreType.DMA((COPIES,))))
    items.append(("rs", pltpu.SemaphoreType.DMA((COPIES,))))
    items.append(("ls", pltpu.SemaphoreType.DMA((1,))))
    return items


IN_NAMES = ("tok", "wq", "wk", "wv", "wo", "ga", "ba", "wu", "wd", "gf", "bf", "len", "off", "og")
OUT_NAMES = ("out", "ig", "dwq", "dwk", "dwv", "dwo", "dga", "dba", "dwu", "dwd", "dgf", "dbf")


def layer_kernel(*refs):
    names = IN_NAMES + OUT_NAMES + tuple(n for n, _ in scratch_list())
    named = dict(zip(names, refs))
    r = types.SimpleNamespace(**named)
    for key in PER_PIECE:
        setattr(r, key, {p: named[key + p] for p in PIECES})
    me = lax.axis_index(DP)
    c = lax.axis_index(HEAD)
    x = lax.rem(me, 2)
    y = lax.rem(lax.div(me, 2), 2)
    z = lax.div(me, 4)
    u = x + c * (y - x)
    v = y + c * (x - y)
    ub = 1 + c
    vb = 2 - c
    zs = (z, z + 1 - 2 * lax.rem(z, 2), lax.rem(z + 2, 4), 3 - z)

    def chip(m):
        zm, du, dv = m // 4, (m // 2) % 2, m % 2
        uu = 1 - u if du else u
        vv = 1 - v if dv else v
        return 4 * zs[zm] + ub * uu + vb * vv

    ids = [chip(m) for m in range(16)]
    partner = (me, 1 - c)
    base256, base24, other24 = 256 * c, 24 * c, 24 * (1 - c)
    own_rows = pl.ds(pl.multiple_of(256 * c, 256), 256)
    oth_rows = pl.ds(pl.multiple_of(256 * (1 - c), 256), 256)

    peers = [partner] + [(ids[m], c) for m in (MU, MV, 4, 8, 12)]
    barrier = pltpu.get_barrier_semaphore()
    for dev in peers:
        pl.semaphore_signal(barrier, inc=1, device_id=dev, device_id_type=MESH)
    pl.semaphore_wait(barrier, len(peers))

    sends = []
    recv_ids = {}

    def recv_sem(key):
        if key not in recv_ids:
            recv_ids[key] = len(recv_ids)
        return r.rs.at[recv_ids[key]]

    def send(key, src, dst, dev):
        cp = pltpu.make_async_remote_copy(
            src_ref=src,
            dst_ref=dst,
            send_sem=r.ss.at[len(sends)],
            recv_sem=recv_sem(key),
            device_id=dev,
            device_id_type=MESH,
        )
        cp.start()
        sends.append((src, dst, len(sends), key, dev))

    def wait_send(entry):
        src, dst, k, key, dev = entry
        pltpu.make_async_remote_copy(
            src_ref=src,
            dst_ref=dst,
            send_sem=r.ss.at[k],
            recv_sem=recv_sem(key),
            device_id=dev,
            device_id_type=MESH,
        ).wait_send()

    waited = set()

    def wait_sent(key):
        for entry in sends:
            if entry[3] == key:
                wait_send(entry)
                waited.add(key)

    def wait_recv(key, ref):
        pltpu.make_async_remote_copy(
            src_ref=ref,
            dst_ref=ref,
            send_sem=r.ss.at[0],
            recv_sem=recv_sem(key),
            device_id=partner,
            device_id_type=MESH,
        ).wait_recv()

    def wbuf(p):
        return {"Q": r.WQ, "O": r.WOP.at[c], "U": r.WU, "D": r.WD}[p]

    starts = {}
    for n_rows in (48, 96):
        for m in range(16):
            first = pl.multiple_of(ids[m] * n_rows, 16)
            third = pl.multiple_of(ids[m] * n_rows + 2 * n_rows // 3, 16)
            starts[n_rows, m] = (first, third)

    def wslice(p, part, m):
        a, rows = APART[p], ROWS[p]
        first, third = starts[rows, m]
        if part == "A":
            return wbuf(p).at[pl.ds(first, a), :]
        return wbuf(p).at[pl.ds(third, rows - a), :]

    def forward(p, part, m, f):
        ref = wslice(p, part, m)
        send(("ag", p, part, m ^ f), ref, ref, (ids[f], c))

    def got(p, part, m):
        wait_recv(("ag", p, part, m), wslice(p, part, m))

    def ag_own(p):
        forward(p, "C", 0, MU)
        for f in (4, 8, 12):
            forward(p, "A", 0, f)
        forward(p, "A", 0, MU)
        forward(p, "A", 0, MV)
        for f in (4, 8, 12):
            forward(p, "C", 0, f)
        forward(p, "C", 0, MV)

    def ag_steps(p):
        steps = []

        def step(part, m, flips):
            def run():
                got(p, part, m)
                for f in flips:
                    forward(p, part, m, f)

            steps.append(run)

        step("C", MU, (4, 8, 12, MV))
        step("A", MU, (MV,))
        for zz in (4, 8, 12):
            step("A", zz, (MU, MV))
        for zz in (4, 8, 12):
            step("C", zz, (MV,))
            step("C", zz + MU, (MV,))
        for zz in (4, 8, 12):
            step("A", zz + MU, (MV,))
        return steps

    def ag_plane(p, zm):
        for m in (4 * zm + MV, 4 * zm + MU + MV):
            got(p, "A", m)
            got(p, "C", m)

    def run(steps):
        for s in steps:
            s()

    vec_peers = (
        (partner, (ids[MU], c), (ids[MV], c), (ids[4], c), (ids[8], c)),
        (partner, (ids[4], c), (ids[8], c), (ids[MU], c), (ids[MV], c)),
    )

    def vec_send(k, s):
        send(("v", k, s), r.VS.at[pl.ds(48 * k + 8 * s, 8), :], r.VR.at[pl.ds(40 * k + 8 * s, 8), :], vec_peers[k][s])

    def vec_step(k, s):
        src, got_row = pl.ds(48 * k + 8 * s, 8), pl.ds(40 * k + 8 * s, 8)
        wait_recv(("v", k, s), r.VR.at[got_row, :])
        r.VS[pl.ds(48 * k + 8 * s + 8, 8), :] = r.VS[src, :] + r.VR[got_row, :]
        if s < 4:
            vec_send(k, s + 1)

    def rs1_send(p, zm):
        rows = 2 * ROWS[p]
        s = pl.ds(zm * rows, rows)
        send(("r1", p, zm), r.S1[p].at[s, :], r.R1[p].at[s, :], (ids[MV], c))

    def rs_sum1(p, zm):
        rows, a = ROWS[p], APART[p]
        b = rows - a
        g, r1 = r.G[p], r.R1[p]
        s = pl.ds(zm * 2 * rows, 2 * rows)
        wait_recv(("r1", p, zm), r1.at[s, :])
        for du in (1, 0):
            o = (2 * zm + du) * rows
            top = g[o : o + a, :] + r1[o : o + a, :].astype(F32)
            low = g[o + a : o + rows, :] + r1[o + a : o + rows, :].astype(F32)
            if du == 1:
                q = pl.ds(zm * a, a)
                r.S2A[p][q, :] = top.astype(BF)
                send(("r2a", p, zm), r.S2A[p].at[q, :], r.R2A[p].at[q, :], (ids[MU], c))
            else:
                g[o : o + a, :] = top
            if zm:
                q = pl.ds(((zm - 1) * 2 + du) * b, b)
                r.S2C[p][q, :] = low.astype(BF)
            else:
                g[o + a : o + rows, :] = low
        if zm:
            q = pl.ds((zm - 1) * 2 * b, 2 * b)
            send(("r2c", p, zm), r.S2C[p].at[q, :], r.R2C[p].at[q, :], (ids[4 * zm], c))

    def rs_sum2a(p, zm):
        rows, a = ROWS[p], APART[p]
        g, r2 = r.G[p], r.R2A[p]
        q = pl.ds(zm * a, a)
        wait_recv(("r2a", p, zm), r2.at[q, :])
        o = 2 * zm * rows
        val = g[o : o + a, :] + r2[q, :].astype(F32)
        if zm:
            k = pl.ds((zm - 1) * a, a)
            r.S3A[p][k, :] = val.astype(BF)
            send(("r3a", p, zm), r.S3A[p].at[k, :], r.R3A[p].at[k, :], (ids[4 * zm], c))
        else:
            g[o : o + a, :] = val

    def rs_sum2c(p):
        rows, a = ROWS[p], APART[p]
        b = rows - a
        g, r2 = r.G[p], r.R2C[p]
        for zm in (1, 2, 3):
            wait_recv(("r2c", p, zm), r2.at[pl.ds((zm - 1) * 2 * b, 2 * b), :])
        for du in (1, 0):
            o = du * rows + a
            val = g[o : o + b, :]
            for zm in (1, 2, 3):
                k = ((zm - 1) * 2 + du) * b
                val = val + r2[k : k + b, :].astype(F32)
            if du == 1:
                r.S3C[p][...] = val.astype(BF)
                send(("r3c", p), r.S3C[p], r.R3C[p], (ids[MU], c))
            else:
                g[o : o + b, :] = val

    def rs_final(p):
        rows, a = ROWS[p], APART[p]
        g = r.G[p]
        r3a, r3c = r.R3A[p], r.R3C[p]
        for zm in (1, 2, 3):
            wait_recv(("r3a", p, zm), r3a.at[pl.ds((zm - 1) * a, a), :])
        val = g[0:a, :]
        for zm in (1, 2, 3):
            val = val + r3a[(zm - 1) * a : zm * a, :].astype(F32)
        g[0:a, :] = val
        wait_recv(("r3c", p), r3c)
        g[a:rows, :] = g[a:rows, :] + r3c[...].astype(F32)

    def block_row(zm, du, dv):
        uu = 1 - u if du else u
        vv = 1 - v if dv else v
        return ub * uu + vb * vv

    def stage(p, zm, src, base):
        rows, cols = ROWS[p], COLS[p]
        for du in (1, 0):
            k = (2 * zm + du) * rows
            far = pl.ds(pl.multiple_of(base + block_row(zm, du, 1) * rows, 8), rows)
            near = pl.ds(pl.multiple_of(base + block_row(zm, du, 0) * rows, 8), rows)
            r.S1[p][k : k + rows, :] = src[far, 0:cols].astype(BF)
            r.G[p][k : k + rows, :] = src[near, 0:cols]
        rs1_send(p, zm)

    r.WQ[pl.ds(pl.multiple_of(me * 48, 16), 48), 0:384] = r.wq[...].astype(BF)
    r.WQ[pl.ds(pl.multiple_of(me * 48, 16), 48), 384:768] = r.wk[...].astype(BF)
    r.WQ[pl.ds(pl.multiple_of(me * 48, 16), 48), 768:1152] = r.wv[...].astype(BF)
    ag_own("Q")
    send("tok", r.tok, r.X.at[own_rows, :], partner)
    local = pltpu.make_async_copy(r.tok, r.X.at[own_rows, :], r.ls.at[0])
    local.start()
    flat = 2 * me + c
    r.VS[0:8, :] = jnp.zeros((8, 768), F32)
    for k, n in enumerate(("ga", "ba", "gf", "bf")):
        r.VS[k : k + 1, 0:24] = getattr(r, n)[...].reshape(1, 24).astype(BF).astype(F32)
    r.VS[0:8, :] = pltpu.roll(r.VS[0:8, :], 24 * flat, 1)
    vec_send(0, 0)
    wo = r.wo[...]
    r.WOP[c, pl.ds(pl.multiple_of(me * 48, 16), 48), :] = jnp.concatenate(
        [wo[:, 0:384], wo[:, 384:768]], axis=0
    ).astype(BF)
    ag_own("O")
    r.WU[pl.ds(pl.multiple_of(me * 96, 16), 96), :] = r.wu[...].astype(BF)
    r.WD[pl.ds(pl.multiple_of(me * 96, 16), 96), :] = r.wd[...].astype(BF)

    col_pos = lax.broadcasted_iota(jnp.int32, (512, 128), 0)
    row_pos = lax.broadcasted_iota(jnp.int32, (8, 512), 1)
    col_lab = jnp.zeros((512, 128), jnp.int32)
    row_lab = jnp.zeros((8, 512), jnp.int32)
    for j in range(8):
        lo = r.off[0, j]
        hi = lo + r.len[0, j]
        col_lab = jnp.where((col_pos >= lo) & (col_pos < hi), j + 1, col_lab)
        row_lab = jnp.where((row_pos >= lo) & (row_pos < hi), j + 1, row_lab)
    r.LIVE[...] = jnp.where(col_lab > 0, 1.0, 0.0).astype(F32)
    row_lab = jnp.where(row_lab > 0, row_lab, -1)
    for t in range(4):
        q = slice(128 * t, 128 * t + 128)
        lab = jnp.concatenate([col_lab[q]] * 4, axis=1)
        same = lab == jnp.broadcast_to(row_lab[0:1], (128, 512))
        r.BIAS[q, :] = jnp.where(same, 0.0, -1e30).astype(F32)

    q_steps, o_steps, u_steps, d_steps = (ag_steps(p) for p in PIECES)
    run(q_steps[:5])
    ag_own("U")
    vec_step(0, 0)
    run(o_steps[:5])
    run(q_steps[5:])
    ag_own("D")
    wait_recv("tok", r.X.at[own_rows, :])
    local.wait()
    for zm in range(4):
        ag_plane("Q", zm)

    for k, n in enumerate(("Q3", "K3", "V3")):
        full = mm(r.X[...], r.WQ[:, 384 * k : 384 * k + 384])
        full = full.astype(BF)
        if k == 0:
            full = full * BF(0.125)
        for i in range(3):
            getattr(r, n)[i] = full[:, 128 * i : 128 * i + 128]
    vec_step(0, 1)
    run(u_steps[:2])

    for i in range(3):
        r.ATT[i] = jnp.zeros((512, 128), BF)
    fw_hooks = [
        u_steps[2:5],
        [functools.partial(vec_step, 0, 2)] + o_steps[5:8],
        o_steps[8:12],
        o_steps[12:] + d_steps[:1] + [functools.partial(vec_step, 0, 3)],
        d_steps[1:3],
        d_steps[3:5],
    ]
    lane = lax.broadcasted_iota(jnp.int32, (1, 128), 1)

    def half(val, a):
        keep = (lane >= 64 * a) & (lane < 64 * a + 64)
        return jnp.where(keep, val, jnp.zeros_like(val))

    def at_index(h, hooks):
        for k, steps in enumerate(hooks):

            def go(steps=steps):
                run(steps)

            pl.when(h == k)(go)

    def fwd_head(h, carry):
        at_index(h, fw_hooks)
        i = lax.div(h, 2)
        a = lax.rem(h, 2)
        vals = half(r.V3[i], a)
        keys = half(r.K3[i], a)
        for t in range(4):
            q = slice(128 * t, 128 * t + 128)
            s = mm(r.Q3[i, q, :], keys, 1, 1) + r.BIAS[q, :]
            live = r.LIVE[q, 0:1]
            top = jnp.where(live > 0, jnp.max(s, axis=1, keepdims=True), 0.0)
            w = jnp.exp(s - top)
            total = jnp.sum(w, axis=1, keepdims=True) + (1.0 - live)
            prob = w * (1.0 / total)
            r.P32[h, q, :] = prob
            o = mm(prob.astype(BF), vals)
            r.ATT[i, q, :] = r.ATT[i, q, :] + o.astype(BF)
        return carry

    lax.fori_loop(0, 6, fwd_head, 0)

    send("att", r.ATT.at[:, oth_rows, :], r.ATTR, partner)
    for zm in range(4):
        ag_plane("O", zm)
    send("wop", r.WOP.at[c], r.WOP.at[c], partner)
    run(u_steps[5:8])
    vec_step(0, 4)
    wait_recv("wop", r.WOP.at[1 - c])

    def build_out(i, carry):
        for k in range(2):
            blk = r.WOP[k, pl.ds(pl.multiple_of(48 * i, 16), 48), :].astype(F32)
            rows = jnp.concatenate([blk[0:24], blk[24:48]], axis=1)
            r.T[pl.ds(pl.multiple_of(48 * i + 24 * k, 8), 24), 0:768] = rows
        return carry

    lax.fori_loop(0, 16, build_out, 0)
    r.WO[...] = r.T[:, 0:768].astype(BF)
    wait_recv("att", r.ATTR)
    own_heads = pl.ds(pl.multiple_of(384 * c, 128), 384)
    oth_heads = pl.ds(pl.multiple_of(384 * (1 - c), 128), 384)

    def joined(ref, rows):
        return jnp.concatenate([ref[i, rows, :] for i in range(3)], axis=1)

    all256 = pl.ds(0, 256)
    branch = mm(joined(r.ATT, own_rows), r.WO[own_heads, :])
    branch = branch + mm(joined(r.ATTR, all256), r.WO[oth_heads, :])
    r.GS[...] = branch
    run(u_steps[8:11])

    def norm(val):
        mean = jnp.mean(val, axis=1, keepdims=True)
        cen = val - mean
        inv = lax.rsqrt(jnp.mean(cen * cen, axis=1, keepdims=True) + EPS)
        return cen * inv, inv

    def ln1(t, carry):
        q = pl.ds(pl.multiple_of(64 * t, 64), 64)
        unit, inv = norm(r.tok[q, :].astype(F32) + r.GS[q, :])
        r.U1[q, :] = unit
        r.INV1[q, :] = jnp.broadcast_to(inv, (64, 128))
        one = unit * r.VS[40:41, :] + r.VS[41:42, :]
        r.N1[q, :] = one
        r.FIN[pl.ds(pl.multiple_of(base256 + 64 * t, 64), 64), :] = one.astype(BF)
        return carry

    lax.fori_loop(0, 4, ln1, 0)
    send("fin", r.FIN.at[own_rows, :], r.FIN.at[own_rows, :], partner)
    run(u_steps[11:])
    wait_recv("fin", r.FIN.at[oth_rows, :])

    def plane_rows(zm):
        return pl.ds(pl.multiple_of(384 * zs[zm], 128), 384)

    def ffn_up(zm):
        for t in range(2):
            q = slice(256 * t, 256 * t + 256)
            pre = mm(r.FIN[q, :], r.WU[plane_rows(zm), :], 1, 1)
            r.GEL[zm, q, :] = pre

        def act(t, carry):
            q = pl.ds(pl.multiple_of(64 * t, 64), 64)
            pre = r.GEL[zm, q, :]
            cdf = 0.5 * (1.0 + lax.erf(pre * (2.0**-0.5)))
            pdf = jnp.exp(-0.5 * pre * pre) * (1.0 / math.sqrt(2.0 * math.pi))
            r.HID[zm, q, :] = (pre * cdf).astype(BF)
            r.GEL[zm, q, :] = cdf + pre * pdf
            return carry

        lax.fori_loop(0, 8, act, 0)

    d_groups = (d_steps[5:8], d_steps[8:11], d_steps[11:], [])
    for zm in range(4):
        ag_plane("U", zm)
        ffn_up(zm)
        run(d_groups[zm])
    for zm in range(4):
        ag_plane("D", zm)
        for rows in (oth_rows, own_rows):
            part = mm(r.HID[zm, rows, :], r.WD[plane_rows(zm), :])
            if zm:
                part = part + r.SEC[rows, :]
            r.SEC[rows, :] = part
            if zm == 3 and rows is oth_rows:
                send("sec", r.SEC.at[oth_rows, :], r.SECR, partner)
    wait_recv("sec", r.SECR)

    def ln2(t, sums):
        dg, db = sums
        q = pl.ds(pl.multiple_of(64 * t, 64), 64)
        qq = pl.ds(pl.multiple_of(base256 + 64 * t, 64), 64)
        unit, inv = norm(r.N1[q, :] + (r.SEC[qq, :] + r.SECR[q, :]))
        gain = r.VS[42:43, :]
        r.out[q, :] = (unit * gain + r.VS[43:44, :]).astype(BF)
        e = r.og[q, :].astype(F32)
        dg = dg + jnp.sum(e * unit, axis=0, keepdims=True)
        db = db + jnp.sum(e, axis=0, keepdims=True)
        eg = e * gain
        inner = jnp.mean(eg * unit, axis=1, keepdims=True)
        gs = inv * (eg - jnp.mean(eg, axis=1, keepdims=True) - unit * inner)
        r.GS[q, :] = gs
        r.GFB[qq, :] = gs.astype(BF)
        return dg, db

    zero = jnp.zeros((1, 768), F32)
    dg2, db2 = lax.fori_loop(0, 4, ln2, (zero, zero))
    send("gfb", r.GFB.at[own_rows, :], r.GFB.at[own_rows, :], partner)
    wait_recv("gfb", r.GFB.at[oth_rows, :])
    wait_sent("sec")

    for n_done, zm in enumerate((3, 2, 1, 0)):
        r.T[0:384, 0:768] = mm(r.HID[zm], r.GFB[...], 0, 0)
        stage("D", zm, r.T, 0)
        for t in range(2):
            q = slice(256 * t, 256 * t + 256)
            gh = mm(r.GFB[q, :], r.WD[plane_rows(zm), :], 1, 1)
            r.HID[zm, q, :] = (gh * r.GEL[zm, q, :]).astype(BF)
        r.T[384:768, 0:768] = mm(r.HID[zm], r.FIN[...], 0, 0)
        stage("U", zm, r.T, 384)
        for rows in (oth_rows, own_rows):
            part = mm(r.HID[zm, rows, :], r.WU[plane_rows(zm), :])
            if n_done:
                part = part + r.SEC[rows, :]
            r.SEC[rows, :] = part
            if n_done == 3 and rows is oth_rows:
                send("gn", r.SEC.at[oth_rows, :], r.SECR, partner)
        if n_done == 2:
            rs_sum1("D", 3)
    rs_sum1("U", 3)
    wait_recv("gn", r.SECR)

    def ln1_back(t, sums):
        dg, db = sums
        q = pl.ds(pl.multiple_of(64 * t, 64), 64)
        qq = pl.ds(pl.multiple_of(base256 + 64 * t, 64), 64)
        e = r.GS[q, :] + (r.SEC[qq, :] + r.SECR[q, :])
        unit = r.U1[q, :]
        inv = r.INV1[q, 0:1]
        dg = dg + jnp.sum(e * unit, axis=0, keepdims=True)
        db = db + jnp.sum(e, axis=0, keepdims=True)
        eg = e * r.VS[40:41, :]
        inner = jnp.mean(eg * unit, axis=1, keepdims=True)
        first = inv * (eg - jnp.mean(eg, axis=1, keepdims=True) - unit * inner)
        r.GS[q, :] = first
        r.GB[q, :] = first.astype(BF)
        return dg, db

    dg1, db1 = lax.fori_loop(0, 4, ln1_back, (zero, zero))
    r.VS[48:56, :] = jnp.zeros((8, 768), F32)
    for k, val in enumerate((dg1, db1, dg2, db2)):
        r.VS[48 + k : 49 + k, :] = val
    vec_send(1, 0)

    gview = mm(r.GB[...], r.WO[oth_heads, :], 1, 1).astype(BF)
    for i in range(3):
        r.GAS[i] = gview[:, 128 * i : 128 * i + 128]
    send("gas", r.GAS, r.GA.at[:, own_rows, :], partner)
    gview = mm(r.GB[...], r.WO[own_heads, :], 1, 1).astype(BF)
    for i in range(3):
        r.GA[i, own_rows, :] = gview[:, 128 * i : 128 * i + 128]
    vec_step(1, 0)
    rs_sum1("D", 2)
    r.T[own_heads, 0:768] = mm(joined(r.ATT, own_rows), r.GB[...], 0, 0)
    r.T[oth_heads, 0:768] = mm(joined(r.ATTR, all256), r.GB[...], 0, 0)

    def pair_out(i, carry):
        q = pl.ds(pl.multiple_of(48 * i, 16), 48)
        blk = r.T[pl.ds(pl.multiple_of(48 * i + other24, 8), 24), 0:768]
        r.S0[q, :] = jnp.concatenate([blk[:, 0:384], blk[:, 384:768]], axis=0).astype(BF)
        return carry

    lax.fori_loop(0, 16, pair_out, 0)
    send("s0", r.S0, r.R0, partner)
    rs_sum2a("D", 3)
    wait_recv("s0", r.R0)

    def out_block(m):
        i = ids[m]
        blk = r.T[pl.ds(pl.multiple_of(48 * i + base24, 8), 24), 0:768]
        blk = jnp.concatenate([blk[:, 0:384], blk[:, 384:768]], axis=0)
        return blk + r.R0[pl.ds(pl.multiple_of(48 * i, 16), 48), :].astype(F32)

    for zm in (3, 2, 1, 0):
        for du in (1, 0):
            k = (2 * zm + du) * 48
            r.S1["O"][k : k + 48, :] = out_block(4 * zm + 2 * du + 1).astype(BF)
            r.G["O"][k : k + 48, :] = out_block(4 * zm + 2 * du)
        rs1_send("O", zm)

    wait_recv("gas", r.GA.at[:, oth_rows, :])
    for n in ("DQ", "DK", "DV"):
        for i in range(3):
            getattr(r, n)[i] = jnp.zeros((512, 128), BF)

    def s1(p, zm):
        return functools.partial(rs_sum1, p, zm)

    def s2a(p, zm):
        return functools.partial(rs_sum2a, p, zm)

    def s2c(p):
        return functools.partial(rs_sum2c, p)

    def vs(s):
        return functools.partial(vec_step, 1, s)

    bw_hooks = [
        [s2a("U", 3), vs(1)],
        [s1("U", 2)],
        [s2a("D", 2), vs(2)],
        [s1("D", 1)],
        [s2a("U", 2), vs(3)],
        [],
    ]

    def bwd_head(h, carry):
        at_index(h, bw_hooks)
        i = lax.div(h, 2)
        a = lax.rem(h, 2)
        go = half(r.GA[i], a)
        for t in range(4):
            q = slice(128 * t, 128 * t + 128)
            prob = r.P32[h, q, :]
            dp = mm(go[q], r.V3[i], 1, 1)
            delta = jnp.sum(prob * dp, axis=1, keepdims=True)
            r.DSB[q, :] = (prob * (dp - delta)).astype(BF)
            r.PB[q, :] = prob.astype(BF)
        r.DV[i] = r.DV[i] + mm(r.PB[...], go, 0, 0).astype(BF)
        dq = mm(r.DSB[...], half(r.K3[i], a)) * 0.125
        r.DQ[i] = r.DQ[i] + dq.astype(BF)
        dk = mm(r.DSB[...], half(r.Q3[i], a), 0, 0)
        r.DK[i] = r.DK[i] + dk.astype(BF)
        return carry

    lax.fori_loop(0, 6, bwd_head, 0)

    all512 = pl.ds(0, 512)
    for k, n in enumerate(("DQ", "DK", "DV")):
        r.T[:, 384 * k : 384 * k + 384] = mm(r.X[...], joined(getattr(r, n), all512), 0, 0)
    for zm in (3, 2, 1, 0):
        stage("Q", zm, r.T, 192 * zs[zm])
    run([s1("U", 1), s2a("D", 1)])

    for rows in (oth_rows, own_rows):
        acc = mm(joined(r.DQ, rows), r.WQ[:, 0:384], 1, 1)
        acc = acc + mm(joined(r.DK, rows), r.WQ[:, 384:768], 1, 1)
        acc = acc + mm(joined(r.DV, rows), r.WQ[:, 768:1152], 1, 1)
        if rows is oth_rows:
            r.IGS[...] = acc.astype(BF)
            send("ig", r.IGS, r.IGR, partner)
            run([s1("D", 0), s2a("U", 1)])
        else:
            r.GS[...] = r.GS[...] + acc
    wait_recv("ig", r.IGR)
    r.ig[...] = (r.GS[...] + r.IGR[...].astype(F32)).astype(BF)

    run([s1("U", 0), s2a("D", 0), s2c("D"), s2a("U", 0), s2c("U")])
    run([s1("O", 3), s1("O", 2), s2a("O", 3), s1("O", 1), s2a("O", 2), s1("O", 0)])
    run([s2a("O", 1), s2a("O", 0), vs(4), s2c("O")])
    run([s1("Q", 3), s1("Q", 2), s2a("Q", 3), s1("Q", 1), s2a("Q", 2), s1("Q", 0)])
    run([s2a("Q", 1), s2a("Q", 0), s2c("Q")])
    for p in ("D", "U", "O"):
        rs_final(p)
    r.dwd[...] = r.G["D"][0:96, :]
    r.dwu[...] = r.G["U"][0:96, :]
    go = r.G["O"][0:48, :]
    r.dwo[...] = jnp.concatenate([go[0:24], go[24:48]], axis=1)
    back = pltpu.roll(r.VS[88:96, :], lax.rem(768 - 24 * flat, 768), 1)
    for k, n in enumerate(("dga", "dba", "dgf", "dbf")):
        getattr(r, n)[...] = back[k, 0:24]
    rs_final("Q")
    r.dwq[...] = r.G["Q"][0:48, 0:384]
    r.dwk[...] = r.G["Q"][0:48, 384:768]
    r.dwv[...] = r.G["Q"][0:48, 768:1152]

    for entry in sends:
        if entry[3] not in waited:
            wait_send(entry)


def hand_over(*refs):
    half = len(refs) // 2
    for src, dst in zip(refs[:half], refs[half:]):
        dst[...] = src[...]


def layer_small(*args):
    shapes = (
        ((256, 768), BF),
        ((256, 768), BF),
        ((48, 384), F32),
        ((48, 384), F32),
        ((48, 384), F32),
        ((24, 768), F32),
        ((24,), F32),
        ((24,), F32),
        ((96, 768), F32),
        ((96, 768), F32),
        ((24,), F32),
        ((24,), F32),
    )
    vmem = pl.BlockSpec(memory_space=pltpu.VMEM)
    smem = pl.BlockSpec(memory_space=pltpu.SMEM)
    out_shape = tuple(jax.ShapeDtypeStruct(s, d) for s, d in shapes)
    up = IN_NAMES.index("wu")
    args = args[:up] + (args[up].T,) + args[up + 1 :]
    outs = pl.pallas_call(
        layer_kernel,
        out_shape=out_shape,
        in_specs=[smem if n in ("len", "off") else vmem for n in IN_NAMES],
        out_specs=tuple(vmem for _ in shapes),
        scratch_shapes=[s for _, s in scratch_list()],
        compiler_params=pltpu.CompilerParams(
            collective_id=0, has_side_effects=True, vmem_limit_bytes=67043328
        ),
    )(*args)
    outs = pl.pallas_call(
        hand_over,
        out_shape=out_shape,
        in_specs=[vmem for _ in shapes],
        out_specs=tuple(vmem for _ in shapes),
    )(*outs)
    up = OUT_NAMES.index("dwu")
    return outs[:up] + (outs[up].T,) + outs[up + 1 :]


def labels_of(lengths, offsets):
    position = jnp.arange(BIN, dtype=jnp.int32)[:, None]
    starts = offsets[None, :]
    inside = (position >= starts) & (position < starts + lengths[None, :])
    slot_order = jnp.arange(1, lengths.shape[0] + 1, dtype=jnp.int32)[None, :]
    return jnp.sum(jnp.where(inside, slot_order, 0), axis=1)


def layer_norm(operand, gain_vec, bias_vec):
    row_mean = jnp.mean(operand, axis=-1, keepdims=True)
    centered = operand - row_mean
    inverse = lax.rsqrt(jnp.mean(centered * centered, axis=-1, keepdims=True) + EPS)
    normed = centered * inverse
    return (normed * gain_vec + bias_vec, normed, inverse)


def norm_back(grad_rows, normed, inverse, gain_vec):
    scaled = grad_rows * gain_vec
    inner = jnp.mean(scaled * normed, axis=-1, keepdims=True)
    return inverse * (scaled - jnp.mean(scaled, axis=-1, keepdims=True) - normed * inner)


def gelu_exact(operand):
    return jax.nn.gelu(operand, approximate=False)


def contract_rows(left, right):
    return lax.dot_general(
        left, right, (((0,), (0,)), ((), ())), preferred_element_type=F32
    )


def contract_cols(left, right):
    return lax.dot_general(
        left, right, (((1,), (1,)), ((), ())), preferred_element_type=F32
    )


def score_block(queries, key_rows, labels_bin, factor):
    scores = (
        jnp.einsum("qhd,khd->hqk", queries, key_rows, preferred_element_type=F32) * factor
    )
    allowed = ((labels_bin[:, None] == labels_bin[None, :]) & (labels_bin[:, None] > 0))[None]
    live_rows = (labels_bin > 0)[None, :, None]
    return (scores, allowed, live_rows)


def masked_exp(scores, allowed, row_top):
    return jnp.where(allowed, jnp.exp(jnp.where(allowed, scores - row_top, 0.0)), 0.0)


def attend_bin(pieces, factor):
    queries, key_rows, value_rows, labels_bin = pieces
    scores, allowed, live_rows = score_block(queries, key_rows, labels_bin, factor)
    row_top = jnp.max(jnp.where(allowed, scores, -1e30), axis=2, keepdims=True)
    row_top = jnp.where(live_rows, row_top, 0.0)
    weights = masked_exp(scores, allowed, row_top)
    denominator = jnp.sum(weights, axis=2, keepdims=True) + jnp.where(live_rows, 0.0, 1.0)
    probability = (weights / denominator).astype(jnp.bfloat16)
    mixed_rows = jnp.einsum(
        "hqk,khd->qhd", probability, value_rows, preferred_element_type=F32
    )
    return (mixed_rows.astype(jnp.bfloat16), row_top, denominator)


def attend_back(pieces, factor):
    queries, key_rows, value_rows, labels_bin, row_top, denominator, grad_mixed = pieces
    scores, allowed, live_rows = score_block(queries, key_rows, labels_bin, factor)
    probability = masked_exp(scores, allowed, row_top) / denominator
    grad_values = jnp.einsum(
        "hqk,qhd->khd",
        probability.astype(jnp.bfloat16),
        grad_mixed,
        preferred_element_type=F32,
    )
    grad_probs = jnp.einsum(
        "qhd,khd->hqk", grad_mixed, value_rows, preferred_element_type=F32
    )
    row_delta = jnp.sum(probability * grad_probs, axis=2, keepdims=True)
    grad_scores = (probability * (grad_probs - row_delta)).astype(jnp.bfloat16)
    grad_queries = (
        jnp.einsum("hqk,khd->qhd", grad_scores, key_rows, preferred_element_type=F32)
        * factor
    )
    grad_keys = (
        jnp.einsum("hqk,qhd->khd", grad_scores, queries, preferred_element_type=F32)
        * factor
    )
    return (
        grad_queries.astype(jnp.bfloat16),
        grad_keys.astype(jnp.bfloat16),
        grad_values.astype(jnp.bfloat16),
    )


def per_device(
    tokens,
    w_query,
    w_key,
    w_value,
    w_out,
    gain_attn,
    bias_attn,
    w_up,
    w_down,
    gain_ffn,
    bias_ffn,
    seq_lengths,
    seq_offsets,
    out_grad,
):
    low_type = jnp.bfloat16
    bin_count = seq_lengths.shape[0]
    group_rows = bin_count * BIN
    head_width = w_query.shape[1]
    local_heads = head_width // HD
    factor = 1.0 / math.sqrt(HD)
    labels = jax.vmap(labels_of)(seq_lengths, seq_offsets)
    full_query, full_key, full_value = (
        lax.all_gather(w_query.astype(low_type), DP, axis=0, tiled=True),
        lax.all_gather(w_key.astype(low_type), DP, axis=0, tiled=True),
        lax.all_gather(w_value.astype(low_type), DP, axis=0, tiled=True),
    )
    projection = jnp.concatenate([full_query, full_key, full_value], axis=1)
    whole_rows = lax.all_gather(tokens, HEAD, axis=0, tiled=True)
    projected = jnp.dot(whole_rows, projection, preferred_element_type=F32).astype(low_type)
    shape_bins = (bin_count, BIN, local_heads, HD)
    queries = projected[:, :head_width].reshape(shape_bins)
    key_rows = projected[:, head_width : 2 * head_width].reshape(shape_bins)
    value_rows = projected[:, 2 * head_width :].reshape(shape_bins)
    mixed_bins, row_tops, denominators = lax.map(
        lambda pieces: attend_bin(pieces, factor), (queries, key_rows, value_rows, labels)
    )
    attended = mixed_bins.reshape(group_rows, head_width)
    out_full, up_part, down_part, gain_one, bias_one, gain_two, bias_two = (
        lax.all_gather(w_out.astype(low_type), BOTH, axis=0, tiled=True),
        lax.all_gather(w_up.astype(low_type), BOTH, axis=1, tiled=True),
        lax.all_gather(w_down.astype(low_type), BOTH, axis=0, tiled=True),
        lax.all_gather(gain_attn.astype(low_type), BOTH, axis=0, tiled=True),
        lax.all_gather(bias_attn.astype(low_type), BOTH, axis=0, tiled=True),
        lax.all_gather(gain_ffn.astype(low_type), BOTH, axis=0, tiled=True),
        lax.all_gather(bias_ffn.astype(low_type), BOTH, axis=0, tiled=True),
    )
    gain_first = gain_one.astype(F32)
    gain_second = gain_two.astype(F32)
    token_view = lax.all_to_all(attended, HEAD, split_axis=0, concat_axis=1, tiled=True)
    first_sum = tokens.astype(F32) + jnp.dot(
        token_view, out_full, preferred_element_type=F32
    )
    normed_one, unit_one, inverse_one = layer_norm(
        first_sum, gain_first, bias_one.astype(F32)
    )
    ffn_input = normed_one.astype(low_type)
    pre_act = jnp.dot(ffn_input, up_part, preferred_element_type=F32)
    activated, gelu_pull = jax.vjp(gelu_exact, pre_act)
    hidden = activated.astype(low_type)
    second_sum = normed_one + jnp.dot(hidden, down_part, preferred_element_type=F32)
    result, unit_two, inverse_two = layer_norm(
        second_sum, gain_second, bias_two.astype(F32)
    )
    output = result.astype(low_type)
    grad_result = out_grad.astype(F32)
    grad_gain_two = jnp.sum(grad_result * unit_two, axis=0)
    grad_bias_two = jnp.sum(grad_result, axis=0)
    grad_second = norm_back(grad_result, unit_two, inverse_two, gain_second)
    grad_ffn = grad_second.astype(low_type)
    grad_down_part = contract_rows(hidden, grad_ffn)
    grad_pre = gelu_pull(contract_cols(grad_ffn, down_part))[0].astype(low_type)
    grad_up_part = contract_rows(ffn_input, grad_pre)
    grad_normed = grad_second + contract_cols(grad_pre, up_part)
    grad_gain_one = jnp.sum(grad_normed * unit_one, axis=0)
    grad_bias_one = jnp.sum(grad_normed, axis=0)
    grad_first = norm_back(grad_normed, unit_one, inverse_one, gain_first)
    grad_branch = grad_first.astype(low_type)
    grad_out_full = contract_rows(token_view, grad_branch)
    part_out, part_up, part_down, part_gain_one, part_bias_one, part_gain_two, part_bias_two = (
        lax.psum_scatter(grad_out_full, BOTH, scatter_dimension=0, tiled=True),
        lax.psum_scatter(grad_up_part, BOTH, scatter_dimension=1, tiled=True),
        lax.psum_scatter(grad_down_part, BOTH, scatter_dimension=0, tiled=True),
        lax.psum_scatter(grad_gain_one, BOTH, scatter_dimension=0, tiled=True),
        lax.psum_scatter(grad_bias_one, BOTH, scatter_dimension=0, tiled=True),
        lax.psum_scatter(grad_gain_two, BOTH, scatter_dimension=0, tiled=True),
        lax.psum_scatter(grad_bias_two, BOTH, scatter_dimension=0, tiled=True),
    )
    grad_token_view = contract_cols(grad_branch, out_full).astype(low_type)
    grad_attended = lax.all_to_all(grad_token_view, HEAD, split_axis=1, concat_axis=0, tiled=True)
    grad_bins = grad_attended.reshape(shape_bins)
    grad_queries, grad_keys, grad_values = lax.map(
        lambda pieces: attend_back(pieces, factor),
        (queries, key_rows, value_rows, labels, row_tops, denominators, grad_bins),
    )
    grad_projected = jnp.concatenate(
        [
            grad_queries.reshape(group_rows, head_width),
            grad_keys.reshape(group_rows, head_width),
            grad_values.reshape(group_rows, head_width),
        ],
        axis=1,
    )
    grad_projection = contract_rows(whole_rows, grad_projected)
    part_query, part_key, part_value = (
        lax.psum_scatter(grad_projection[:, :head_width], DP, scatter_dimension=0, tiled=True),
        lax.psum_scatter(
            grad_projection[:, head_width : 2 * head_width], DP, scatter_dimension=0, tiled=True
        ),
        lax.psum_scatter(
            grad_projection[:, 2 * head_width :], DP, scatter_dimension=0, tiled=True
        ),
    )
    input_grad = (
        grad_first
        + lax.psum_scatter(
            contract_cols(grad_projected, projection).astype(jnp.bfloat16),
            HEAD,
            scatter_dimension=0,
            tiled=True,
        ).astype(F32)
    ).astype(low_type)
    return (
        output,
        input_grad,
        part_query,
        part_key,
        part_value,
        part_out,
        part_gain_one,
        part_bias_one,
        part_up,
        part_down,
        part_gain_two,
        part_bias_two,
    )


def solution(mesh):
    small = mesh.shape[DP] == 16 and mesh.shape[HEAD] == 2
    return jax.shard_map(
        layer_small if small else per_device,
        mesh=mesh,
        in_specs=(
            P(BOTH, None),
            P(DP, HEAD),
            P(DP, HEAD),
            P(DP, HEAD),
            P(BOTH, None),
            P(BOTH),
            P(BOTH),
            P(None, BOTH),
            P(BOTH, None),
            P(BOTH),
            P(BOTH),
            P(DP, None),
            P(DP, None),
            P(BOTH, None),
        ),
        out_specs=(
            P(BOTH, None),
            P(BOTH, None),
            P(DP, HEAD),
            P(DP, HEAD),
            P(DP, HEAD),
            P(BOTH, None),
            P(BOTH),
            P(BOTH),
            P(None, BOTH),
            P(BOTH, None),
            P(BOTH),
            P(BOTH),
        ),
        check_vma=False,
    )
```

```python
import functools
import math
import types

import jax
import jax.numpy as jnp
from jax import lax
from jax.experimental import pallas as pl
from jax.experimental.pallas import tpu as pltpu
from jax.sharding import PartitionSpec as P

HD = 64
BIN = 512
EPS = 1e-12
F32 = jnp.float32
BF = jnp.bfloat16
MESH = pl.DeviceIdType.MESH

MU, MV = 2, 1
ROWS = {"Q": 48, "O": 48, "U": 96, "D": 96}
COLS = {"Q": 1152, "O": 384, "U": 768, "D": 768}
APART = {"Q": 32, "O": 32, "U": 64, "D": 64}
PIECES = ("Q", "O", "U", "D")
PER_PIECE = ("G", "S1", "R1", "S2A", "R2A", "S3A", "R3A", "S2C", "R2C", "S3C", "R3C")
DP, HEAD = "dp", "head"
BOTH = (DP, HEAD)
COPIES = 202


def mm(a, b, ca=1, cb=0):
    return lax.dot_general(a, b, (((ca,), (cb,)), ((), ())), preferred_element_type=F32)


def scratch_list():
    items = []
    for name, shape, dtype in MOVED_IN + MOVED_OUT:
        items.append((name, pltpu.VMEM(shape, dtype)))

    def add(name, shape, dtype):
        items.append((name, pltpu.VMEM(shape, dtype)))

    add("X", (512, 768), BF)
    add("WQ", (768, 1152), BF)
    add("WOP", (2, 768, 384), BF)
    add("WO", (768, 768), BF)
    add("WU", (1536, 768), BF)
    add("WD", (1536, 768), BF)
    for n in ("Q3", "K3", "V3", "ATT", "GA", "DQ", "DK", "DV"):
        add(n, (3, 512, 128), BF)
    add("ATTR", (3, 256, 128), BF)
    add("GAS", (3, 256, 128), BF)
    add("BIAS", (512, 512), F32)
    add("LIVE", (512, 128), F32)
    add("P32", (6, 512, 512), F32)
    add("PB", (512, 512), BF)
    add("DSB", (512, 512), BF)
    add("U1", (256, 768), F32)
    add("N1", (256, 768), F32)
    add("INV1", (256, 128), F32)
    add("FIN", (512, 768), BF)
    add("HID", (4, 512, 384), BF)
    add("GEL", (4, 512, 384), F32)
    add("SEC", (512, 768), F32)
    add("SECR", (256, 768), F32)
    add("GS", (256, 768), F32)
    add("GFB", (512, 768), BF)
    add("GB", (256, 768), BF)
    add("IGS", (256, 768), BF)
    add("IGR", (256, 768), BF)
    add("T", (768, 1152), F32)
    add("S0", (768, 384), BF)
    add("R0", (768, 384), BF)
    for p in PIECES:
        r, c, a = ROWS[p], COLS[p], APART[p]
        b = r - a
        sizes = (8 * r, 8 * r, 8 * r, 4 * a, 4 * a, 3 * a, 3 * a, 6 * b, 6 * b, b, b)
        for key, size in zip(PER_PIECE, sizes):
            add(key + p, (size, c), F32 if key == "G" else BF)
    add("VS", (96, 768), F32)
    add("VR", (80, 768), F32)
    items.append(("ss", pltpu.SemaphoreType.DMA((COPIES,))))
    items.append(("rs", pltpu.SemaphoreType.DMA((COPIES,))))
    items.append(("ls", pltpu.SemaphoreType.DMA((1 + len(MOVED_IN) + len(MOVED_OUT),))))
    return items


IN_NAMES = ("tok", "wq", "wk", "wv", "wo", "ga", "ba", "wu", "wd", "gf", "bf", "len", "off", "og")
MOVED_IN = (
    ("wq", (48, 384), F32),
    ("wk", (48, 384), F32),
    ("wv", (48, 384), F32),
    ("ga", (24,), F32),
    ("ba", (24,), F32),
    ("gf", (24,), F32),
    ("bf", (24,), F32),
    ("tok", (256, 768), BF),
    ("wo", (24, 768), F32),
    ("wu", (96, 768), F32),
    ("wd", (96, 768), F32),
    ("og", (256, 768), BF),
)
MOVED_OUT = (
    ("out", (256, 768), BF),
    ("ig", (256, 768), BF),
    ("dwq", (48, 384), F32),
    ("dwk", (48, 384), F32),
    ("dwv", (48, 384), F32),
    ("dwo", (24, 768), F32),
    ("dga", (24,), F32),
    ("dba", (24,), F32),
    ("dwu", (96, 768), F32),
    ("dwd", (96, 768), F32),
    ("dgf", (24,), F32),
    ("dbf", (24,), F32),
)
OUT_NAMES = ("out", "ig", "dwq", "dwk", "dwv", "dwo", "dga", "dba", "dwu", "dwd", "dgf", "dbf")


def layer_kernel(*refs):
    ins = tuple(n if n in ("len", "off") else "far_" + n for n in IN_NAMES)
    outs = tuple("far_" + n for n in OUT_NAMES)
    names = ins + outs + tuple(n for n, _ in scratch_list())
    named = dict(zip(names, refs))
    r = types.SimpleNamespace(**named)
    for key in PER_PIECE:
        setattr(r, key, {p: named[key + p] for p in PIECES})
    me = lax.axis_index(DP)
    c = lax.axis_index(HEAD)
    x = lax.rem(me, 2)
    y = lax.rem(lax.div(me, 2), 2)
    z = lax.div(me, 4)
    u = x + c * (y - x)
    v = y + c * (x - y)
    ub = 1 + c
    vb = 2 - c
    zs = (z, z + 1 - 2 * lax.rem(z, 2), lax.rem(z + 2, 4), 3 - z)

    def chip(m):
        zm, du, dv = m // 4, (m // 2) % 2, m % 2
        uu = 1 - u if du else u
        vv = 1 - v if dv else v
        return 4 * zs[zm] + ub * uu + vb * vv

    ids = [chip(m) for m in range(16)]
    partner = (me, 1 - c)
    base256, base24, other24 = 256 * c, 24 * c, 24 * (1 - c)
    own_rows = pl.ds(pl.multiple_of(256 * c, 256), 256)
    oth_rows = pl.ds(pl.multiple_of(256 * (1 - c), 256), 256)

    in_copies, out_copies = {}, []
    for k, (n, _, _) in enumerate(MOVED_IN):
        in_copies[n] = pltpu.make_async_copy(named["far_" + n], named[n], r.ls.at[1 + k])
        in_copies[n].start()

    def arrived(*keys):
        for n in keys:
            in_copies[n].wait()

    def put(*keys):
        for n in keys:
            k = 1 + len(MOVED_IN) + OUT_NAMES.index(n)
            cp = pltpu.make_async_copy(named[n], named["far_" + n], r.ls.at[k])
            cp.start()
            out_copies.append(cp)

    peers = [partner] + [(ids[m], c) for m in (MU, MV, 4, 8, 12)]
    barrier = pltpu.get_barrier_semaphore()
    for dev in peers:
        pl.semaphore_signal(barrier, inc=1, device_id=dev, device_id_type=MESH)
    pl.semaphore_wait(barrier, len(peers))

    sends = []
    recv_ids = {}

    def recv_sem(key):
        if key not in recv_ids:
            recv_ids[key] = len(recv_ids)
        return r.rs.at[recv_ids[key]]

    def send(key, src, dst, dev):
        cp = pltpu.make_async_remote_copy(
            src_ref=src,
            dst_ref=dst,
            send_sem=r.ss.at[len(sends)],
            recv_sem=recv_sem(key),
            device_id=dev,
            device_id_type=MESH,
        )
        cp.start()
        sends.append((src, dst, len(sends), key, dev))

    def wait_send(entry):
        src, dst, k, key, dev = entry
        pltpu.make_async_remote_copy(
            src_ref=src,
            dst_ref=dst,
            send_sem=r.ss.at[k],
            recv_sem=recv_sem(key),
            device_id=dev,
            device_id_type=MESH,
        ).wait_send()

    waited = set()

    def wait_sent(key):
        for entry in sends:
            if entry[3] == key:
                wait_send(entry)
                waited.add(key)

    def wait_recv(key, ref):
        pltpu.make_async_remote_copy(
            src_ref=ref,
            dst_ref=ref,
            send_sem=r.ss.at[0],
            recv_sem=recv_sem(key),
            device_id=partner,
            device_id_type=MESH,
        ).wait_recv()

    def wbuf(p):
        return {"Q": r.WQ, "O": r.WOP.at[c], "U": r.WU, "D": r.WD}[p]

    starts = {}
    for n_rows in (48, 96):
        for m in range(16):
            first = pl.multiple_of(ids[m] * n_rows, 16)
            third = pl.multiple_of(ids[m] * n_rows + 2 * n_rows // 3, 16)
            starts[n_rows, m] = (first, third)

    def wslice(p, part, m):
        a, rows = APART[p], ROWS[p]
        first, third = starts[rows, m]
        if part == "A":
            return wbuf(p).at[pl.ds(first, a), :]
        return wbuf(p).at[pl.ds(third, rows - a), :]

    def forward(p, part, m, f):
        ref = wslice(p, part, m)
        send(("ag", p, part, m ^ f), ref, ref, (ids[f], c))

    def got(p, part, m):
        wait_recv(("ag", p, part, m), wslice(p, part, m))

    def ag_own(p):
        forward(p, "C", 0, MU)
        for f in (4, 8, 12):
            forward(p, "A", 0, f)
        forward(p, "A", 0, MU)
        forward(p, "A", 0, MV)
        for f in (4, 8, 12):
            forward(p, "C", 0, f)
        forward(p, "C", 0, MV)

    def ag_steps(p):
        steps = []

        def step(part, m, flips):
            def run():
                got(p, part, m)
                for f in flips:
                    forward(p, part, m, f)

            steps.append(run)

        step("C", MU, (4, 8, 12, MV))
        step("A", MU, (MV,))
        for zz in (4, 8, 12):
            step("A", zz, (MU, MV))
        for zz in (4, 8, 12):
            step("C", zz, (MV,))
            step("C", zz + MU, (MV,))
        for zz in (4, 8, 12):
            step("A", zz + MU, (MV,))
        return steps

    def ag_plane(p, zm):
        for m in (4 * zm + MV, 4 * zm + MU + MV):
            got(p, "A", m)
            got(p, "C", m)

    def run(steps):
        for s in steps:
            s()

    vec_peers = (
        ((ids[4], c), (ids[8], c), (ids[MV], c), (ids[MU], c), partner),
        ((ids[MV], c), (ids[MU], c), (ids[4], c), (ids[8], c), partner),
    )

    def vec_send(k, s):
        send(("v", k, s), r.VS.at[pl.ds(48 * k + 8 * s, 8), :], r.VR.at[pl.ds(40 * k + 8 * s, 8), :], vec_peers[k][s])

    def vec_step(k, s):
        src, got_row = pl.ds(48 * k + 8 * s, 8), pl.ds(40 * k + 8 * s, 8)
        wait_recv(("v", k, s), r.VR.at[got_row, :])
        r.VS[pl.ds(48 * k + 8 * s + 8, 8), :] = r.VS[src, :] + r.VR[got_row, :]
        if s < 4:
            vec_send(k, s + 1)

    def rs1_send(p, zm):
        rows = 2 * ROWS[p]
        s = pl.ds(zm * rows, rows)
        send(("r1", p, zm), r.S1[p].at[s, :], r.R1[p].at[s, :], (ids[MV], c))

    def rs_sum1(p, zm):
        rows, a = ROWS[p], APART[p]
        b = rows - a
        g, r1 = r.G[p], r.R1[p]
        s = pl.ds(zm * 2 * rows, 2 * rows)
        wait_recv(("r1", p, zm), r1.at[s, :])
        for du in (1, 0):
            o = (2 * zm + du) * rows
            top = g[o : o + a, :] + r1[o : o + a, :].astype(F32)
            low = g[o + a : o + rows, :] + r1[o + a : o + rows, :].astype(F32)
            if du == 1:
                q = pl.ds(zm * a, a)
                r.S2A[p][q, :] = top.astype(BF)
                send(("r2a", p, zm), r.S2A[p].at[q, :], r.R2A[p].at[q, :], (ids[MU], c))
            else:
                g[o : o + a, :] = top
            if zm:
                q = pl.ds(((zm - 1) * 2 + du) * b, b)
                r.S2C[p][q, :] = low.astype(BF)
            else:
                g[o + a : o + rows, :] = low
        if zm:
            q = pl.ds((zm - 1) * 2 * b, 2 * b)
            send(("r2c", p, zm), r.S2C[p].at[q, :], r.R2C[p].at[q, :], (ids[4 * zm], c))

    def rs_sum2a(p, zm):
        rows, a = ROWS[p], APART[p]
        g, r2 = r.G[p], r.R2A[p]
        q = pl.ds(zm * a, a)
        wait_recv(("r2a", p, zm), r2.at[q, :])
        o = 2 * zm * rows
        val = g[o : o + a, :] + r2[q, :].astype(F32)
        if zm:
            k = pl.ds((zm - 1) * a, a)
            r.S3A[p][k, :] = val.astype(BF)
            send(("r3a", p, zm), r.S3A[p].at[k, :], r.R3A[p].at[k, :], (ids[4 * zm], c))
        else:
            g[o : o + a, :] = val

    def rs_sum2c(p):
        rows, a = ROWS[p], APART[p]
        b = rows - a
        g, r2 = r.G[p], r.R2C[p]
        for zm in (1, 2, 3):
            wait_recv(("r2c", p, zm), r2.at[pl.ds((zm - 1) * 2 * b, 2 * b), :])
        for du in (1, 0):
            o = du * rows + a
            val = g[o : o + b, :]
            for zm in (1, 2, 3):
                k = ((zm - 1) * 2 + du) * b
                val = val + r2[k : k + b, :].astype(F32)
            if du == 1:
                r.S3C[p][...] = val.astype(BF)
                send(("r3c", p), r.S3C[p], r.R3C[p], (ids[MU], c))
            else:
                g[o : o + b, :] = val

    def rs_final(p):
        rows, a = ROWS[p], APART[p]
        g = r.G[p]
        r3a, r3c = r.R3A[p], r.R3C[p]
        for zm in (1, 2, 3):
            wait_recv(("r3a", p, zm), r3a.at[pl.ds((zm - 1) * a, a), :])
        val = g[0:a, :]
        for zm in (1, 2, 3):
            val = val + r3a[(zm - 1) * a : zm * a, :].astype(F32)
        g[0:a, :] = val
        wait_recv(("r3c", p), r3c)
        g[a:rows, :] = g[a:rows, :] + r3c[...].astype(F32)

    def block_row(zm, du, dv):
        uu = 1 - u if du else u
        vv = 1 - v if dv else v
        return ub * uu + vb * vv

    def stage(p, zm, src, base):
        rows, cols = ROWS[p], COLS[p]
        for du in (1, 0):
            k = (2 * zm + du) * rows
            far = pl.ds(pl.multiple_of(base + block_row(zm, du, 1) * rows, 8), rows)
            near = pl.ds(pl.multiple_of(base + block_row(zm, du, 0) * rows, 8), rows)
            r.S1[p][k : k + rows, :] = src[far, 0:cols].astype(BF)
            r.G[p][k : k + rows, :] = src[near, 0:cols]

    flat = 2 * me + c
    arrived("ga", "ba", "gf", "bf")
    r.VS[0:8, :] = jnp.zeros((8, 768), F32)
    for k, n in enumerate(("ga", "ba", "gf", "bf")):
        r.VS[k : k + 1, 0:24] = getattr(r, n)[...].reshape(1, 24).astype(BF).astype(F32)
    r.VS[0:8, :] = pltpu.roll(r.VS[0:8, :], 24 * flat, 1)
    vec_send(0, 0)
    arrived("wq", "wk", "wv")
    r.WQ[pl.ds(pl.multiple_of(me * 48, 16), 48), 0:384] = r.wq[...].astype(BF)
    r.WQ[pl.ds(pl.multiple_of(me * 48, 16), 48), 384:768] = r.wk[...].astype(BF)
    r.WQ[pl.ds(pl.multiple_of(me * 48, 16), 48), 768:1152] = r.wv[...].astype(BF)
    ag_own("Q")
    arrived("tok")
    send("tok", r.tok, r.X.at[own_rows, :], partner)
    local = pltpu.make_async_copy(r.tok, r.X.at[own_rows, :], r.ls.at[0])
    local.start()
    arrived("wo")
    wo = r.wo[...]
    r.WOP[c, pl.ds(pl.multiple_of(me * 48, 16), 48), :] = jnp.concatenate(
        [wo[:, 0:384], wo[:, 384:768]], axis=0
    ).astype(BF)
    arrived("wu", "wd", "og")
    r.WU[pl.ds(pl.multiple_of(me * 96, 16), 96), :] = r.wu[...].astype(BF)
    r.WD[pl.ds(pl.multiple_of(me * 96, 16), 96), :] = r.wd[...].astype(BF)

    q_steps, o_steps, u_steps, d_steps = (ag_steps(p) for p in PIECES)
    run(q_steps[:5])
    ag_own("O")
    vec_step(0, 0)
    run(o_steps[:1])

    col_pos = lax.broadcasted_iota(jnp.int32, (512, 128), 0)
    row_pos = lax.broadcasted_iota(jnp.int32, (8, 512), 1)
    col_lab = jnp.zeros((512, 128), jnp.int32)
    row_lab = jnp.zeros((8, 512), jnp.int32)
    for j in range(8):
        lo = r.off[0, j]
        hi = lo + r.len[0, j]
        col_lab = jnp.where((col_pos >= lo) & (col_pos < hi), j + 1, col_lab)
        row_lab = jnp.where((row_pos >= lo) & (row_pos < hi), j + 1, row_lab)
    r.LIVE[...] = jnp.where(col_lab > 0, 1.0, 0.0).astype(F32)
    row_lab = jnp.where(row_lab > 0, row_lab, -1)
    for t in range(4):
        q = slice(128 * t, 128 * t + 128)
        lab = jnp.concatenate([col_lab[q]] * 4, axis=1)
        same = lab == jnp.broadcast_to(row_lab[0:1], (128, 512))
        r.BIAS[q, :] = jnp.where(same, 0.0, -1e30).astype(F32)

    run(q_steps[5:])
    vec_step(0, 1)
    run(o_steps[1:5])
    ag_own("U")
    wait_recv("tok", r.X.at[own_rows, :])
    local.wait()
    for zm in range(4):
        ag_plane("Q", zm)

    for k, n in enumerate(("Q3", "K3", "V3")):
        full = mm(r.X[...], r.WQ[:, 384 * k : 384 * k + 384])
        full = full.astype(BF)
        if k == 0:
            full = full * BF(0.125)
        for i in range(3):
            getattr(r, n)[i] = full[:, 128 * i : 128 * i + 128]
    vec_step(0, 2)
    run(u_steps[:1])

    for i in range(3):
        r.ATT[i] = jnp.zeros((512, 128), BF)
    fw_hooks = [
        o_steps[5:8],
        o_steps[8:],
        [functools.partial(vec_step, 0, 3)] + u_steps[1:3],
        u_steps[3:5],
        u_steps[5:8],
        u_steps[8:10],
    ]
    lane = lax.broadcasted_iota(jnp.int32, (1, 128), 1)

    def half(val, a):
        keep = (lane >= 64 * a) & (lane < 64 * a + 64)
        return jnp.where(keep, val, jnp.zeros_like(val))

    def at_index(h, hooks):
        for k, steps in enumerate(hooks):

            def go(steps=steps):
                run(steps)

            pl.when(h == k)(go)

    def fwd_head(h, carry):
        at_index(h, fw_hooks)
        i = lax.div(h, 2)
        a = lax.rem(h, 2)
        vals = half(r.V3[i], a)
        keys = half(r.K3[i], a)
        for t in range(4):
            q = slice(128 * t, 128 * t + 128)
            s = mm(r.Q3[i, q, :], keys, 1, 1) + r.BIAS[q, :]
            live = r.LIVE[q, 0:1]
            top = jnp.where(live > 0, jnp.max(s, axis=1, keepdims=True), 0.0)
            w = jnp.exp(s - top)
            total = jnp.sum(w, axis=1, keepdims=True) + (1.0 - live)
            prob = w * (1.0 / total)
            r.P32[h, q, :] = prob
            o = mm(prob.astype(BF), vals)
            r.ATT[i, q, :] = r.ATT[i, q, :] + o.astype(BF)
        return carry

    lax.fori_loop(0, 6, fwd_head, 0)

    send("att", r.ATT.at[:, oth_rows, :], r.ATTR, partner)
    ag_own("D")
    for zm in range(4):
        ag_plane("O", zm)
    send("wop", r.WOP.at[c], r.WOP.at[c], partner)
    run(d_steps[:1] + u_steps[10:12])
    vec_step(0, 4)
    wait_recv("wop", r.WOP.at[1 - c])

    def build_out(i, carry):
        for k in range(2):
            blk = r.WOP[k, pl.ds(pl.multiple_of(48 * i, 16), 48), :].astype(F32)
            rows = jnp.concatenate([blk[0:24], blk[24:48]], axis=1)
            r.T[pl.ds(pl.multiple_of(48 * i + 24 * k, 8), 24), 0:768] = rows
        return carry

    lax.fori_loop(0, 16, build_out, 0)
    r.WO[...] = r.T[:, 0:768].astype(BF)
    wait_recv("att", r.ATTR)
    own_heads = pl.ds(pl.multiple_of(384 * c, 128), 384)
    oth_heads = pl.ds(pl.multiple_of(384 * (1 - c), 128), 384)

    def joined(ref, rows):
        return jnp.concatenate([ref[i, rows, :] for i in range(3)], axis=1)

    all256 = pl.ds(0, 256)
    branch = mm(joined(r.ATT, own_rows), r.WO[own_heads, :])
    branch = branch + mm(joined(r.ATTR, all256), r.WO[oth_heads, :])
    r.GS[...] = branch
    run(u_steps[12:] + d_steps[1:2])

    def norm(val):
        mean = jnp.mean(val, axis=1, keepdims=True)
        cen = val - mean
        inv = lax.rsqrt(jnp.mean(cen * cen, axis=1, keepdims=True) + EPS)
        return cen * inv, inv

    def ln1(t, carry):
        q = pl.ds(pl.multiple_of(64 * t, 64), 64)
        unit, inv = norm(r.tok[q, :].astype(F32) + r.GS[q, :])
        r.U1[q, :] = unit
        r.INV1[q, :] = jnp.broadcast_to(inv, (64, 128))
        one = unit * r.VS[40:41, :] + r.VS[41:42, :]
        r.N1[q, :] = one
        r.FIN[pl.ds(pl.multiple_of(base256 + 64 * t, 64), 64), :] = one.astype(BF)
        return carry

    lax.fori_loop(0, 4, ln1, 0)
    send("fin", r.FIN.at[own_rows, :], r.FIN.at[own_rows, :], partner)
    run(d_steps[2:5])
    wait_recv("fin", r.FIN.at[oth_rows, :])

    def plane_rows(zm):
        return pl.ds(pl.multiple_of(384 * zs[zm], 128), 384)

    def ffn_up(zm):
        for t in range(2):
            q = slice(256 * t, 256 * t + 256)
            pre = mm(r.FIN[q, :], r.WU[plane_rows(zm), :], 1, 1)
            r.GEL[zm, q, :] = pre

        def act(t, carry):
            q = pl.ds(pl.multiple_of(64 * t, 64), 64)
            pre = r.GEL[zm, q, :]
            cdf = 0.5 * (1.0 + lax.erf(pre * (2.0**-0.5)))
            pdf = jnp.exp(-0.5 * pre * pre) * (1.0 / math.sqrt(2.0 * math.pi))
            r.HID[zm, q, :] = (pre * cdf).astype(BF)
            r.GEL[zm, q, :] = cdf + pre * pdf
            return carry

        lax.fori_loop(0, 8, act, 0)

    d_groups = ([], d_steps[5:8], d_steps[8:11], d_steps[11:])
    for zm in range(4):
        ag_plane("U", zm)
        run(d_groups[zm])
        ffn_up(zm)
    for zm in range(4):
        ag_plane("D", zm)
        for rows in (oth_rows, own_rows):
            part = mm(r.HID[zm, rows, :], r.WD[plane_rows(zm), :])
            if zm:
                part = part + r.SEC[rows, :]
            r.SEC[rows, :] = part
            if zm == 3 and rows is oth_rows:
                for h in range(2):
                    part_rows = pl.ds(pl.multiple_of(256 * (1 - c) + 128 * h, 128), 128)
                    send(("sec", h), r.SEC.at[part_rows, :], r.SECR.at[pl.ds(128 * h, 128), :], partner)

    def ln2(t, sums):
        dg, db = sums
        q = pl.ds(pl.multiple_of(64 * t, 64), 64)
        qq = pl.ds(pl.multiple_of(base256 + 64 * t, 64), 64)
        unit, inv = norm(r.N1[q, :] + (r.SEC[qq, :] + r.SECR[q, :]))
        gain = r.VS[42:43, :]
        r.out[q, :] = (unit * gain + r.VS[43:44, :]).astype(BF)
        e = r.og[q, :].astype(F32)
        dg = dg + jnp.sum(e * unit, axis=0, keepdims=True)
        db = db + jnp.sum(e, axis=0, keepdims=True)
        eg = e * gain
        inner = jnp.mean(eg * unit, axis=1, keepdims=True)
        gs = inv * (eg - jnp.mean(eg, axis=1, keepdims=True) - unit * inner)
        r.GS[q, :] = gs
        r.GFB[qq, :] = gs.astype(BF)
        return dg, db

    zero = jnp.zeros((1, 768), F32)
    dg2, db2 = zero, zero
    for h in range(2):
        wait_recv(("sec", h), r.SECR.at[pl.ds(128 * h, 128), :])
        dg2, db2 = lax.fori_loop(2 * h, 2 * h + 2, ln2, (dg2, db2))
        part_rows = r.GFB.at[pl.ds(pl.multiple_of(base256 + 128 * h, 128), 128), :]
        send(("gfb", h), part_rows, part_rows, partner)
    put("out")
    r.T[0:384, 0:768] = mm(r.HID[3, own_rows, :], r.GFB[own_rows, :], 0, 0)
    for h in range(2):
        wait_recv(("gfb", h), r.GFB.at[pl.ds(pl.multiple_of(256 * (1 - c) + 128 * h, 128), 128), :])
    for h in range(2):
        wait_sent(("sec", h))

    for n_done, zm in enumerate((3, 2, 1, 0)):
        if zm == 3:
            r.T[0:384, 0:768] = r.T[0:384, 0:768] + mm(r.HID[3, oth_rows, :], r.GFB[oth_rows, :], 0, 0)
        else:
            r.T[0:384, 0:768] = mm(r.HID[zm], r.GFB[...], 0, 0)
        stage("D", zm, r.T, 0)
        if zm:
            rs1_send("D", zm)
        for t in range(2):
            q = slice(256 * t, 256 * t + 256)
            gh = mm(r.GFB[q, :], r.WD[plane_rows(zm), :], 1, 1)
            r.HID[zm, q, :] = (gh * r.GEL[zm, q, :]).astype(BF)
        r.T[384:768, 0:768] = mm(r.HID[zm], r.FIN[...], 0, 0)
        stage("U", zm, r.T, 384)
        if zm > 1:
            rs1_send("U", zm)
        for rows in (oth_rows, own_rows):
            part = mm(r.HID[zm, rows, :], r.WU[plane_rows(zm), :])
            if n_done:
                part = part + r.SEC[rows, :]
            r.SEC[rows, :] = part
            if n_done == 3 and rows is oth_rows:
                send("gn", r.SEC.at[oth_rows, :], r.SECR, partner)
        if n_done == 2:
            rs_sum1("D", 3)
    rs_sum1("U", 3)
    wait_recv("gn", r.SECR)

    def ln1_back(t, sums):
        dg, db = sums
        q = pl.ds(pl.multiple_of(64 * t, 64), 64)
        qq = pl.ds(pl.multiple_of(base256 + 64 * t, 64), 64)
        e = r.GS[q, :] + (r.SEC[qq, :] + r.SECR[q, :])
        unit = r.U1[q, :]
        inv = r.INV1[q, 0:1]
        dg = dg + jnp.sum(e * unit, axis=0, keepdims=True)
        db = db + jnp.sum(e, axis=0, keepdims=True)
        eg = e * r.VS[40:41, :]
        inner = jnp.mean(eg * unit, axis=1, keepdims=True)
        first = inv * (eg - jnp.mean(eg, axis=1, keepdims=True) - unit * inner)
        r.GS[q, :] = first
        r.GB[q, :] = first.astype(BF)
        return dg, db

    dg1, db1 = lax.fori_loop(0, 4, ln1_back, (zero, zero))
    r.VS[48:56, :] = jnp.zeros((8, 768), F32)
    for k, val in enumerate((dg1, db1, dg2, db2)):
        r.VS[48 + k : 49 + k, :] = val
    vec_send(1, 0)

    gview = mm(r.GB[...], r.WO[oth_heads, :], 1, 1).astype(BF)
    for i in range(3):
        r.GAS[i] = gview[:, 128 * i : 128 * i + 128]
    send("gas", r.GAS, r.GA.at[:, own_rows, :], partner)
    gview = mm(r.GB[...], r.WO[own_heads, :], 1, 1).astype(BF)
    for i in range(3):
        r.GA[i, own_rows, :] = gview[:, 128 * i : 128 * i + 128]
    rs_sum2a("D", 3)
    r.T[own_heads, 0:768] = mm(joined(r.ATT, own_rows), r.GB[...], 0, 0)
    r.T[oth_heads, 0:768] = mm(joined(r.ATTR, all256), r.GB[...], 0, 0)

    def pair_out(i, carry):
        q = pl.ds(pl.multiple_of(48 * i, 16), 48)
        blk = r.T[pl.ds(pl.multiple_of(48 * i + other24, 8), 24), 0:768]
        r.S0[q, :] = jnp.concatenate([blk[:, 0:384], blk[:, 384:768]], axis=0).astype(BF)
        return carry

    lax.fori_loop(0, 16, pair_out, 0)
    send("s0", r.S0, r.R0, partner)
    rs_sum1("D", 2)
    rs_sum2a("U", 3)
    wait_recv("s0", r.R0)

    def out_block(m):
        i = ids[m]
        blk = r.T[pl.ds(pl.multiple_of(48 * i + base24, 8), 24), 0:768]
        blk = jnp.concatenate([blk[:, 0:384], blk[:, 384:768]], axis=0)
        return blk + r.R0[pl.ds(pl.multiple_of(48 * i, 16), 48), :].astype(F32)

    for zm in (3, 2, 1, 0):
        for du in (1, 0):
            k = (2 * zm + du) * 48
            r.S1["O"][k : k + 48, :] = out_block(4 * zm + 2 * du + 1).astype(BF)
            r.G["O"][k : k + 48, :] = out_block(4 * zm + 2 * du)
        if zm > 1:
            rs1_send("O", zm)
    rs1_send("U", 1)

    wait_recv("gas", r.GA.at[:, oth_rows, :])
    for n in ("DQ", "DK", "DV"):
        for i in range(3):
            getattr(r, n)[i] = jnp.zeros((512, 128), BF)

    def s1(p, zm):
        return functools.partial(rs_sum1, p, zm)

    def s2a(p, zm):
        return functools.partial(rs_sum2a, p, zm)

    def s2c(p):
        return functools.partial(rs_sum2c, p)

    def vs(s):
        return functools.partial(vec_step, 1, s)

    bw_hooks = [
        [],
        [s1("U", 2)],
        [s2a("D", 2)],
        [],
        [s1("D", 1)],
        [s2a("U", 2), vs(0)],
    ]

    def bwd_head(h, carry):
        at_index(h, bw_hooks)
        i = lax.div(h, 2)
        a = lax.rem(h, 2)
        go = half(r.GA[i], a)
        for t in range(4):
            q = slice(128 * t, 128 * t + 128)
            prob = r.P32[h, q, :]
            dp = mm(go[q], r.V3[i], 1, 1)
            delta = jnp.sum(prob * dp, axis=1, keepdims=True)
            r.DSB[q, :] = (prob * (dp - delta)).astype(BF)
            r.PB[q, :] = prob.astype(BF)
        r.DV[i] = r.DV[i] + mm(r.PB[...], go, 0, 0).astype(BF)
        dq = mm(r.DSB[...], half(r.K3[i], a)) * 0.125
        r.DQ[i] = r.DQ[i] + dq.astype(BF)
        dk = mm(r.DSB[...], half(r.Q3[i], a), 0, 0)
        r.DK[i] = r.DK[i] + dk.astype(BF)
        return carry

    lax.fori_loop(0, 6, bwd_head, 0)

    all512 = pl.ds(0, 512)
    for k, n in enumerate(("DQ", "DK", "DV")):
        r.T[:, 384 * k : 384 * k + 384] = mm(r.X[...], joined(getattr(r, n), all512), 0, 0)
    for zm in (3, 2, 1, 0):
        stage("Q", zm, r.T, 192 * zs[zm])
        if zm:
            rs1_send("Q", zm)
    for p, zm in (("O", 1), ("Q", 0), ("D", 0), ("U", 0), ("O", 0)):
        rs1_send(p, zm)
    run([s2a("D", 1), s1("O", 3), vs(1), s1("O", 2)])

    for rows in (oth_rows, own_rows):
        acc = mm(joined(r.DQ, rows), r.WQ[:, 0:384], 1, 1)
        acc = acc + mm(joined(r.DK, rows), r.WQ[:, 384:768], 1, 1)
        acc = acc + mm(joined(r.DV, rows), r.WQ[:, 768:1152], 1, 1)
        if rows is oth_rows:
            r.IGS[...] = acc.astype(BF)
            send("ig", r.IGS, r.IGR, partner)
            run([s2a("O", 3), s2a("O", 2), s1("U", 1), vs(2)])
        else:
            r.GS[...] = r.GS[...] + acc
    wait_recv("ig", r.IGR)
    r.ig[...] = (r.GS[...] + r.IGR[...].astype(F32)).astype(BF)
    put("ig")

    run([s1("Q", 3), s2a("U", 1), s1("Q", 2), s2a("Q", 3), s1("Q", 1), s2a("Q", 2), vs(3)])
    run([s1("O", 1), s2a("Q", 1), s1("Q", 0), s2c("Q"), s2a("O", 1)])
    run([s1("D", 0), s2c("D"), s2a("Q", 0), s1("U", 0), s2c("U"), s2a("D", 0)])
    run([s1("O", 0), s2c("O"), s2a("U", 0), s2a("O", 0), vs(4)])
    rs_final("Q")
    r.dwq[...] = r.G["Q"][0:48, 0:384]
    r.dwk[...] = r.G["Q"][0:48, 384:768]
    r.dwv[...] = r.G["Q"][0:48, 768:1152]
    rs_final("D")
    r.dwd[...] = r.G["D"][0:96, :]
    put("dwq", "dwk", "dwv", "dwd")
    rs_final("U")
    r.dwu[...] = r.G["U"][0:96, :]
    rs_final("O")
    go = r.G["O"][0:48, :]
    r.dwo[...] = jnp.concatenate([go[0:24], go[24:48]], axis=1)
    back = pltpu.roll(r.VS[88:96, :], lax.rem(768 - 24 * flat, 768), 1)
    for k, n in enumerate(("dga", "dba", "dgf", "dbf")):
        getattr(r, n)[...] = back[k, 0:24]
    put("dwu", "dwo", "dga", "dba", "dgf", "dbf")

    for entry in sends:
        if entry[3] not in waited:
            wait_send(entry)
    for cp in out_copies:
        cp.wait()


def hand_over(*refs):
    half = len(refs) // 2
    for src, dst in zip(refs[:half], refs[half:]):
        dst[...] = src[...]


def layer_small(*args):
    shapes = tuple((shape, dtype) for _, shape, dtype in MOVED_OUT)
    vmem = pl.BlockSpec(memory_space=pltpu.VMEM)
    smem = pl.BlockSpec(memory_space=pltpu.SMEM)
    anywhere = pl.BlockSpec(memory_space=pl.ANY)
    out_shape = tuple(jax.ShapeDtypeStruct(s, d) for s, d in shapes)
    up = IN_NAMES.index("wu")
    args = args[:up] + (args[up].T,) + args[up + 1 :]
    outs = pl.pallas_call(
        layer_kernel,
        out_shape=out_shape,
        in_specs=[smem if n in ("len", "off") else anywhere for n in IN_NAMES],
        out_specs=tuple(anywhere for _ in shapes),
        scratch_shapes=[s for _, s in scratch_list()],
        compiler_params=pltpu.CompilerParams(
            collective_id=0, has_side_effects=True, vmem_limit_bytes=67043328
        ),
    )(*args)
    outs = pl.pallas_call(
        hand_over,
        out_shape=out_shape,
        in_specs=[vmem for _ in shapes],
        out_specs=tuple(vmem for _ in shapes),
    )(*outs)
    up = OUT_NAMES.index("dwu")
    return outs[:up] + (outs[up].T,) + outs[up + 1 :]


def labels_of(lengths, offsets):
    position = jnp.arange(BIN, dtype=jnp.int32)[:, None]
    starts = offsets[None, :]
    inside = (position >= starts) & (position < starts + lengths[None, :])
    slot_order = jnp.arange(1, lengths.shape[0] + 1, dtype=jnp.int32)[None, :]
    return jnp.sum(jnp.where(inside, slot_order, 0), axis=1)


def layer_norm(operand, gain_vec, bias_vec):
    row_mean = jnp.mean(operand, axis=-1, keepdims=True)
    centered = operand - row_mean
    inverse = lax.rsqrt(jnp.mean(centered * centered, axis=-1, keepdims=True) + EPS)
    normed = centered * inverse
    return (normed * gain_vec + bias_vec, normed, inverse)


def norm_back(grad_rows, normed, inverse, gain_vec):
    scaled = grad_rows * gain_vec
    inner = jnp.mean(scaled * normed, axis=-1, keepdims=True)
    return inverse * (scaled - jnp.mean(scaled, axis=-1, keepdims=True) - normed * inner)


def gelu_exact(operand):
    return jax.nn.gelu(operand, approximate=False)


def contract_rows(left, right):
    return lax.dot_general(
        left, right, (((0,), (0,)), ((), ())), preferred_element_type=F32
    )


def contract_cols(left, right):
    return lax.dot_general(
        left, right, (((1,), (1,)), ((), ())), preferred_element_type=F32
    )


def score_block(queries, key_rows, labels_bin, factor):
    scores = (
        jnp.einsum("qhd,khd->hqk", queries, key_rows, preferred_element_type=F32) * factor
    )
    allowed = ((labels_bin[:, None] == labels_bin[None, :]) & (labels_bin[:, None] > 0))[None]
    live_rows = (labels_bin > 0)[None, :, None]
    return (scores, allowed, live_rows)


def masked_exp(scores, allowed, row_top):
    return jnp.where(allowed, jnp.exp(jnp.where(allowed, scores - row_top, 0.0)), 0.0)


def attend_bin(pieces, factor):
    queries, key_rows, value_rows, labels_bin = pieces
    scores, allowed, live_rows = score_block(queries, key_rows, labels_bin, factor)
    row_top = jnp.max(jnp.where(allowed, scores, -1e30), axis=2, keepdims=True)
    row_top = jnp.where(live_rows, row_top, 0.0)
    weights = masked_exp(scores, allowed, row_top)
    denominator = jnp.sum(weights, axis=2, keepdims=True) + jnp.where(live_rows, 0.0, 1.0)
    probability = (weights / denominator).astype(jnp.bfloat16)
    mixed_rows = jnp.einsum(
        "hqk,khd->qhd", probability, value_rows, preferred_element_type=F32
    )
    return (mixed_rows.astype(jnp.bfloat16), row_top, denominator)


def attend_back(pieces, factor):
    queries, key_rows, value_rows, labels_bin, row_top, denominator, grad_mixed = pieces
    scores, allowed, live_rows = score_block(queries, key_rows, labels_bin, factor)
    probability = masked_exp(scores, allowed, row_top) / denominator
    grad_values = jnp.einsum(
        "hqk,qhd->khd",
        probability.astype(jnp.bfloat16),
        grad_mixed,
        preferred_element_type=F32,
    )
    grad_probs = jnp.einsum(
        "qhd,khd->hqk", grad_mixed, value_rows, preferred_element_type=F32
    )
    row_delta = jnp.sum(probability * grad_probs, axis=2, keepdims=True)
    grad_scores = (probability * (grad_probs - row_delta)).astype(jnp.bfloat16)
    grad_queries = (
        jnp.einsum("hqk,khd->qhd", grad_scores, key_rows, preferred_element_type=F32)
        * factor
    )
    grad_keys = (
        jnp.einsum("hqk,qhd->khd", grad_scores, queries, preferred_element_type=F32)
        * factor
    )
    return (
        grad_queries.astype(jnp.bfloat16),
        grad_keys.astype(jnp.bfloat16),
        grad_values.astype(jnp.bfloat16),
    )


def per_device(
    tokens,
    w_query,
    w_key,
    w_value,
    w_out,
    gain_attn,
    bias_attn,
    w_up,
    w_down,
    gain_ffn,
    bias_ffn,
    seq_lengths,
    seq_offsets,
    out_grad,
):
    low_type = jnp.bfloat16
    bin_count = seq_lengths.shape[0]
    group_rows = bin_count * BIN
    head_width = w_query.shape[1]
    local_heads = head_width // HD
    factor = 1.0 / math.sqrt(HD)
    labels = jax.vmap(labels_of)(seq_lengths, seq_offsets)
    full_query, full_key, full_value = (
        lax.all_gather(w_query.astype(low_type), DP, axis=0, tiled=True),
        lax.all_gather(w_key.astype(low_type), DP, axis=0, tiled=True),
        lax.all_gather(w_value.astype(low_type), DP, axis=0, tiled=True),
    )
    projection = jnp.concatenate([full_query, full_key, full_value], axis=1)
    whole_rows = lax.all_gather(tokens, HEAD, axis=0, tiled=True)
    projected = jnp.dot(whole_rows, projection, preferred_element_type=F32).astype(low_type)
    shape_bins = (bin_count, BIN, local_heads, HD)
    queries = projected[:, :head_width].reshape(shape_bins)
    key_rows = projected[:, head_width : 2 * head_width].reshape(shape_bins)
    value_rows = projected[:, 2 * head_width :].reshape(shape_bins)
    mixed_bins, row_tops, denominators = lax.map(
        lambda pieces: attend_bin(pieces, factor), (queries, key_rows, value_rows, labels)
    )
    attended = mixed_bins.reshape(group_rows, head_width)
    out_full, up_part, down_part, gain_one, bias_one, gain_two, bias_two = (
        lax.all_gather(w_out.astype(low_type), BOTH, axis=0, tiled=True),
        lax.all_gather(w_up.astype(low_type), BOTH, axis=1, tiled=True),
        lax.all_gather(w_down.astype(low_type), BOTH, axis=0, tiled=True),
        lax.all_gather(gain_attn.astype(low_type), BOTH, axis=0, tiled=True),
        lax.all_gather(bias_attn.astype(low_type), BOTH, axis=0, tiled=True),
        lax.all_gather(gain_ffn.astype(low_type), BOTH, axis=0, tiled=True),
        lax.all_gather(bias_ffn.astype(low_type), BOTH, axis=0, tiled=True),
    )
    gain_first = gain_one.astype(F32)
    gain_second = gain_two.astype(F32)
    token_view = lax.all_to_all(attended, HEAD, split_axis=0, concat_axis=1, tiled=True)
    first_sum = tokens.astype(F32) + jnp.dot(
        token_view, out_full, preferred_element_type=F32
    )
    normed_one, unit_one, inverse_one = layer_norm(
        first_sum, gain_first, bias_one.astype(F32)
    )
    ffn_input = normed_one.astype(low_type)
    pre_act = jnp.dot(ffn_input, up_part, preferred_element_type=F32)
    activated, gelu_pull = jax.vjp(gelu_exact, pre_act)
    hidden = activated.astype(low_type)
    second_sum = normed_one + jnp.dot(hidden, down_part, preferred_element_type=F32)
    result, unit_two, inverse_two = layer_norm(
        second_sum, gain_second, bias_two.astype(F32)
    )
    output = result.astype(low_type)
    grad_result = out_grad.astype(F32)
    grad_gain_two = jnp.sum(grad_result * unit_two, axis=0)
    grad_bias_two = jnp.sum(grad_result, axis=0)
    grad_second = norm_back(grad_result, unit_two, inverse_two, gain_second)
    grad_ffn = grad_second.astype(low_type)
    grad_down_part = contract_rows(hidden, grad_ffn)
    grad_pre = gelu_pull(contract_cols(grad_ffn, down_part))[0].astype(low_type)
    grad_up_part = contract_rows(ffn_input, grad_pre)
    grad_normed = grad_second + contract_cols(grad_pre, up_part)
    grad_gain_one = jnp.sum(grad_normed * unit_one, axis=0)
    grad_bias_one = jnp.sum(grad_normed, axis=0)
    grad_first = norm_back(grad_normed, unit_one, inverse_one, gain_first)
    grad_branch = grad_first.astype(low_type)
    grad_out_full = contract_rows(token_view, grad_branch)
    part_out, part_up, part_down, part_gain_one, part_bias_one, part_gain_two, part_bias_two = (
        lax.psum_scatter(grad_out_full, BOTH, scatter_dimension=0, tiled=True),
        lax.psum_scatter(grad_up_part, BOTH, scatter_dimension=1, tiled=True),
        lax.psum_scatter(grad_down_part, BOTH, scatter_dimension=0, tiled=True),
        lax.psum_scatter(grad_gain_one, BOTH, scatter_dimension=0, tiled=True),
        lax.psum_scatter(grad_bias_one, BOTH, scatter_dimension=0, tiled=True),
        lax.psum_scatter(grad_gain_two, BOTH, scatter_dimension=0, tiled=True),
        lax.psum_scatter(grad_bias_two, BOTH, scatter_dimension=0, tiled=True),
    )
    grad_token_view = contract_cols(grad_branch, out_full).astype(low_type)
    grad_attended = lax.all_to_all(grad_token_view, HEAD, split_axis=1, concat_axis=0, tiled=True)
    grad_bins = grad_attended.reshape(shape_bins)
    grad_queries, grad_keys, grad_values = lax.map(
        lambda pieces: attend_back(pieces, factor),
        (queries, key_rows, value_rows, labels, row_tops, denominators, grad_bins),
    )
    grad_projected = jnp.concatenate(
        [
            grad_queries.reshape(group_rows, head_width),
            grad_keys.reshape(group_rows, head_width),
            grad_values.reshape(group_rows, head_width),
        ],
        axis=1,
    )
    grad_projection = contract_rows(whole_rows, grad_projected)
    part_query, part_key, part_value = (
        lax.psum_scatter(grad_projection[:, :head_width], DP, scatter_dimension=0, tiled=True),
        lax.psum_scatter(
            grad_projection[:, head_width : 2 * head_width], DP, scatter_dimension=0, tiled=True
        ),
        lax.psum_scatter(
            grad_projection[:, 2 * head_width :], DP, scatter_dimension=0, tiled=True
        ),
    )
    input_grad = (
        grad_first
        + lax.psum_scatter(
            contract_cols(grad_projected, projection).astype(jnp.bfloat16),
            HEAD,
            scatter_dimension=0,
            tiled=True,
        ).astype(F32)
    ).astype(low_type)
    return (
        output,
        input_grad,
        part_query,
        part_key,
        part_value,
        part_out,
        part_gain_one,
        part_bias_one,
        part_up,
        part_down,
        part_gain_two,
        part_bias_two,
    )


def solution(mesh):
    small = mesh.shape[DP] == 16 and mesh.shape[HEAD] == 2
    return jax.shard_map(
        layer_small if small else per_device,
        mesh=mesh,
        in_specs=(
            P(BOTH, None),
            P(DP, HEAD),
            P(DP, HEAD),
            P(DP, HEAD),
            P(BOTH, None),
            P(BOTH),
            P(BOTH),
            P(None, BOTH),
            P(BOTH, None),
            P(BOTH),
            P(BOTH),
            P(DP, None),
            P(DP, None),
            P(BOTH, None),
        ),
        out_specs=(
            P(BOTH, None),
            P(BOTH, None),
            P(DP, HEAD),
            P(DP, HEAD),
            P(DP, HEAD),
            P(BOTH, None),
            P(BOTH),
            P(BOTH),
            P(None, BOTH),
            P(BOTH, None),
            P(BOTH),
            P(BOTH),
        ),
        check_vma=False,
    )
```

```python
import functools
import math
import types

import jax
import jax.numpy as jnp
from jax import lax
from jax.experimental import pallas as pl
from jax.experimental.pallas import tpu as pltpu
from jax.sharding import PartitionSpec as P

HD = 64
BIN = 512
EPS = 1e-12
F32 = jnp.float32
BF = jnp.bfloat16
MESH = pl.DeviceIdType.MESH

MU, MV = 2, 1
ROWS = {"Q": 48, "O": 48, "U": 96, "D": 96}
COLS = {"Q": 1152, "O": 384, "U": 768, "D": 768}
APART = {"Q": 32, "O": 32, "U": 64, "D": 64}
PIECES = ("Q", "O", "U", "D")
PER_PIECE = ("G", "S1", "R1", "S2A", "R2A", "S3A", "R3A", "S2C", "R2C", "S3C", "R3C")
DP, HEAD = "dp", "head"
BOTH = (DP, HEAD)
COPIES = 204


def mm(a, b, ca=1, cb=0):
    return lax.dot_general(a, b, (((ca,), (cb,)), ((), ())), preferred_element_type=F32)


def scratch_list():
    items = []
    for name, shape, dtype in MOVED_IN + MOVED_OUT:
        items.append((name, pltpu.VMEM(shape, dtype)))

    def add(name, shape, dtype):
        items.append((name, pltpu.VMEM(shape, dtype)))

    add("X", (512, 768), BF)
    add("WQ", (768, 1152), BF)
    add("WOP", (2, 768, 384), BF)
    add("WO", (768, 768), BF)
    add("WU", (1536, 768), BF)
    add("WD", (1536, 768), BF)
    for n in ("Q3", "K3", "V3", "ATT", "GA", "DQ", "DK", "DV"):
        add(n, (3, 512, 128), BF)
    add("ATTR", (3, 256, 128), BF)
    add("GAS", (3, 256, 128), BF)
    add("BIAS", (512, 512), F32)
    add("LIVE", (512, 128), F32)
    add("P32", (6, 512, 512), F32)
    add("PB", (512, 512), BF)
    add("DSB", (512, 512), BF)
    add("U1", (256, 768), F32)
    add("N1", (256, 768), F32)
    add("INV1", (256, 128), F32)
    add("FIN", (512, 768), BF)
    add("HID", (4, 512, 384), BF)
    add("GEL", (4, 512, 384), F32)
    add("SEC", (512, 768), F32)
    add("SECR", (256, 768), F32)
    add("GS", (256, 768), F32)
    add("GFB", (512, 768), BF)
    add("GB", (256, 768), BF)
    add("IGS", (256, 768), BF)
    add("IGR", (256, 768), BF)
    add("T", (768, 1152), F32)
    add("S0", (768, 384), BF)
    add("R0", (768, 384), BF)
    for p in PIECES:
        r, c, a = ROWS[p], COLS[p], APART[p]
        b = r - a
        sizes = (8 * r, 8 * r, 8 * r, 4 * a, 4 * a, 3 * a, 3 * a, 6 * b, 6 * b, b, b)
        for key, size in zip(PER_PIECE, sizes):
            add(key + p, (size, c), F32 if key == "G" else BF)
    add("VS", (96, 768), F32)
    add("VR", (96, 768), F32)
    items.append(("ss", pltpu.SemaphoreType.DMA((COPIES,))))
    items.append(("rs", pltpu.SemaphoreType.DMA((COPIES,))))
    items.append(("ls", pltpu.SemaphoreType.DMA((1 + len(MOVED_IN) + len(MOVED_OUT),))))
    return items


IN_NAMES = ("tok", "wq", "wk", "wv", "wo", "ga", "ba", "wu", "wd", "gf", "bf", "len", "off", "og")
MOVED_IN = (
    ("wq", (48, 384), F32),
    ("wk", (48, 384), F32),
    ("wv", (48, 384), F32),
    ("ga", (24,), F32),
    ("ba", (24,), F32),
    ("gf", (24,), F32),
    ("bf", (24,), F32),
    ("tok", (256, 768), BF),
    ("wo", (24, 768), F32),
    ("wu", (96, 768), F32),
    ("wd", (96, 768), F32),
    ("og", (256, 768), BF),
)
MOVED_OUT = (
    ("out", (256, 768), BF),
    ("ig", (256, 768), BF),
    ("dwq", (48, 384), F32),
    ("dwk", (48, 384), F32),
    ("dwv", (48, 384), F32),
    ("dwo", (24, 768), F32),
    ("dga", (24,), F32),
    ("dba", (24,), F32),
    ("dwu", (96, 768), F32),
    ("dwd", (96, 768), F32),
    ("dgf", (24,), F32),
    ("dbf", (24,), F32),
)
OUT_NAMES = ("out", "ig", "dwq", "dwk", "dwv", "dwo", "dga", "dba", "dwu", "dwd", "dgf", "dbf")


def layer_kernel(*refs):
    ins = tuple(n if n in ("len", "off") else "far_" + n for n in IN_NAMES)
    outs = tuple("far_" + n for n in OUT_NAMES)
    names = ins + outs + tuple(n for n, _ in scratch_list())
    named = dict(zip(names, refs))
    r = types.SimpleNamespace(**named)
    for key in PER_PIECE:
        setattr(r, key, {p: named[key + p] for p in PIECES})
    me = lax.axis_index(DP)
    c = lax.axis_index(HEAD)
    x = lax.rem(me, 2)
    y = lax.rem(lax.div(me, 2), 2)
    z = lax.div(me, 4)
    u = x + c * (y - x)
    v = y + c * (x - y)
    ub = 1 + c
    vb = 2 - c
    zs = (z, z + 1 - 2 * lax.rem(z, 2), lax.rem(z + 2, 4), 3 - z)

    def chip(m):
        zm, du, dv = m // 4, (m // 2) % 2, m % 2
        uu = 1 - u if du else u
        vv = 1 - v if dv else v
        return 4 * zs[zm] + ub * uu + vb * vv

    ids = [chip(m) for m in range(16)]
    partner = (me, 1 - c)
    base256, base24, other24 = 256 * c, 24 * c, 24 * (1 - c)
    own_rows = pl.ds(pl.multiple_of(256 * c, 256), 256)
    oth_rows = pl.ds(pl.multiple_of(256 * (1 - c), 256), 256)

    in_copies, out_copies = {}, []
    for k, (n, _, _) in enumerate(MOVED_IN):
        in_copies[n] = pltpu.make_async_copy(named["far_" + n], named[n], r.ls.at[1 + k])
        in_copies[n].start()

    def arrived(*keys):
        for n in keys:
            in_copies[n].wait()

    def put(*keys):
        for n in keys:
            k = 1 + len(MOVED_IN) + OUT_NAMES.index(n)
            cp = pltpu.make_async_copy(named[n], named["far_" + n], r.ls.at[k])
            cp.start()
            out_copies.append(cp)

    peers = [partner] + [(ids[m], c) for m in (MU, MV, 4, 8, 12)]
    barrier = pltpu.get_barrier_semaphore()
    for dev in peers:
        pl.semaphore_signal(barrier, inc=1, device_id=dev, device_id_type=MESH)
    pl.semaphore_wait(barrier, len(peers))

    sends = []
    recv_ids = {}

    def recv_sem(key):
        if key not in recv_ids:
            recv_ids[key] = len(recv_ids)
        return r.rs.at[recv_ids[key]]

    def send(key, src, dst, dev):
        cp = pltpu.make_async_remote_copy(
            src_ref=src,
            dst_ref=dst,
            send_sem=r.ss.at[len(sends)],
            recv_sem=recv_sem(key),
            device_id=dev,
            device_id_type=MESH,
        )
        cp.start()
        sends.append((src, dst, len(sends), key, dev))

    def wait_send(entry):
        src, dst, k, key, dev = entry
        pltpu.make_async_remote_copy(
            src_ref=src,
            dst_ref=dst,
            send_sem=r.ss.at[k],
            recv_sem=recv_sem(key),
            device_id=dev,
            device_id_type=MESH,
        ).wait_send()

    waited = set()

    def wait_sent(key):
        for entry in sends:
            if entry[3] == key:
                wait_send(entry)
                waited.add(key)

    def wait_recv(key, ref):
        pltpu.make_async_remote_copy(
            src_ref=ref,
            dst_ref=ref,
            send_sem=r.ss.at[0],
            recv_sem=recv_sem(key),
            device_id=partner,
            device_id_type=MESH,
        ).wait_recv()

    def wbuf(p):
        return {"Q": r.WQ, "O": r.WOP.at[c], "U": r.WU, "D": r.WD}[p]

    starts = {}
    for n_rows in (48, 96):
        for m in range(16):
            first = pl.multiple_of(ids[m] * n_rows, 16)
            third = pl.multiple_of(ids[m] * n_rows + 2 * n_rows // 3, 16)
            starts[n_rows, m] = (first, third)

    def wslice(p, part, m):
        a, rows = APART[p], ROWS[p]
        first, third = starts[rows, m]
        if part == "A":
            return wbuf(p).at[pl.ds(first, a), :]
        return wbuf(p).at[pl.ds(third, rows - a), :]

    def forward(p, part, m, f):
        ref = wslice(p, part, m)
        send(("ag", p, part, m ^ f), ref, ref, (ids[f], c))

    def got(p, part, m):
        wait_recv(("ag", p, part, m), wslice(p, part, m))

    def ag_own(p):
        forward(p, "C", 0, MU)
        for f in (4, 8, 12):
            forward(p, "A", 0, f)
        forward(p, "A", 0, MU)
        forward(p, "A", 0, MV)
        for f in (4, 8, 12):
            forward(p, "C", 0, f)
        forward(p, "C", 0, MV)

    def ag_steps(p):
        steps = []

        def step(part, m, flips):
            def run():
                got(p, part, m)
                for f in flips:
                    forward(p, part, m, f)

            steps.append(run)

        step("C", MU, (4, 8, 12, MV))
        step("A", MU, (MV,))
        for zz in (4, 8, 12):
            step("A", zz, (MU, MV))
        for zz in (4, 8, 12):
            step("C", zz, (MV,))
            step("C", zz + MU, (MV,))
        for zz in (4, 8, 12):
            step("A", zz + MU, (MV,))
        return steps

    def ag_plane(p, zm):
        for m in (4 * zm + MV, 4 * zm + MU + MV):
            got(p, "A", m)
            got(p, "C", m)

    def run(steps):
        for s in steps:
            s()

    flip_u, flip_v = ((ids[MU], c),), ((ids[MV], c),)
    line = tuple((ids[m], c) for m in (4, 8, 12))
    vec_peers = ((line, flip_v, flip_u, (partner,)), ((partner,), flip_v, flip_u, line))

    def vec_slots(k, s):
        first = 48 * k + 8 * (s + (2 if k == 0 and s else 0))
        return [pl.ds(first + 8 * j, 8) for j in range(len(vec_peers[k][s]))]

    def vec_send(k, s):
        for j, (slot, dev) in enumerate(zip(vec_slots(k, s), vec_peers[k][s])):
            send(("v", k, s, j), r.VS.at[pl.ds(48 * k + 8 * s, 8), :], r.VR.at[slot, :], dev)

    def vec_step(k, s):
        total = r.VS[pl.ds(48 * k + 8 * s, 8), :]
        for j, slot in enumerate(vec_slots(k, s)):
            wait_recv(("v", k, s, j), r.VR.at[slot, :])
            total = total + r.VR[slot, :]
        r.VS[pl.ds(48 * k + (8 * s + 8 if s < 3 else 40), 8), :] = total
        if s < 3:
            vec_send(k, s + 1)

    def rs1_send(p, zm):
        rows = 2 * ROWS[p]
        s = pl.ds(zm * rows, rows)
        send(("r1", p, zm), r.S1[p].at[s, :], r.R1[p].at[s, :], (ids[MV], c))

    def rs_sum1(p, zm):
        rows, a = ROWS[p], APART[p]
        b = rows - a
        g, r1 = r.G[p], r.R1[p]
        s = pl.ds(zm * 2 * rows, 2 * rows)
        wait_recv(("r1", p, zm), r1.at[s, :])
        for du in (1, 0):
            o = (2 * zm + du) * rows
            top = g[o : o + a, :] + r1[o : o + a, :].astype(F32)
            low = g[o + a : o + rows, :] + r1[o + a : o + rows, :].astype(F32)
            if du == 1:
                q = pl.ds(zm * a, a)
                r.S2A[p][q, :] = top.astype(BF)
                send(("r2a", p, zm), r.S2A[p].at[q, :], r.R2A[p].at[q, :], (ids[MU], c))
            else:
                g[o : o + a, :] = top
            if zm:
                q = pl.ds(((zm - 1) * 2 + du) * b, b)
                r.S2C[p][q, :] = low.astype(BF)
            else:
                g[o + a : o + rows, :] = low
        if zm:
            q = pl.ds((zm - 1) * 2 * b, 2 * b)
            send(("r2c", p, zm), r.S2C[p].at[q, :], r.R2C[p].at[q, :], (ids[4 * zm], c))

    def rs_sum2a(p, zm):
        rows, a = ROWS[p], APART[p]
        g, r2 = r.G[p], r.R2A[p]
        q = pl.ds(zm * a, a)
        wait_recv(("r2a", p, zm), r2.at[q, :])
        o = 2 * zm * rows
        val = g[o : o + a, :] + r2[q, :].astype(F32)
        if zm:
            k = pl.ds((zm - 1) * a, a)
            r.S3A[p][k, :] = val.astype(BF)
            send(("r3a", p, zm), r.S3A[p].at[k, :], r.R3A[p].at[k, :], (ids[4 * zm], c))
        else:
            g[o : o + a, :] = val

    def rs_sum2c(p):
        rows, a = ROWS[p], APART[p]
        b = rows - a
        g, r2 = r.G[p], r.R2C[p]
        for zm in (1, 2, 3):
            wait_recv(("r2c", p, zm), r2.at[pl.ds((zm - 1) * 2 * b, 2 * b), :])
        for du in (1, 0):
            o = du * rows + a
            val = g[o : o + b, :]
            for zm in (1, 2, 3):
                k = ((zm - 1) * 2 + du) * b
                val = val + r2[k : k + b, :].astype(F32)
            if du == 1:
                r.S3C[p][...] = val.astype(BF)
                send(("r3c", p), r.S3C[p], r.R3C[p], (ids[MU], c))
            else:
                g[o : o + b, :] = val

    def rs_final(p):
        rows, a = ROWS[p], APART[p]
        g = r.G[p]
        r3a, r3c = r.R3A[p], r.R3C[p]
        for zm in (1, 2, 3):
            wait_recv(("r3a", p, zm), r3a.at[pl.ds((zm - 1) * a, a), :])
        val = g[0:a, :]
        for zm in (1, 2, 3):
            val = val + r3a[(zm - 1) * a : zm * a, :].astype(F32)
        g[0:a, :] = val
        wait_recv(("r3c", p), r3c)
        g[a:rows, :] = g[a:rows, :] + r3c[...].astype(F32)

    def block_row(zm, du, dv):
        uu = 1 - u if du else u
        vv = 1 - v if dv else v
        return ub * uu + vb * vv

    def stage(p, zm, src, base):
        rows, cols = ROWS[p], COLS[p]
        for du in (1, 0):
            k = (2 * zm + du) * rows
            far = pl.ds(pl.multiple_of(base + block_row(zm, du, 1) * rows, 8), rows)
            near = pl.ds(pl.multiple_of(base + block_row(zm, du, 0) * rows, 8), rows)
            r.S1[p][k : k + rows, :] = src[far, 0:cols].astype(BF)
            r.G[p][k : k + rows, :] = src[near, 0:cols]

    flat = 2 * me + c
    arrived("wq", "wk", "wv")
    r.WQ[pl.ds(pl.multiple_of(me * 48, 16), 48), 0:384] = r.wq[...].astype(BF)
    r.WQ[pl.ds(pl.multiple_of(me * 48, 16), 48), 384:768] = r.wk[...].astype(BF)
    r.WQ[pl.ds(pl.multiple_of(me * 48, 16), 48), 768:1152] = r.wv[...].astype(BF)
    ag_own("Q")
    arrived("tok")
    send("tok", r.tok, r.X.at[own_rows, :], partner)
    local = pltpu.make_async_copy(r.tok, r.X.at[own_rows, :], r.ls.at[0])
    local.start()
    arrived("ga", "ba", "gf", "bf")
    r.VS[0:8, :] = jnp.zeros((8, 768), F32)
    for k, n in enumerate(("ga", "ba", "gf", "bf")):
        r.VS[k : k + 1, 0:24] = getattr(r, n)[...].reshape(1, 24).astype(BF).astype(F32)
    r.VS[0:8, :] = pltpu.roll(r.VS[0:8, :], 24 * flat, 1)
    vec_send(0, 0)
    arrived("wo")
    wo = r.wo[...]
    r.WOP[c, pl.ds(pl.multiple_of(me * 48, 16), 48), :] = jnp.concatenate(
        [wo[:, 0:384], wo[:, 384:768]], axis=0
    ).astype(BF)
    arrived("wu", "wd", "og")
    r.WU[pl.ds(pl.multiple_of(me * 96, 16), 96), :] = r.wu[...].astype(BF)
    r.WD[pl.ds(pl.multiple_of(me * 96, 16), 96), :] = r.wd[...].astype(BF)

    q_steps, o_steps, u_steps, d_steps = (ag_steps(p) for p in PIECES)
    run(q_steps[:5])
    ag_own("O")
    run(o_steps[:1])

    col_pos = lax.broadcasted_iota(jnp.int32, (512, 128), 0)
    row_pos = lax.broadcasted_iota(jnp.int32, (8, 512), 1)
    col_lab = jnp.zeros((512, 128), jnp.int32)
    row_lab = jnp.zeros((8, 512), jnp.int32)
    for j in range(8):
        lo = r.off[0, j]
        hi = lo + r.len[0, j]
        col_lab = jnp.where((col_pos >= lo) & (col_pos < hi), j + 1, col_lab)
        row_lab = jnp.where((row_pos >= lo) & (row_pos < hi), j + 1, row_lab)
    r.LIVE[...] = jnp.where(col_lab > 0, 1.0, 0.0).astype(F32)
    row_lab = jnp.where(row_lab > 0, row_lab, -1)
    for t in range(4):
        q = slice(128 * t, 128 * t + 128)
        lab = jnp.concatenate([col_lab[q]] * 4, axis=1)
        same = lab == jnp.broadcast_to(row_lab[0:1], (128, 512))
        r.BIAS[q, :] = jnp.where(same, 0.0, -1e30).astype(F32)

    run(q_steps[5:])
    vec_step(0, 0)
    run(o_steps[1:5])
    ag_own("U")
    wait_recv("tok", r.X.at[own_rows, :])
    local.wait()
    for zm in range(4):
        ag_plane("Q", zm)

    for k, n in enumerate(("Q3", "K3", "V3")):
        full = mm(r.X[...], r.WQ[:, 384 * k : 384 * k + 384])
        full = full.astype(BF)
        if k == 0:
            full = full * BF(0.125)
        for i in range(3):
            getattr(r, n)[i] = full[:, 128 * i : 128 * i + 128]
    run(u_steps[:1])
    vec_step(0, 1)

    for i in range(3):
        r.ATT[i] = jnp.zeros((512, 128), BF)
    fw_hooks = [
        o_steps[5:8],
        o_steps[8:],
        [functools.partial(vec_step, 0, 2)] + u_steps[1:3],
        u_steps[3:5],
        u_steps[5:8],
        u_steps[8:10],
    ]
    lane = lax.broadcasted_iota(jnp.int32, (1, 128), 1)

    def half(val, a):
        keep = (lane >= 64 * a) & (lane < 64 * a + 64)
        return jnp.where(keep, val, jnp.zeros_like(val))

    def at_index(h, hooks):
        for k, steps in enumerate(hooks):

            def go(steps=steps):
                run(steps)

            pl.when(h == k)(go)

    def fwd_head(h, carry):
        at_index(h, fw_hooks)
        i = lax.div(h, 2)
        a = lax.rem(h, 2)
        vals = half(r.V3[i], a)
        keys = half(r.K3[i], a)
        for t in range(4):
            q = slice(128 * t, 128 * t + 128)
            s = mm(r.Q3[i, q, :], keys, 1, 1) + r.BIAS[q, :]
            live = r.LIVE[q, 0:1]
            top = jnp.where(live > 0, jnp.max(s, axis=1, keepdims=True), 0.0)
            w = jnp.exp(s - top)
            total = jnp.sum(w, axis=1, keepdims=True) + (1.0 - live)
            prob = w * (1.0 / total)
            r.P32[h, q, :] = prob
            o = mm(prob.astype(BF), vals)
            r.ATT[i, q, :] = r.ATT[i, q, :] + o.astype(BF)
        return carry

    lax.fori_loop(0, 6, fwd_head, 0)

    send("att", r.ATT.at[:, oth_rows, :], r.ATTR, partner)
    ag_own("D")
    for zm in range(4):
        ag_plane("O", zm)
    send("wop", r.WOP.at[c], r.WOP.at[c], partner)
    run(d_steps[:1] + u_steps[10:12])
    vec_step(0, 3)
    wait_recv("wop", r.WOP.at[1 - c])

    def build_out(i, carry):
        for k in range(2):
            blk = r.WOP[k, pl.ds(pl.multiple_of(48 * i, 16), 48), :].astype(F32)
            rows = jnp.concatenate([blk[0:24], blk[24:48]], axis=1)
            r.T[pl.ds(pl.multiple_of(48 * i + 24 * k, 8), 24), 0:768] = rows
        return carry

    lax.fori_loop(0, 16, build_out, 0)
    r.WO[...] = r.T[:, 0:768].astype(BF)
    wait_recv("att", r.ATTR)
    own_heads = pl.ds(pl.multiple_of(384 * c, 128), 384)
    oth_heads = pl.ds(pl.multiple_of(384 * (1 - c), 128), 384)

    def joined(ref, rows):
        return jnp.concatenate([ref[i, rows, :] for i in range(3)], axis=1)

    all256 = pl.ds(0, 256)
    branch = mm(joined(r.ATT, own_rows), r.WO[own_heads, :])
    branch = branch + mm(joined(r.ATTR, all256), r.WO[oth_heads, :])
    r.GS[...] = branch
    run(u_steps[12:] + d_steps[1:2])

    def norm(val):
        mean = jnp.mean(val, axis=1, keepdims=True)
        cen = val - mean
        inv = lax.rsqrt(jnp.mean(cen * cen, axis=1, keepdims=True) + EPS)
        return cen * inv, inv

    def ln1(t, carry):
        q = pl.ds(pl.multiple_of(64 * t, 64), 64)
        unit, inv = norm(r.tok[q, :].astype(F32) + r.GS[q, :])
        r.U1[q, :] = unit
        r.INV1[q, :] = jnp.broadcast_to(inv, (64, 128))
        one = unit * r.VS[40:41, :] + r.VS[41:42, :]
        r.N1[q, :] = one
        r.FIN[pl.ds(pl.multiple_of(base256 + 64 * t, 64), 64), :] = one.astype(BF)
        return carry

    lax.fori_loop(0, 4, ln1, 0)
    send("fin", r.FIN.at[own_rows, :], r.FIN.at[own_rows, :], partner)
    run(d_steps[2:5])
    wait_recv("fin", r.FIN.at[oth_rows, :])

    def plane_rows(zm):
        return pl.ds(pl.multiple_of(384 * zs[zm], 128), 384)

    def ffn_up(zm):
        for t in range(2):
            q = slice(256 * t, 256 * t + 256)
            pre = mm(r.FIN[q, :], r.WU[plane_rows(zm), :], 1, 1)
            r.GEL[zm, q, :] = pre

        def act(t, carry):
            q = pl.ds(pl.multiple_of(64 * t, 64), 64)
            pre = r.GEL[zm, q, :]
            cdf = 0.5 * (1.0 + lax.erf(pre * (2.0**-0.5)))
            pdf = jnp.exp(-0.5 * pre * pre) * (1.0 / math.sqrt(2.0 * math.pi))
            r.HID[zm, q, :] = (pre * cdf).astype(BF)
            r.GEL[zm, q, :] = cdf + pre * pdf
            return carry

        lax.fori_loop(0, 8, act, 0)

    d_groups = ([], d_steps[5:8], d_steps[8:11], d_steps[11:])
    for zm in range(4):
        ag_plane("U", zm)
        run(d_groups[zm])
        ffn_up(zm)
    for zm in range(4):
        ag_plane("D", zm)
        for rows in (oth_rows, own_rows):
            part = mm(r.HID[zm, rows, :], r.WD[plane_rows(zm), :])
            if zm:
                part = part + r.SEC[rows, :]
            r.SEC[rows, :] = part
            if zm == 3 and rows is oth_rows:
                for h in range(2):
                    part_rows = pl.ds(pl.multiple_of(256 * (1 - c) + 128 * h, 128), 128)
                    send(("sec", h), r.SEC.at[part_rows, :], r.SECR.at[pl.ds(128 * h, 128), :], partner)

    def ln2(t, sums):
        dg, db = sums
        q = pl.ds(pl.multiple_of(64 * t, 64), 64)
        qq = pl.ds(pl.multiple_of(base256 + 64 * t, 64), 64)
        unit, inv = norm(r.N1[q, :] + (r.SEC[qq, :] + r.SECR[q, :]))
        gain = r.VS[42:43, :]
        r.out[q, :] = (unit * gain + r.VS[43:44, :]).astype(BF)
        e = r.og[q, :].astype(F32)
        dg = dg + jnp.sum(e * unit, axis=0, keepdims=True)
        db = db + jnp.sum(e, axis=0, keepdims=True)
        eg = e * gain
        inner = jnp.mean(eg * unit, axis=1, keepdims=True)
        gs = inv * (eg - jnp.mean(eg, axis=1, keepdims=True) - unit * inner)
        r.GS[q, :] = gs
        r.GFB[qq, :] = gs.astype(BF)
        return dg, db

    zero = jnp.zeros((1, 768), F32)
    dg2, db2 = zero, zero
    for h in range(2):
        wait_recv(("sec", h), r.SECR.at[pl.ds(128 * h, 128), :])
        dg2, db2 = lax.fori_loop(2 * h, 2 * h + 2, ln2, (dg2, db2))
        part_rows = r.GFB.at[pl.ds(pl.multiple_of(base256 + 128 * h, 128), 128), :]
        send(("gfb", h), part_rows, part_rows, partner)
    put("out")
    r.T[0:384, 0:768] = mm(r.HID[3, own_rows, :], r.GFB[own_rows, :], 0, 0)
    for h in range(2):
        wait_recv(("gfb", h), r.GFB.at[pl.ds(pl.multiple_of(256 * (1 - c) + 128 * h, 128), 128), :])
    for h in range(2):
        wait_sent(("sec", h))

    for n_done, zm in enumerate((3, 2, 1, 0)):
        if zm == 3:
            r.T[0:384, 0:768] = r.T[0:384, 0:768] + mm(r.HID[3, oth_rows, :], r.GFB[oth_rows, :], 0, 0)
        else:
            r.T[0:384, 0:768] = mm(r.HID[zm], r.GFB[...], 0, 0)
        stage("D", zm, r.T, 0)
        if zm > 1:
            rs1_send("D", zm)
        for t in range(2):
            q = slice(256 * t, 256 * t + 256)
            gh = mm(r.GFB[q, :], r.WD[plane_rows(zm), :], 1, 1)
            r.HID[zm, q, :] = (gh * r.GEL[zm, q, :]).astype(BF)
        r.T[384:768, 0:768] = mm(r.HID[zm], r.FIN[...], 0, 0)
        stage("U", zm, r.T, 384)
        if zm > 1:
            rs1_send("U", zm)
        for rows in (oth_rows, own_rows):
            part = mm(r.HID[zm, rows, :], r.WU[plane_rows(zm), :])
            if n_done:
                part = part + r.SEC[rows, :]
            r.SEC[rows, :] = part
            if n_done == 3 and rows is oth_rows:
                send("gn", r.SEC.at[oth_rows, :], r.SECR, partner)
        if n_done == 2:
            rs_sum1("D", 3)
    rs_sum1("U", 3)
    rs1_send("D", 1)
    wait_recv("gn", r.SECR)

    def ln1_back(t, sums):
        dg, db = sums
        q = pl.ds(pl.multiple_of(64 * t, 64), 64)
        qq = pl.ds(pl.multiple_of(base256 + 64 * t, 64), 64)
        e = r.GS[q, :] + (r.SEC[qq, :] + r.SECR[q, :])
        unit = r.U1[q, :]
        inv = r.INV1[q, 0:1]
        dg = dg + jnp.sum(e * unit, axis=0, keepdims=True)
        db = db + jnp.sum(e, axis=0, keepdims=True)
        eg = e * r.VS[40:41, :]
        inner = jnp.mean(eg * unit, axis=1, keepdims=True)
        first = inv * (eg - jnp.mean(eg, axis=1, keepdims=True) - unit * inner)
        r.GS[q, :] = first
        r.GB[q, :] = first.astype(BF)
        return dg, db

    dg1, db1 = lax.fori_loop(0, 4, ln1_back, (zero, zero))
    r.VS[48:56, :] = jnp.zeros((8, 768), F32)
    for k, val in enumerate((dg1, db1, dg2, db2)):
        r.VS[48 + k : 49 + k, :] = val
    vec_send(1, 0)

    gview = mm(r.GB[...], r.WO[oth_heads, :], 1, 1).astype(BF)
    for i in range(3):
        r.GAS[i] = gview[:, 128 * i : 128 * i + 128]
    send("gas", r.GAS, r.GA.at[:, own_rows, :], partner)
    gview = mm(r.GB[...], r.WO[own_heads, :], 1, 1).astype(BF)
    for i in range(3):
        r.GA[i, own_rows, :] = gview[:, 128 * i : 128 * i + 128]
    vec_step(1, 0)
    rs_sum2a("D", 3)
    rs1_send("U", 1)
    r.T[own_heads, 0:768] = mm(joined(r.ATT, own_rows), r.GB[...], 0, 0)
    r.T[oth_heads, 0:768] = mm(joined(r.ATTR, all256), r.GB[...], 0, 0)

    def pair_out(i, carry):
        q = pl.ds(pl.multiple_of(48 * i, 16), 48)
        blk = r.T[pl.ds(pl.multiple_of(48 * i + other24, 8), 24), 0:768]
        r.S0[q, :] = jnp.concatenate([blk[:, 0:384], blk[:, 384:768]], axis=0).astype(BF)
        return carry

    lax.fori_loop(0, 16, pair_out, 0)
    send("s0", r.S0, r.R0, partner)
    rs_sum1("D", 2)
    rs_sum2a("U", 3)
    wait_recv("s0", r.R0)

    def out_block(m):
        i = ids[m]
        blk = r.T[pl.ds(pl.multiple_of(48 * i + base24, 8), 24), 0:768]
        blk = jnp.concatenate([blk[:, 0:384], blk[:, 384:768]], axis=0)
        return blk + r.R0[pl.ds(pl.multiple_of(48 * i, 16), 48), :].astype(F32)

    for zm in (3, 2, 1, 0):
        for du in (1, 0):
            k = (2 * zm + du) * 48
            r.S1["O"][k : k + 48, :] = out_block(4 * zm + 2 * du + 1).astype(BF)
            r.G["O"][k : k + 48, :] = out_block(4 * zm + 2 * du)
        if zm > 1:
            rs1_send("O", zm)

    wait_recv("gas", r.GA.at[:, oth_rows, :])
    for n in ("DQ", "DK", "DV"):
        for i in range(3):
            getattr(r, n)[i] = jnp.zeros((512, 128), BF)

    def s1(p, zm):
        return functools.partial(rs_sum1, p, zm)

    def s2a(p, zm):
        return functools.partial(rs_sum2a, p, zm)

    def s2c(p):
        return functools.partial(rs_sum2c, p)

    def vs(s):
        return functools.partial(vec_step, 1, s)

    bw_hooks = [
        [],
        [s1("U", 2)],
        [s2a("D", 2)],
        [],
        [s1("D", 1)],
        [s2a("U", 2), vs(1)],
    ]

    def bwd_head(h, carry):
        at_index(h, bw_hooks)
        i = lax.div(h, 2)
        a = lax.rem(h, 2)
        go = half(r.GA[i], a)
        for t in range(4):
            q = slice(128 * t, 128 * t + 128)
            prob = r.P32[h, q, :]
            dp = mm(go[q], r.V3[i], 1, 1)
            delta = jnp.sum(prob * dp, axis=1, keepdims=True)
            r.DSB[q, :] = (prob * (dp - delta)).astype(BF)
            r.PB[q, :] = prob.astype(BF)
        r.DV[i] = r.DV[i] + mm(r.PB[...], go, 0, 0).astype(BF)
        dq = mm(r.DSB[...], half(r.K3[i], a)) * 0.125
        r.DQ[i] = r.DQ[i] + dq.astype(BF)
        dk = mm(r.DSB[...], half(r.Q3[i], a), 0, 0)
        r.DK[i] = r.DK[i] + dk.astype(BF)
        return carry

    lax.fori_loop(0, 6, bwd_head, 0)

    all512 = pl.ds(0, 512)
    for k, n in enumerate(("DQ", "DK", "DV")):
        r.T[:, 384 * k : 384 * k + 384] = mm(r.X[...], joined(getattr(r, n), all512), 0, 0)
    for zm in (3, 2, 1, 0):
        stage("Q", zm, r.T, 192 * zs[zm])
        if zm > 1:
            rs1_send("Q", zm)

    def s0(p, zm):
        return functools.partial(rs1_send, p, zm)

    run([s1("U", 1), s2a("D", 1), vs(2), s0("Q", 1), s0("O", 1)])

    for rows in (oth_rows, own_rows):
        acc = mm(joined(r.DQ, rows), r.WQ[:, 0:384], 1, 1)
        acc = acc + mm(joined(r.DK, rows), r.WQ[:, 384:768], 1, 1)
        acc = acc + mm(joined(r.DV, rows), r.WQ[:, 768:1152], 1, 1)
        if rows is oth_rows:
            r.IGS[...] = acc.astype(BF)
            send("ig", r.IGS, r.IGR, partner)
            run([s1("O", 3), s1("O", 2), s2a("U", 1), s2a("O", 3), s0("D", 0)])
        else:
            r.GS[...] = r.GS[...] + acc
    wait_recv("ig", r.IGR)
    r.ig[...] = (r.GS[...] + r.IGR[...].astype(F32)).astype(BF)
    put("ig")

    run([s1("Q", 3), s2a("O", 2), s0("U", 0), s1("Q", 2), s2a("Q", 3), s0("Q", 0)])
    run([s1("Q", 1), s2a("Q", 2), s1("O", 1), s2a("Q", 1), s1("D", 0), s2a("O", 1), s2c("D")])
    run([s1("U", 0), s2c("U"), s2a("D", 0), s0("O", 0), s1("Q", 0), s2c("Q"), s2a("U", 0)])
    run([s2a("Q", 0), s1("O", 0), s2c("O"), s2a("O", 0)])
    rs_final("Q")
    r.dwq[...] = r.G["Q"][0:48, 0:384]
    r.dwk[...] = r.G["Q"][0:48, 384:768]
    r.dwv[...] = r.G["Q"][0:48, 768:1152]
    rs_final("D")
    r.dwd[...] = r.G["D"][0:96, :]
    put("dwq", "dwk", "dwv", "dwd")
    rs_final("U")
    r.dwu[...] = r.G["U"][0:96, :]
    rs_final("O")
    vec_step(1, 3)
    go = r.G["O"][0:48, :]
    r.dwo[...] = jnp.concatenate([go[0:24], go[24:48]], axis=1)
    back = pltpu.roll(r.VS[88:96, :], lax.rem(768 - 24 * flat, 768), 1)
    for k, n in enumerate(("dga", "dba", "dgf", "dbf")):
        getattr(r, n)[...] = back[k, 0:24]
    put("dwu", "dwo", "dga", "dba", "dgf", "dbf")

    for entry in sends:
        if entry[3] not in waited:
            wait_send(entry)
    for cp in out_copies:
        cp.wait()


def hand_over(*refs):
    half = len(refs) // 2
    for src, dst in zip(refs[:half], refs[half:]):
        dst[...] = src[...]


def layer_small(*args):
    shapes = tuple((shape, dtype) for _, shape, dtype in MOVED_OUT)
    vmem = pl.BlockSpec(memory_space=pltpu.VMEM)
    smem = pl.BlockSpec(memory_space=pltpu.SMEM)
    anywhere = pl.BlockSpec(memory_space=pl.ANY)
    out_shape = tuple(jax.ShapeDtypeStruct(s, d) for s, d in shapes)
    up = IN_NAMES.index("wu")
    args = args[:up] + (args[up].T,) + args[up + 1 :]
    outs = pl.pallas_call(
        layer_kernel,
        out_shape=out_shape,
        in_specs=[smem if n in ("len", "off") else anywhere for n in IN_NAMES],
        out_specs=tuple(anywhere for _ in shapes),
        scratch_shapes=[s for _, s in scratch_list()],
        compiler_params=pltpu.CompilerParams(
            collective_id=0, has_side_effects=True, vmem_limit_bytes=67043328
        ),
    )(*args)
    outs = pl.pallas_call(
        hand_over,
        out_shape=out_shape,
        in_specs=[vmem for _ in shapes],
        out_specs=tuple(vmem for _ in shapes),
    )(*outs)
    up = OUT_NAMES.index("dwu")
    return outs[:up] + (outs[up].T,) + outs[up + 1 :]


def labels_of(lengths, offsets):
    position = jnp.arange(BIN, dtype=jnp.int32)[:, None]
    starts = offsets[None, :]
    inside = (position >= starts) & (position < starts + lengths[None, :])
    slot_order = jnp.arange(1, lengths.shape[0] + 1, dtype=jnp.int32)[None, :]
    return jnp.sum(jnp.where(inside, slot_order, 0), axis=1)


def layer_norm(operand, gain_vec, bias_vec):
    row_mean = jnp.mean(operand, axis=-1, keepdims=True)
    centered = operand - row_mean
    inverse = lax.rsqrt(jnp.mean(centered * centered, axis=-1, keepdims=True) + EPS)
    normed = centered * inverse
    return (normed * gain_vec + bias_vec, normed, inverse)


def norm_back(grad_rows, normed, inverse, gain_vec):
    scaled = grad_rows * gain_vec
    inner = jnp.mean(scaled * normed, axis=-1, keepdims=True)
    return inverse * (scaled - jnp.mean(scaled, axis=-1, keepdims=True) - normed * inner)


def gelu_exact(operand):
    return jax.nn.gelu(operand, approximate=False)


def contract_rows(left, right):
    return lax.dot_general(
        left, right, (((0,), (0,)), ((), ())), preferred_element_type=F32
    )


def contract_cols(left, right):
    return lax.dot_general(
        left, right, (((1,), (1,)), ((), ())), preferred_element_type=F32
    )


def score_block(queries, key_rows, labels_bin, factor):
    scores = (
        jnp.einsum("qhd,khd->hqk", queries, key_rows, preferred_element_type=F32) * factor
    )
    allowed = ((labels_bin[:, None] == labels_bin[None, :]) & (labels_bin[:, None] > 0))[None]
    live_rows = (labels_bin > 0)[None, :, None]
    return (scores, allowed, live_rows)


def masked_exp(scores, allowed, row_top):
    return jnp.where(allowed, jnp.exp(jnp.where(allowed, scores - row_top, 0.0)), 0.0)


def attend_bin(pieces, factor):
    queries, key_rows, value_rows, labels_bin = pieces
    scores, allowed, live_rows = score_block(queries, key_rows, labels_bin, factor)
    row_top = jnp.max(jnp.where(allowed, scores, -1e30), axis=2, keepdims=True)
    row_top = jnp.where(live_rows, row_top, 0.0)
    weights = masked_exp(scores, allowed, row_top)
    denominator = jnp.sum(weights, axis=2, keepdims=True) + jnp.where(live_rows, 0.0, 1.0)
    probability = (weights / denominator).astype(jnp.bfloat16)
    mixed_rows = jnp.einsum(
        "hqk,khd->qhd", probability, value_rows, preferred_element_type=F32
    )
    return (mixed_rows.astype(jnp.bfloat16), row_top, denominator)


def attend_back(pieces, factor):
    queries, key_rows, value_rows, labels_bin, row_top, denominator, grad_mixed = pieces
    scores, allowed, live_rows = score_block(queries, key_rows, labels_bin, factor)
    probability = masked_exp(scores, allowed, row_top) / denominator
    grad_values = jnp.einsum(
        "hqk,qhd->khd",
        probability.astype(jnp.bfloat16),
        grad_mixed,
        preferred_element_type=F32,
    )
    grad_probs = jnp.einsum(
        "qhd,khd->hqk", grad_mixed, value_rows, preferred_element_type=F32
    )
    row_delta = jnp.sum(probability * grad_probs, axis=2, keepdims=True)
    grad_scores = (probability * (grad_probs - row_delta)).astype(jnp.bfloat16)
    grad_queries = (
        jnp.einsum("hqk,khd->qhd", grad_scores, key_rows, preferred_element_type=F32)
        * factor
    )
    grad_keys = (
        jnp.einsum("hqk,qhd->khd", grad_scores, queries, preferred_element_type=F32)
        * factor
    )
    return (
        grad_queries.astype(jnp.bfloat16),
        grad_keys.astype(jnp.bfloat16),
        grad_values.astype(jnp.bfloat16),
    )


def per_device(
    tokens,
    w_query,
    w_key,
    w_value,
    w_out,
    gain_attn,
    bias_attn,
    w_up,
    w_down,
    gain_ffn,
    bias_ffn,
    seq_lengths,
    seq_offsets,
    out_grad,
):
    low_type = jnp.bfloat16
    bin_count = seq_lengths.shape[0]
    group_rows = bin_count * BIN
    head_width = w_query.shape[1]
    local_heads = head_width // HD
    factor = 1.0 / math.sqrt(HD)
    labels = jax.vmap(labels_of)(seq_lengths, seq_offsets)
    full_query, full_key, full_value = (
        lax.all_gather(w_query.astype(low_type), DP, axis=0, tiled=True),
        lax.all_gather(w_key.astype(low_type), DP, axis=0, tiled=True),
        lax.all_gather(w_value.astype(low_type), DP, axis=0, tiled=True),
    )
    projection = jnp.concatenate([full_query, full_key, full_value], axis=1)
    whole_rows = lax.all_gather(tokens, HEAD, axis=0, tiled=True)
    projected = jnp.dot(whole_rows, projection, preferred_element_type=F32).astype(low_type)
    shape_bins = (bin_count, BIN, local_heads, HD)
    queries = projected[:, :head_width].reshape(shape_bins)
    key_rows = projected[:, head_width : 2 * head_width].reshape(shape_bins)
    value_rows = projected[:, 2 * head_width :].reshape(shape_bins)
    mixed_bins, row_tops, denominators = lax.map(
        lambda pieces: attend_bin(pieces, factor), (queries, key_rows, value_rows, labels)
    )
    attended = mixed_bins.reshape(group_rows, head_width)
    out_full, up_part, down_part, gain_one, bias_one, gain_two, bias_two = (
        lax.all_gather(w_out.astype(low_type), BOTH, axis=0, tiled=True),
        lax.all_gather(w_up.astype(low_type), BOTH, axis=1, tiled=True),
        lax.all_gather(w_down.astype(low_type), BOTH, axis=0, tiled=True),
        lax.all_gather(gain_attn.astype(low_type), BOTH, axis=0, tiled=True),
        lax.all_gather(bias_attn.astype(low_type), BOTH, axis=0, tiled=True),
        lax.all_gather(gain_ffn.astype(low_type), BOTH, axis=0, tiled=True),
        lax.all_gather(bias_ffn.astype(low_type), BOTH, axis=0, tiled=True),
    )
    gain_first = gain_one.astype(F32)
    gain_second = gain_two.astype(F32)
    token_view = lax.all_to_all(attended, HEAD, split_axis=0, concat_axis=1, tiled=True)
    first_sum = tokens.astype(F32) + jnp.dot(
        token_view, out_full, preferred_element_type=F32
    )
    normed_one, unit_one, inverse_one = layer_norm(
        first_sum, gain_first, bias_one.astype(F32)
    )
    ffn_input = normed_one.astype(low_type)
    pre_act = jnp.dot(ffn_input, up_part, preferred_element_type=F32)
    activated, gelu_pull = jax.vjp(gelu_exact, pre_act)
    hidden = activated.astype(low_type)
    second_sum = normed_one + jnp.dot(hidden, down_part, preferred_element_type=F32)
    result, unit_two, inverse_two = layer_norm(
        second_sum, gain_second, bias_two.astype(F32)
    )
    output = result.astype(low_type)
    grad_result = out_grad.astype(F32)
    grad_gain_two = jnp.sum(grad_result * unit_two, axis=0)
    grad_bias_two = jnp.sum(grad_result, axis=0)
    grad_second = norm_back(grad_result, unit_two, inverse_two, gain_second)
    grad_ffn = grad_second.astype(low_type)
    grad_down_part = contract_rows(hidden, grad_ffn)
    grad_pre = gelu_pull(contract_cols(grad_ffn, down_part))[0].astype(low_type)
    grad_up_part = contract_rows(ffn_input, grad_pre)
    grad_normed = grad_second + contract_cols(grad_pre, up_part)
    grad_gain_one = jnp.sum(grad_normed * unit_one, axis=0)
    grad_bias_one = jnp.sum(grad_normed, axis=0)
    grad_first = norm_back(grad_normed, unit_one, inverse_one, gain_first)
    grad_branch = grad_first.astype(low_type)
    grad_out_full = contract_rows(token_view, grad_branch)
    part_out, part_up, part_down, part_gain_one, part_bias_one, part_gain_two, part_bias_two = (
        lax.psum_scatter(grad_out_full, BOTH, scatter_dimension=0, tiled=True),
        lax.psum_scatter(grad_up_part, BOTH, scatter_dimension=1, tiled=True),
        lax.psum_scatter(grad_down_part, BOTH, scatter_dimension=0, tiled=True),
        lax.psum_scatter(grad_gain_one, BOTH, scatter_dimension=0, tiled=True),
        lax.psum_scatter(grad_bias_one, BOTH, scatter_dimension=0, tiled=True),
        lax.psum_scatter(grad_gain_two, BOTH, scatter_dimension=0, tiled=True),
        lax.psum_scatter(grad_bias_two, BOTH, scatter_dimension=0, tiled=True),
    )
    grad_token_view = contract_cols(grad_branch, out_full).astype(low_type)
    grad_attended = lax.all_to_all(grad_token_view, HEAD, split_axis=1, concat_axis=0, tiled=True)
    grad_bins = grad_attended.reshape(shape_bins)
    grad_queries, grad_keys, grad_values = lax.map(
        lambda pieces: attend_back(pieces, factor),
        (queries, key_rows, value_rows, labels, row_tops, denominators, grad_bins),
    )
    grad_projected = jnp.concatenate(
        [
            grad_queries.reshape(group_rows, head_width),
            grad_keys.reshape(group_rows, head_width),
            grad_values.reshape(group_rows, head_width),
        ],
        axis=1,
    )
    grad_projection = contract_rows(whole_rows, grad_projected)
    part_query, part_key, part_value = (
        lax.psum_scatter(grad_projection[:, :head_width], DP, scatter_dimension=0, tiled=True),
        lax.psum_scatter(
            grad_projection[:, head_width : 2 * head_width], DP, scatter_dimension=0, tiled=True
        ),
        lax.psum_scatter(
            grad_projection[:, 2 * head_width :], DP, scatter_dimension=0, tiled=True
        ),
    )
    input_grad = (
        grad_first
        + lax.psum_scatter(
            contract_cols(grad_projected, projection).astype(jnp.bfloat16),
            HEAD,
            scatter_dimension=0,
            tiled=True,
        ).astype(F32)
    ).astype(low_type)
    return (
        output,
        input_grad,
        part_query,
        part_key,
        part_value,
        part_out,
        part_gain_one,
        part_bias_one,
        part_up,
        part_down,
        part_gain_two,
        part_bias_two,
    )


def solution(mesh):
    small = mesh.shape[DP] == 16 and mesh.shape[HEAD] == 2
    return jax.shard_map(
        layer_small if small else per_device,
        mesh=mesh,
        in_specs=(
            P(BOTH, None),
            P(DP, HEAD),
            P(DP, HEAD),
            P(DP, HEAD),
            P(BOTH, None),
            P(BOTH),
            P(BOTH),
            P(None, BOTH),
            P(BOTH, None),
            P(BOTH),
            P(BOTH),
            P(DP, None),
            P(DP, None),
            P(BOTH, None),
        ),
        out_specs=(
            P(BOTH, None),
            P(BOTH, None),
            P(DP, HEAD),
            P(DP, HEAD),
            P(DP, HEAD),
            P(BOTH, None),
            P(BOTH),
            P(BOTH),
            P(None, BOTH),
            P(BOTH, None),
            P(BOTH),
            P(BOTH),
        ),
        check_vma=False,
    )
```

```python
import functools
import math
import types

import jax
import jax.numpy as jnp
from jax import lax
from jax.experimental import pallas as pl
from jax.experimental.pallas import tpu as pltpu
from jax.sharding import PartitionSpec as P

HD = 64
BIN = 512
EPS = 1e-12
F32 = jnp.float32
BF = jnp.bfloat16
MESH = pl.DeviceIdType.MESH

MU, MV = 2, 1
ROWS = {"Q": 48, "O": 48, "U": 96, "D": 96}
COLS = {"Q": 1152, "O": 384, "U": 768, "D": 768}
APART = {"Q": 32, "O": 32, "U": 64, "D": 64}
PIECES = ("Q", "O", "U", "D")
PER_PIECE = ("G", "S1", "R1", "S2A", "R2A", "S3A", "R3A", "S2C", "R2C", "S3C", "R3C")
DP, HEAD = "dp", "head"
BOTH = (DP, HEAD)
SENT, RECEIVED = 52, 140


def mm(a, b, ca=1, cb=0):
    return lax.dot_general(a, b, (((ca,), (cb,)), ((), ())), preferred_element_type=F32)


def scratch_list():
    items = []
    for name, shape, dtype in MOVED_IN + MOVED_OUT:
        items.append((name, pltpu.VMEM(shape, dtype)))

    def add(name, shape, dtype):
        items.append((name, pltpu.VMEM(shape, dtype)))

    add("X", (512, 768), BF)
    add("WQ", (768, 1152), BF)
    add("WOP", (2, 768, 384), BF)
    add("WO", (768, 768), BF)
    add("WU", (1536, 768), BF)
    add("WD", (1536, 768), BF)
    for n in ("Q3", "K3", "V3", "ATT", "GA", "DQ", "DK", "DV"):
        add(n, (3, 512, 128), BF)
    add("ATTR", (3, 256, 128), BF)
    add("GAS", (3, 256, 128), BF)
    add("BIAS", (512, 512), F32)
    add("LIVE", (512, 128), F32)
    add("P32", (6, 512, 512), F32)
    add("PB", (512, 512), BF)
    add("DSB", (512, 512), BF)
    add("U1", (256, 768), F32)
    add("N1", (256, 768), F32)
    add("INV1", (256, 128), F32)
    add("FIN", (512, 768), BF)
    add("HID", (4, 512, 384), BF)
    add("GEL", (4, 512, 384), F32)
    add("SEC", (512, 768), F32)
    add("SECR", (256, 768), F32)
    add("GS", (256, 768), F32)
    add("GFB", (512, 768), BF)
    add("GB", (256, 768), BF)
    add("IGS", (256, 768), BF)
    add("IGR", (256, 768), BF)
    add("T", (768, 1152), F32)
    add("S0", (768, 384), BF)
    add("R0", (768, 384), BF)
    for p in PIECES:
        r, c, a = ROWS[p], COLS[p], APART[p]
        b = r - a
        sizes = (8 * r, 8 * r, 8 * r, 4 * a, 4 * a, 3 * a, 3 * a, 6 * b, 6 * b, b, b)
        for key, size in zip(PER_PIECE, sizes):
            add(key + p, (size, c), F32 if key == "G" else BF)
    add("VS", (96, 768), F32)
    add("VR", (96, 768), F32)
    items.append(("ss", pltpu.SemaphoreType.DMA((SENT,))))
    items.append(("rs", pltpu.SemaphoreType.DMA((RECEIVED,))))
    items.append(("ls", pltpu.SemaphoreType.DMA((1 + len(MOVED_IN) + len(MOVED_OUT),))))
    return items


IN_NAMES = ("tok", "wq", "wk", "wv", "wo", "ga", "ba", "wu", "wd", "gf", "bf", "len", "off", "og")
MOVED_IN = (
    ("wq", (48, 384), F32),
    ("wk", (48, 384), F32),
    ("wv", (48, 384), F32),
    ("ga", (24,), F32),
    ("ba", (24,), F32),
    ("gf", (24,), F32),
    ("bf", (24,), F32),
    ("tok", (256, 768), BF),
    ("wo", (24, 768), F32),
    ("wu", (96, 768), F32),
    ("wd", (96, 768), F32),
    ("og", (256, 768), BF),
)
MOVED_OUT = (
    ("out", (256, 768), BF),
    ("ig", (256, 768), BF),
    ("dwq", (48, 384), F32),
    ("dwk", (48, 384), F32),
    ("dwv", (48, 384), F32),
    ("dwo", (24, 768), F32),
    ("dga", (24,), F32),
    ("dba", (24,), F32),
    ("dwu", (96, 768), F32),
    ("dwd", (96, 768), F32),
    ("dgf", (24,), F32),
    ("dbf", (24,), F32),
)
OUT_NAMES = ("out", "ig", "dwq", "dwk", "dwv", "dwo", "dga", "dba", "dwu", "dwd", "dgf", "dbf")


def layer_kernel(*refs):
    ins = tuple(n if n in ("len", "off") else "far_" + n for n in IN_NAMES)
    outs = tuple("far_" + n for n in OUT_NAMES)
    names = ins + outs + tuple(n for n, _ in scratch_list())
    named = dict(zip(names, refs))
    r = types.SimpleNamespace(**named)
    for key in PER_PIECE:
        setattr(r, key, {p: named[key + p] for p in PIECES})
    me = lax.axis_index(DP)
    c = lax.axis_index(HEAD)
    x = lax.rem(me, 2)
    y = lax.rem(lax.div(me, 2), 2)
    z = lax.div(me, 4)
    u = x + c * (y - x)
    v = y + c * (x - y)
    ub = 1 + c
    vb = 2 - c
    zs = (z, z + 1 - 2 * lax.rem(z, 2), lax.rem(z + 2, 4), 3 - z)

    def chip(m):
        zm, du, dv = m // 4, (m // 2) % 2, m % 2
        uu = 1 - u if du else u
        vv = 1 - v if dv else v
        return 4 * zs[zm] + ub * uu + vb * vv

    ids = [chip(m) for m in range(16)]
    partner = (me, 1 - c)
    base256, base24, other24 = 256 * c, 24 * c, 24 * (1 - c)
    own_rows = pl.ds(pl.multiple_of(256 * c, 256), 256)
    oth_rows = pl.ds(pl.multiple_of(256 * (1 - c), 256), 256)

    in_copies, out_copies = {}, []
    for k, (n, _, _) in enumerate(MOVED_IN):
        in_copies[n] = pltpu.make_async_copy(named["far_" + n], named[n], r.ls.at[1 + k])
        in_copies[n].start()

    def arrived(*keys):
        for n in keys:
            in_copies[n].wait()

    def put(*keys):
        for n in keys:
            k = 1 + len(MOVED_IN) + OUT_NAMES.index(n)
            cp = pltpu.make_async_copy(named[n], named["far_" + n], r.ls.at[k])
            cp.start()
            out_copies.append(cp)

    peers = [partner] + [(ids[m], c) for m in (MU, MV, 4, 8, 12)]
    barrier = pltpu.get_barrier_semaphore()
    for dev in peers:
        pl.semaphore_signal(barrier, inc=1, device_id=dev, device_id_type=MESH)
    pl.semaphore_wait(barrier, len(peers))

    sends = []
    send_ids, recv_ids = {}, {}

    def sem_of(sems, ids_of, name):
        return sems.at[ids_of.setdefault(name, len(ids_of))]

    def send(key, src, dst, dev, out_group=None, in_group=None):
        out = out_group or ("one", len(sends))
        cp = pltpu.make_async_remote_copy(
            src_ref=src,
            dst_ref=dst,
            send_sem=sem_of(r.ss, send_ids, out),
            recv_sem=sem_of(r.rs, recv_ids, in_group or key),
            device_id=dev,
            device_id_type=MESH,
        )
        cp.start()
        sends.append((src, out, key))

    def wait_send(out, ref):
        pltpu.make_async_remote_copy(
            src_ref=ref,
            dst_ref=ref,
            send_sem=sem_of(r.ss, send_ids, out),
            recv_sem=r.rs.at[0],
            device_id=partner,
            device_id_type=MESH,
        ).wait_send()

    waited = set()

    def wait_sent(key):
        for src, out, k in sends:
            if k == key:
                wait_send(out, src)
                waited.add(out)

    def wait_recv(key, ref):
        pltpu.make_async_remote_copy(
            src_ref=ref,
            dst_ref=ref,
            send_sem=r.ss.at[0],
            recv_sem=sem_of(r.rs, recv_ids, key),
            device_id=partner,
            device_id_type=MESH,
        ).wait_recv()

    def wbuf(p):
        return {"Q": r.WQ, "O": r.WOP.at[c], "U": r.WU, "D": r.WD}[p]

    starts = {}
    for n_rows in (48, 96):
        for m in range(16):
            first = pl.multiple_of(ids[m] * n_rows, 16)
            third = pl.multiple_of(ids[m] * n_rows + 2 * n_rows // 3, 16)
            starts[n_rows, m] = (first, third)

    def wslice(p, part, m):
        a, rows = APART[p], ROWS[p]
        first, third = starts[rows, m]
        if part == "A":
            return wbuf(p).at[pl.ds(first, a), :]
        return wbuf(p).at[pl.ds(third, rows - a), :]

    def forward(p, part, m, f):
        ref = wslice(p, part, m)
        last = ("plane", p, m // 4) if f == MV else None
        send(("ag", p, part, m ^ f), ref, ref, (ids[f], c), ("ag", p, part), last)

    def got(p, part, m):
        wait_recv(("ag", p, part, m), wslice(p, part, m))

    def ag_own(p):
        forward(p, "C", 0, MU)
        for f in (4, 8, 12):
            forward(p, "A", 0, f)
        forward(p, "A", 0, MU)
        forward(p, "A", 0, MV)
        for f in (4, 8, 12):
            forward(p, "C", 0, f)
        forward(p, "C", 0, MV)

    def ag_steps(p):
        steps = []

        def step(part, m, flips):
            def run():
                got(p, part, m)
                for f in flips:
                    forward(p, part, m, f)

            steps.append(run)

        step("C", MU, (4, 8, 12, MV))
        step("A", MU, (MV,))
        for zz in (4, 8, 12):
            step("A", zz, (MU, MV))
        for zz in (4, 8, 12):
            step("C", zz, (MV,))
            step("C", zz + MU, (MV,))
        for zz in (4, 8, 12):
            step("A", zz + MU, (MV,))
        return steps

    def ag_plane(p, zm):
        wait_recv(("plane", p, zm), wbuf(p).at[pl.ds(0, 2 * ROWS[p]), :])

    def run(steps):
        for s in steps:
            s()

    flip_u, flip_v = ((ids[MU], c),), ((ids[MV], c),)
    line = tuple((ids[m], c) for m in (4, 8, 12))
    vec_peers = ((line, flip_v, flip_u, (partner,)), ((partner,), flip_v, flip_u, line))

    def vec_slots(k, s):
        first = 48 * k + 8 * (s + (2 if k == 0 and s else 0))
        return [pl.ds(first + 8 * j, 8) for j in range(len(vec_peers[k][s]))]

    def vec_send(k, s):
        for j, (slot, dev) in enumerate(zip(vec_slots(k, s), vec_peers[k][s])):
            send(("v", k, s, j), r.VS.at[pl.ds(48 * k + 8 * s, 8), :], r.VR.at[slot, :], dev)

    def vec_step(k, s):
        total = r.VS[pl.ds(48 * k + 8 * s, 8), :]
        for j, slot in enumerate(vec_slots(k, s)):
            wait_recv(("v", k, s, j), r.VR.at[slot, :])
            total = total + r.VR[slot, :]
        r.VS[pl.ds(48 * k + (8 * s + 8 if s < 3 else 40), 8), :] = total
        if s < 3:
            vec_send(k, s + 1)

    def rs1_send(p, zm):
        rows = 2 * ROWS[p]
        s = pl.ds(zm * rows, rows)
        send(("r1", p, zm), r.S1[p].at[s, :], r.R1[p].at[s, :], (ids[MV], c), ("S1", p))

    def rs_sum1(p, zm):
        rows, a = ROWS[p], APART[p]
        b = rows - a
        g, r1 = r.G[p], r.R1[p]
        s = pl.ds(zm * 2 * rows, 2 * rows)
        wait_recv(("r1", p, zm), r1.at[s, :])
        for du in (1, 0):
            o = (2 * zm + du) * rows
            top = g[o : o + a, :] + r1[o : o + a, :].astype(F32)
            low = g[o + a : o + rows, :] + r1[o + a : o + rows, :].astype(F32)
            if du == 1:
                q = pl.ds(zm * a, a)
                r.S2A[p][q, :] = top.astype(BF)
                send(("r2a", p, zm), r.S2A[p].at[q, :], r.R2A[p].at[q, :], (ids[MU], c), ("S2A", p))
            else:
                g[o : o + a, :] = top
            if zm:
                q = pl.ds(((zm - 1) * 2 + du) * b, b)
                r.S2C[p][q, :] = low.astype(BF)
            else:
                g[o + a : o + rows, :] = low
        if zm:
            q = pl.ds((zm - 1) * 2 * b, 2 * b)
            send(("r2c", p), r.S2C[p].at[q, :], r.R2C[p].at[q, :], (ids[4 * zm], c), ("S2C", p))

    def rs_sum2a(p, zm):
        rows, a = ROWS[p], APART[p]
        g, r2 = r.G[p], r.R2A[p]
        q = pl.ds(zm * a, a)
        wait_recv(("r2a", p, zm), r2.at[q, :])
        o = 2 * zm * rows
        val = g[o : o + a, :] + r2[q, :].astype(F32)
        if zm:
            k = pl.ds((zm - 1) * a, a)
            r.S3A[p][k, :] = val.astype(BF)
            send(("r3a", p), r.S3A[p].at[k, :], r.R3A[p].at[k, :], (ids[4 * zm], c), ("S3A", p))
        else:
            g[o : o + a, :] = val

    def rs_sum2c(p):
        rows, a = ROWS[p], APART[p]
        b = rows - a
        g, r2 = r.G[p], r.R2C[p]
        wait_recv(("r2c", p), r2)
        for du in (1, 0):
            o = du * rows + a
            val = g[o : o + b, :]
            for zm in (1, 2, 3):
                k = ((zm - 1) * 2 + du) * b
                val = val + r2[k : k + b, :].astype(F32)
            if du == 1:
                r.S3C[p][...] = val.astype(BF)
                send(("r3c", p), r.S3C[p], r.R3C[p], (ids[MU], c))
            else:
                g[o : o + b, :] = val

    def rs_final(p):
        rows, a = ROWS[p], APART[p]
        g = r.G[p]
        r3a, r3c = r.R3A[p], r.R3C[p]
        wait_recv(("r3a", p), r3a)
        val = g[0:a, :]
        for zm in (1, 2, 3):
            val = val + r3a[(zm - 1) * a : zm * a, :].astype(F32)
        g[0:a, :] = val
        wait_recv(("r3c", p), r3c)
        g[a:rows, :] = g[a:rows, :] + r3c[...].astype(F32)

    def block_row(zm, du, dv):
        uu = 1 - u if du else u
        vv = 1 - v if dv else v
        return ub * uu + vb * vv

    def stage(p, zm, src, base):
        rows, cols = ROWS[p], COLS[p]
        for du in (1, 0):
            k = (2 * zm + du) * rows
            far = pl.ds(pl.multiple_of(base + block_row(zm, du, 1) * rows, 8), rows)
            near = pl.ds(pl.multiple_of(base + block_row(zm, du, 0) * rows, 8), rows)
            r.S1[p][k : k + rows, :] = src[far, 0:cols].astype(BF)
            r.G[p][k : k + rows, :] = src[near, 0:cols]

    flat = 2 * me + c
    arrived("wq", "wk", "wv")
    r.WQ[pl.ds(pl.multiple_of(me * 48, 16), 48), 0:384] = r.wq[...].astype(BF)
    r.WQ[pl.ds(pl.multiple_of(me * 48, 16), 48), 384:768] = r.wk[...].astype(BF)
    r.WQ[pl.ds(pl.multiple_of(me * 48, 16), 48), 768:1152] = r.wv[...].astype(BF)
    ag_own("Q")
    arrived("tok")
    send("tok", r.tok, r.X.at[own_rows, :], partner)
    local = pltpu.make_async_copy(r.tok, r.X.at[own_rows, :], r.ls.at[0])
    local.start()
    arrived("ga", "ba", "gf", "bf")
    r.VS[0:8, :] = jnp.zeros((8, 768), F32)
    for k, n in enumerate(("ga", "ba", "gf", "bf")):
        r.VS[k : k + 1, 0:24] = getattr(r, n)[...].reshape(1, 24).astype(BF).astype(F32)
    r.VS[0:8, :] = pltpu.roll(r.VS[0:8, :], 24 * flat, 1)
    vec_send(0, 0)
    arrived("wo")
    wo = r.wo[...]
    r.WOP[c, pl.ds(pl.multiple_of(me * 48, 16), 48), :] = jnp.concatenate(
        [wo[:, 0:384], wo[:, 384:768]], axis=0
    ).astype(BF)
    arrived("wu", "wd", "og")
    r.WU[pl.ds(pl.multiple_of(me * 96, 16), 96), :] = r.wu[...].astype(BF)
    r.WD[pl.ds(pl.multiple_of(me * 96, 16), 96), :] = r.wd[...].astype(BF)

    q_steps, o_steps, u_steps, d_steps = (ag_steps(p) for p in PIECES)
    run(q_steps[:5])
    ag_own("O")
    run(o_steps[:1])

    col_pos = lax.broadcasted_iota(jnp.int32, (512, 128), 0)
    row_pos = lax.broadcasted_iota(jnp.int32, (8, 512), 1)
    col_lab = jnp.zeros((512, 128), jnp.int32)
    row_lab = jnp.zeros((8, 512), jnp.int32)
    for j in range(8):
        lo = r.off[0, j]
        hi = lo + r.len[0, j]
        col_lab = jnp.where((col_pos >= lo) & (col_pos < hi), j + 1, col_lab)
        row_lab = jnp.where((row_pos >= lo) & (row_pos < hi), j + 1, row_lab)
    r.LIVE[...] = jnp.where(col_lab > 0, 1.0, 0.0).astype(F32)
    row_lab = jnp.where(row_lab > 0, row_lab, -1)
    for t in range(4):
        q = slice(128 * t, 128 * t + 128)
        lab = jnp.concatenate([col_lab[q]] * 4, axis=1)
        same = lab == jnp.broadcast_to(row_lab[0:1], (128, 512))
        r.BIAS[q, :] = jnp.where(same, 0.0, -1e30).astype(F32)

    run(q_steps[5:])
    vec_step(0, 0)
    run(o_steps[1:5])
    ag_own("U")
    wait_recv("tok", r.X.at[own_rows, :])
    local.wait()
    for zm in range(4):
        ag_plane("Q", zm)

    for k, n in enumerate(("Q3", "K3", "V3")):
        full = mm(r.X[...], r.WQ[:, 384 * k : 384 * k + 384])
        full = full.astype(BF)
        if k == 0:
            full = full * BF(0.125)
        for i in range(3):
            getattr(r, n)[i] = full[:, 128 * i : 128 * i + 128]
    run(u_steps[:1])
    vec_step(0, 1)

    for i in range(3):
        r.ATT[i] = jnp.zeros((512, 128), BF)
    fw_hooks = [
        o_steps[5:8],
        o_steps[8:],
        [functools.partial(vec_step, 0, 2)] + u_steps[1:3],
        u_steps[3:5],
        u_steps[5:8],
        u_steps[8:10],
    ]
    lane = lax.broadcasted_iota(jnp.int32, (1, 128), 1)

    def half(val, a):
        keep = (lane >= 64 * a) & (lane < 64 * a + 64)
        return jnp.where(keep, val, jnp.zeros_like(val))

    def at_index(h, hooks):
        for k, steps in enumerate(hooks):

            def go(steps=steps):
                run(steps)

            pl.when(h == k)(go)

    def fwd_head(h, carry):
        at_index(h, fw_hooks)
        i = lax.div(h, 2)
        a = lax.rem(h, 2)
        vals = half(r.V3[i], a)
        keys = half(r.K3[i], a)
        for t in range(4):
            q = slice(128 * t, 128 * t + 128)
            s = mm(r.Q3[i, q, :], keys, 1, 1) + r.BIAS[q, :]
            live = r.LIVE[q, 0:1]
            top = jnp.where(live > 0, jnp.max(s, axis=1, keepdims=True), 0.0)
            w = jnp.exp(s - top)
            total = jnp.sum(w, axis=1, keepdims=True) + (1.0 - live)
            prob = w * (1.0 / total)
            r.P32[h, q, :] = prob
            o = mm(prob.astype(BF), vals)
            r.ATT[i, q, :] = r.ATT[i, q, :] + o.astype(BF)
        return carry

    lax.fori_loop(0, 6, fwd_head, 0)

    send("att", r.ATT.at[:, oth_rows, :], r.ATTR, partner)
    ag_own("D")
    for zm in range(4):
        ag_plane("O", zm)
    send("wop", r.WOP.at[c], r.WOP.at[c], partner)
    run(d_steps[:1] + u_steps[10:12])
    vec_step(0, 3)
    wait_recv("wop", r.WOP.at[1 - c])

    def build_out(i, carry):
        for k in range(2):
            blk = r.WOP[k, pl.ds(pl.multiple_of(48 * i, 16), 48), :].astype(F32)
            rows = jnp.concatenate([blk[0:24], blk[24:48]], axis=1)
            r.T[pl.ds(pl.multiple_of(48 * i + 24 * k, 8), 24), 0:768] = rows
        return carry

    lax.fori_loop(0, 16, build_out, 0)
    r.WO[...] = r.T[:, 0:768].astype(BF)
    wait_recv("att", r.ATTR)
    own_heads = pl.ds(pl.multiple_of(384 * c, 128), 384)
    oth_heads = pl.ds(pl.multiple_of(384 * (1 - c), 128), 384)

    def joined(ref, rows):
        return jnp.concatenate([ref[i, rows, :] for i in range(3)], axis=1)

    all256 = pl.ds(0, 256)
    branch = mm(joined(r.ATT, own_rows), r.WO[own_heads, :])
    branch = branch + mm(joined(r.ATTR, all256), r.WO[oth_heads, :])
    r.GS[...] = branch
    run(u_steps[12:] + d_steps[1:2])

    def norm(val):
        mean = jnp.mean(val, axis=1, keepdims=True)
        cen = val - mean
        inv = lax.rsqrt(jnp.mean(cen * cen, axis=1, keepdims=True) + EPS)
        return cen * inv, inv

    def ln1(t, carry):
        q = pl.ds(pl.multiple_of(64 * t, 64), 64)
        unit, inv = norm(r.tok[q, :].astype(F32) + r.GS[q, :])
        r.U1[q, :] = unit
        r.INV1[q, :] = jnp.broadcast_to(inv, (64, 128))
        one = unit * r.VS[40:41, :] + r.VS[41:42, :]
        r.N1[q, :] = one
        r.FIN[pl.ds(pl.multiple_of(base256 + 64 * t, 64), 64), :] = one.astype(BF)
        return carry

    lax.fori_loop(0, 4, ln1, 0)
    send("fin", r.FIN.at[own_rows, :], r.FIN.at[own_rows, :], partner)
    run(d_steps[2:5])
    wait_recv("fin", r.FIN.at[oth_rows, :])

    def plane_rows(zm):
        return pl.ds(pl.multiple_of(384 * zs[zm], 128), 384)

    def ffn_up(zm):
        for t in range(2):
            q = slice(256 * t, 256 * t + 256)
            pre = mm(r.FIN[q, :], r.WU[plane_rows(zm), :], 1, 1)
            r.GEL[zm, q, :] = pre

        def act(t, carry):
            q = pl.ds(pl.multiple_of(64 * t, 64), 64)
            pre = r.GEL[zm, q, :]
            cdf = 0.5 * (1.0 + lax.erf(pre * (2.0**-0.5)))
            pdf = jnp.exp(-0.5 * pre * pre) * (1.0 / math.sqrt(2.0 * math.pi))
            r.HID[zm, q, :] = (pre * cdf).astype(BF)
            r.GEL[zm, q, :] = cdf + pre * pdf
            return carry

        lax.fori_loop(0, 8, act, 0)

    d_groups = ([], d_steps[5:8], d_steps[8:11], d_steps[11:])
    for zm in range(4):
        ag_plane("U", zm)
        run(d_groups[zm])
        ffn_up(zm)
    for zm in range(4):
        ag_plane("D", zm)
        for rows in (oth_rows, own_rows):
            part = mm(r.HID[zm, rows, :], r.WD[plane_rows(zm), :])
            if zm:
                part = part + r.SEC[rows, :]
            r.SEC[rows, :] = part
            if zm == 3 and rows is oth_rows:
                for h in range(2):
                    part_rows = pl.ds(pl.multiple_of(256 * (1 - c) + 128 * h, 128), 128)
                    send(("sec", h), r.SEC.at[part_rows, :], r.SECR.at[pl.ds(128 * h, 128), :], partner)

    def ln2(t, sums):
        dg, db = sums
        q = pl.ds(pl.multiple_of(64 * t, 64), 64)
        qq = pl.ds(pl.multiple_of(base256 + 64 * t, 64), 64)
        unit, inv = norm(r.N1[q, :] + (r.SEC[qq, :] + r.SECR[q, :]))
        gain = r.VS[42:43, :]
        r.out[q, :] = (unit * gain + r.VS[43:44, :]).astype(BF)
        e = r.og[q, :].astype(F32)
        dg = dg + jnp.sum(e * unit, axis=0, keepdims=True)
        db = db + jnp.sum(e, axis=0, keepdims=True)
        eg = e * gain
        inner = jnp.mean(eg * unit, axis=1, keepdims=True)
        gs = inv * (eg - jnp.mean(eg, axis=1, keepdims=True) - unit * inner)
        r.GS[q, :] = gs
        r.GFB[qq, :] = gs.astype(BF)
        return dg, db

    zero = jnp.zeros((1, 768), F32)
    dg2, db2 = zero, zero
    for h in range(2):
        wait_recv(("sec", h), r.SECR.at[pl.ds(128 * h, 128), :])
        dg2, db2 = lax.fori_loop(2 * h, 2 * h + 2, ln2, (dg2, db2))
        part_rows = r.GFB.at[pl.ds(pl.multiple_of(base256 + 128 * h, 128), 128), :]
        send(("gfb", h), part_rows, part_rows, partner)
    put("out")
    r.T[0:384, 0:768] = mm(r.HID[3, own_rows, :], r.GFB[own_rows, :], 0, 0)
    for h in range(2):
        wait_recv(("gfb", h), r.GFB.at[pl.ds(pl.multiple_of(256 * (1 - c) + 128 * h, 128), 128), :])
    for h in range(2):
        wait_sent(("sec", h))

    for n_done, zm in enumerate((3, 2, 1, 0)):
        if zm == 3:
            r.T[0:384, 0:768] = r.T[0:384, 0:768] + mm(r.HID[3, oth_rows, :], r.GFB[oth_rows, :], 0, 0)
        else:
            r.T[0:384, 0:768] = mm(r.HID[zm], r.GFB[...], 0, 0)
        stage("D", zm, r.T, 0)
        if zm > 1:
            rs1_send("D", zm)
        for t in range(2):
            q = slice(256 * t, 256 * t + 256)
            gh = mm(r.GFB[q, :], r.WD[plane_rows(zm), :], 1, 1)
            r.HID[zm, q, :] = (gh * r.GEL[zm, q, :]).astype(BF)
        r.T[384:768, 0:768] = mm(r.HID[zm], r.FIN[...], 0, 0)
        stage("U", zm, r.T, 384)
        if zm > 1:
            rs1_send("U", zm)
        for rows in (oth_rows, own_rows):
            part = mm(r.HID[zm, rows, :], r.WU[plane_rows(zm), :])
            if n_done:
                part = part + r.SEC[rows, :]
            r.SEC[rows, :] = part
            if n_done == 3 and rows is oth_rows:
                send("gn", r.SEC.at[oth_rows, :], r.SECR, partner)
        if n_done == 2:
            rs_sum1("D", 3)
    rs_sum1("U", 3)
    rs1_send("D", 1)
    wait_recv("gn", r.SECR)

    def ln1_back(t, sums):
        dg, db = sums
        q = pl.ds(pl.multiple_of(64 * t, 64), 64)
        qq = pl.ds(pl.multiple_of(base256 + 64 * t, 64), 64)
        e = r.GS[q, :] + (r.SEC[qq, :] + r.SECR[q, :])
        unit = r.U1[q, :]
        inv = r.INV1[q, 0:1]
        dg = dg + jnp.sum(e * unit, axis=0, keepdims=True)
        db = db + jnp.sum(e, axis=0, keepdims=True)
        eg = e * r.VS[40:41, :]
        inner = jnp.mean(eg * unit, axis=1, keepdims=True)
        first = inv * (eg - jnp.mean(eg, axis=1, keepdims=True) - unit * inner)
        r.GS[q, :] = first
        r.GB[q, :] = first.astype(BF)
        return dg, db

    dg1, db1 = lax.fori_loop(0, 4, ln1_back, (zero, zero))
    r.VS[48:56, :] = jnp.zeros((8, 768), F32)
    for k, val in enumerate((dg1, db1, dg2, db2)):
        r.VS[48 + k : 49 + k, :] = val
    vec_send(1, 0)

    gview = mm(r.GB[...], r.WO[oth_heads, :], 1, 1).astype(BF)
    for i in range(3):
        r.GAS[i] = gview[:, 128 * i : 128 * i + 128]
    send("gas", r.GAS, r.GA.at[:, own_rows, :], partner)
    gview = mm(r.GB[...], r.WO[own_heads, :], 1, 1).astype(BF)
    for i in range(3):
        r.GA[i, own_rows, :] = gview[:, 128 * i : 128 * i + 128]
    vec_step(1, 0)
    rs_sum2a("D", 3)
    rs1_send("U", 1)
    r.T[own_heads, 0:768] = mm(joined(r.ATT, own_rows), r.GB[...], 0, 0)
    r.T[oth_heads, 0:768] = mm(joined(r.ATTR, all256), r.GB[...], 0, 0)

    def pair_out(i, carry):
        q = pl.ds(pl.multiple_of(48 * i, 16), 48)
        blk = r.T[pl.ds(pl.multiple_of(48 * i + other24, 8), 24), 0:768]
        r.S0[q, :] = jnp.concatenate([blk[:, 0:384], blk[:, 384:768]], axis=0).astype(BF)
        return carry

    lax.fori_loop(0, 16, pair_out, 0)
    send("s0", r.S0, r.R0, partner)
    rs_sum1("D", 2)
    rs_sum2a("U", 3)
    wait_recv("s0", r.R0)

    def out_block(m):
        i = ids[m]
        blk = r.T[pl.ds(pl.multiple_of(48 * i + base24, 8), 24), 0:768]
        blk = jnp.concatenate([blk[:, 0:384], blk[:, 384:768]], axis=0)
        return blk + r.R0[pl.ds(pl.multiple_of(48 * i, 16), 48), :].astype(F32)

    for zm in (3, 2, 1, 0):
        for du in (1, 0):
            k = (2 * zm + du) * 48
            r.S1["O"][k : k + 48, :] = out_block(4 * zm + 2 * du + 1).astype(BF)
            r.G["O"][k : k + 48, :] = out_block(4 * zm + 2 * du)
        if zm > 1:
            rs1_send("O", zm)

    wait_recv("gas", r.GA.at[:, oth_rows, :])
    for n in ("DQ", "DK", "DV"):
        for i in range(3):
            getattr(r, n)[i] = jnp.zeros((512, 128), BF)

    def s1(p, zm):
        return functools.partial(rs_sum1, p, zm)

    def s2a(p, zm):
        return functools.partial(rs_sum2a, p, zm)

    def s2c(p):
        return functools.partial(rs_sum2c, p)

    def vs(s):
        return functools.partial(vec_step, 1, s)

    bw_hooks = [
        [],
        [s1("U", 2)],
        [s2a("D", 2)],
        [],
        [s1("D", 1)],
        [s2a("U", 2), vs(1)],
    ]

    def bwd_head(h, carry):
        at_index(h, bw_hooks)
        i = lax.div(h, 2)
        a = lax.rem(h, 2)
        go = half(r.GA[i], a)
        for t in range(4):
            q = slice(128 * t, 128 * t + 128)
            prob = r.P32[h, q, :]
            dp = mm(go[q], r.V3[i], 1, 1)
            delta = jnp.sum(prob * dp, axis=1, keepdims=True)
            r.DSB[q, :] = (prob * (dp - delta)).astype(BF)
            r.PB[q, :] = prob.astype(BF)
        r.DV[i] = r.DV[i] + mm(r.PB[...], go, 0, 0).astype(BF)
        dq = mm(r.DSB[...], half(r.K3[i], a)) * 0.125
        r.DQ[i] = r.DQ[i] + dq.astype(BF)
        dk = mm(r.DSB[...], half(r.Q3[i], a), 0, 0)
        r.DK[i] = r.DK[i] + dk.astype(BF)
        return carry

    lax.fori_loop(0, 6, bwd_head, 0)

    all512 = pl.ds(0, 512)
    for k, n in enumerate(("DQ", "DK", "DV")):
        r.T[:, 384 * k : 384 * k + 384] = mm(r.X[...], joined(getattr(r, n), all512), 0, 0)
    for zm in (3, 2, 1, 0):
        stage("Q", zm, r.T, 192 * zs[zm])
        if zm > 1:
            rs1_send("Q", zm)

    def s0(p, zm):
        return functools.partial(rs1_send, p, zm)

    run([s1("U", 1), s2a("D", 1), vs(2), s0("Q", 1), s0("O", 1)])

    for rows in (oth_rows, own_rows):
        acc = mm(joined(r.DQ, rows), r.WQ[:, 0:384], 1, 1)
        acc = acc + mm(joined(r.DK, rows), r.WQ[:, 384:768], 1, 1)
        acc = acc + mm(joined(r.DV, rows), r.WQ[:, 768:1152], 1, 1)
        if rows is oth_rows:
            r.IGS[...] = acc.astype(BF)
            send("ig", r.IGS, r.IGR, partner)
            run([s1("O", 3), s1("O", 2), s2a("U", 1), s2a("O", 3), s0("D", 0)])
        else:
            r.GS[...] = r.GS[...] + acc
    wait_recv("ig", r.IGR)
    r.ig[...] = (r.GS[...] + r.IGR[...].astype(F32)).astype(BF)
    put("ig")

    run([s1("Q", 3), s2a("O", 2), s0("U", 0), s1("Q", 2), s2a("Q", 3), s0("Q", 0)])
    run([s1("Q", 1), s2a("Q", 2), s1("O", 1), s2a("Q", 1), s1("D", 0), s2a("O", 1), s2c("D")])
    run([s1("U", 0), s2c("U"), s2a("D", 0), s0("O", 0), s1("Q", 0), s2c("Q"), s2a("U", 0)])
    run([s2a("Q", 0), s1("O", 0), s2c("O"), s2a("O", 0)])
    rs_final("Q")
    r.dwq[...] = r.G["Q"][0:48, 0:384]
    r.dwk[...] = r.G["Q"][0:48, 384:768]
    r.dwv[...] = r.G["Q"][0:48, 768:1152]
    rs_final("D")
    r.dwd[...] = r.G["D"][0:96, :]
    put("dwq", "dwk", "dwv", "dwd")
    rs_final("U")
    r.dwu[...] = r.G["U"][0:96, :]
    rs_final("O")
    vec_step(1, 3)
    go = r.G["O"][0:48, :]
    r.dwo[...] = jnp.concatenate([go[0:24], go[24:48]], axis=1)
    back = pltpu.roll(r.VS[88:96, :], lax.rem(768 - 24 * flat, 768), 1)
    for k, n in enumerate(("dga", "dba", "dgf", "dbf")):
        getattr(r, n)[...] = back[k, 0:24]
    put("dwu", "dwo", "dga", "dba", "dgf", "dbf")

    for src, out, key in sends:
        if out in waited:
            continue
        waited.add(out)
        if out[0] == "one":
            ref = src
        elif out[0] == "ag":
            count = sum(o == out for _, o, _ in sends)
            n_rows = APART[out[1]] if out[2] == "A" else ROWS[out[1]] - APART[out[1]]
            ref = wbuf(out[1]).at[pl.ds(0, count * n_rows), :]
        else:
            ref = getattr(r, out[0])[out[1]]
        wait_send(out, ref)
    assert len(send_ids) == SENT and len(recv_ids) == RECEIVED, (len(send_ids), len(recv_ids))
    for cp in out_copies:
        cp.wait()


def hand_over(*refs):
    half = len(refs) // 2
    for src, dst in zip(refs[:half], refs[half:]):
        dst[...] = src[...]


def layer_small(*args):
    shapes = tuple((shape, dtype) for _, shape, dtype in MOVED_OUT)
    vmem = pl.BlockSpec(memory_space=pltpu.VMEM)
    smem = pl.BlockSpec(memory_space=pltpu.SMEM)
    anywhere = pl.BlockSpec(memory_space=pl.ANY)
    out_shape = tuple(jax.ShapeDtypeStruct(s, d) for s, d in shapes)
    up = IN_NAMES.index("wu")
    args = args[:up] + (args[up].T,) + args[up + 1 :]
    outs = pl.pallas_call(
        layer_kernel,
        out_shape=out_shape,
        in_specs=[smem if n in ("len", "off") else anywhere for n in IN_NAMES],
        out_specs=tuple(anywhere for _ in shapes),
        scratch_shapes=[s for _, s in scratch_list()],
        compiler_params=pltpu.CompilerParams(
            collective_id=0, has_side_effects=True, vmem_limit_bytes=67043328
        ),
    )(*args)
    outs = pl.pallas_call(
        hand_over,
        out_shape=out_shape,
        in_specs=[vmem for _ in shapes],
        out_specs=tuple(vmem for _ in shapes),
    )(*outs)
    up = OUT_NAMES.index("dwu")
    return outs[:up] + (outs[up].T,) + outs[up + 1 :]


def labels_of(lengths, offsets):
    position = jnp.arange(BIN, dtype=jnp.int32)[:, None]
    starts = offsets[None, :]
    inside = (position >= starts) & (position < starts + lengths[None, :])
    slot_order = jnp.arange(1, lengths.shape[0] + 1, dtype=jnp.int32)[None, :]
    return jnp.sum(jnp.where(inside, slot_order, 0), axis=1)


def layer_norm(operand, gain_vec, bias_vec):
    row_mean = jnp.mean(operand, axis=-1, keepdims=True)
    centered = operand - row_mean
    inverse = lax.rsqrt(jnp.mean(centered * centered, axis=-1, keepdims=True) + EPS)
    normed = centered * inverse
    return (normed * gain_vec + bias_vec, normed, inverse)


def norm_back(grad_rows, normed, inverse, gain_vec):
    scaled = grad_rows * gain_vec
    inner = jnp.mean(scaled * normed, axis=-1, keepdims=True)
    return inverse * (scaled - jnp.mean(scaled, axis=-1, keepdims=True) - normed * inner)


def gelu_exact(operand):
    return jax.nn.gelu(operand, approximate=False)


def contract_rows(left, right):
    return lax.dot_general(
        left, right, (((0,), (0,)), ((), ())), preferred_element_type=F32
    )


def contract_cols(left, right):
    return lax.dot_general(
        left, right, (((1,), (1,)), ((), ())), preferred_element_type=F32
    )


def score_block(queries, key_rows, labels_bin, factor):
    scores = (
        jnp.einsum("qhd,khd->hqk", queries, key_rows, preferred_element_type=F32) * factor
    )
    allowed = ((labels_bin[:, None] == labels_bin[None, :]) & (labels_bin[:, None] > 0))[None]
    live_rows = (labels_bin > 0)[None, :, None]
    return (scores, allowed, live_rows)


def masked_exp(scores, allowed, row_top):
    return jnp.where(allowed, jnp.exp(jnp.where(allowed, scores - row_top, 0.0)), 0.0)


def attend_bin(pieces, factor):
    queries, key_rows, value_rows, labels_bin = pieces
    scores, allowed, live_rows = score_block(queries, key_rows, labels_bin, factor)
    row_top = jnp.max(jnp.where(allowed, scores, -1e30), axis=2, keepdims=True)
    row_top = jnp.where(live_rows, row_top, 0.0)
    weights = masked_exp(scores, allowed, row_top)
    denominator = jnp.sum(weights, axis=2, keepdims=True) + jnp.where(live_rows, 0.0, 1.0)
    probability = (weights / denominator).astype(jnp.bfloat16)
    mixed_rows = jnp.einsum(
        "hqk,khd->qhd", probability, value_rows, preferred_element_type=F32
    )
    return (mixed_rows.astype(jnp.bfloat16), row_top, denominator)


def attend_back(pieces, factor):
    queries, key_rows, value_rows, labels_bin, row_top, denominator, grad_mixed = pieces
    scores, allowed, live_rows = score_block(queries, key_rows, labels_bin, factor)
    probability = masked_exp(scores, allowed, row_top) / denominator
    grad_values = jnp.einsum(
        "hqk,qhd->khd",
        probability.astype(jnp.bfloat16),
        grad_mixed,
        preferred_element_type=F32,
    )
    grad_probs = jnp.einsum(
        "qhd,khd->hqk", grad_mixed, value_rows, preferred_element_type=F32
    )
    row_delta = jnp.sum(probability * grad_probs, axis=2, keepdims=True)
    grad_scores = (probability * (grad_probs - row_delta)).astype(jnp.bfloat16)
    grad_queries = (
        jnp.einsum("hqk,khd->qhd", grad_scores, key_rows, preferred_element_type=F32)
        * factor
    )
    grad_keys = (
        jnp.einsum("hqk,qhd->khd", grad_scores, queries, preferred_element_type=F32)
        * factor
    )
    return (
        grad_queries.astype(jnp.bfloat16),
        grad_keys.astype(jnp.bfloat16),
        grad_values.astype(jnp.bfloat16),
    )


def per_device(
    tokens,
    w_query,
    w_key,
    w_value,
    w_out,
    gain_attn,
    bias_attn,
    w_up,
    w_down,
    gain_ffn,
    bias_ffn,
    seq_lengths,
    seq_offsets,
    out_grad,
):
    low_type = jnp.bfloat16
    bin_count = seq_lengths.shape[0]
    group_rows = bin_count * BIN
    head_width = w_query.shape[1]
    local_heads = head_width // HD
    factor = 1.0 / math.sqrt(HD)
    labels = jax.vmap(labels_of)(seq_lengths, seq_offsets)
    full_query, full_key, full_value = (
        lax.all_gather(w_query.astype(low_type), DP, axis=0, tiled=True),
        lax.all_gather(w_key.astype(low_type), DP, axis=0, tiled=True),
        lax.all_gather(w_value.astype(low_type), DP, axis=0, tiled=True),
    )
    projection = jnp.concatenate([full_query, full_key, full_value], axis=1)
    whole_rows = lax.all_gather(tokens, HEAD, axis=0, tiled=True)
    projected = jnp.dot(whole_rows, projection, preferred_element_type=F32).astype(low_type)
    shape_bins = (bin_count, BIN, local_heads, HD)
    queries = projected[:, :head_width].reshape(shape_bins)
    key_rows = projected[:, head_width : 2 * head_width].reshape(shape_bins)
    value_rows = projected[:, 2 * head_width :].reshape(shape_bins)
    mixed_bins, row_tops, denominators = lax.map(
        lambda pieces: attend_bin(pieces, factor), (queries, key_rows, value_rows, labels)
    )
    attended = mixed_bins.reshape(group_rows, head_width)
    out_full, up_part, down_part, gain_one, bias_one, gain_two, bias_two = (
        lax.all_gather(w_out.astype(low_type), BOTH, axis=0, tiled=True),
        lax.all_gather(w_up.astype(low_type), BOTH, axis=1, tiled=True),
        lax.all_gather(w_down.astype(low_type), BOTH, axis=0, tiled=True),
        lax.all_gather(gain_attn.astype(low_type), BOTH, axis=0, tiled=True),
        lax.all_gather(bias_attn.astype(low_type), BOTH, axis=0, tiled=True),
        lax.all_gather(gain_ffn.astype(low_type), BOTH, axis=0, tiled=True),
        lax.all_gather(bias_ffn.astype(low_type), BOTH, axis=0, tiled=True),
    )
    gain_first = gain_one.astype(F32)
    gain_second = gain_two.astype(F32)
    token_view = lax.all_to_all(attended, HEAD, split_axis=0, concat_axis=1, tiled=True)
    first_sum = tokens.astype(F32) + jnp.dot(
        token_view, out_full, preferred_element_type=F32
    )
    normed_one, unit_one, inverse_one = layer_norm(
        first_sum, gain_first, bias_one.astype(F32)
    )
    ffn_input = normed_one.astype(low_type)
    pre_act = jnp.dot(ffn_input, up_part, preferred_element_type=F32)
    activated, gelu_pull = jax.vjp(gelu_exact, pre_act)
    hidden = activated.astype(low_type)
    second_sum = normed_one + jnp.dot(hidden, down_part, preferred_element_type=F32)
    result, unit_two, inverse_two = layer_norm(
        second_sum, gain_second, bias_two.astype(F32)
    )
    output = result.astype(low_type)
    grad_result = out_grad.astype(F32)
    grad_gain_two = jnp.sum(grad_result * unit_two, axis=0)
    grad_bias_two = jnp.sum(grad_result, axis=0)
    grad_second = norm_back(grad_result, unit_two, inverse_two, gain_second)
    grad_ffn = grad_second.astype(low_type)
    grad_down_part = contract_rows(hidden, grad_ffn)
    grad_pre = gelu_pull(contract_cols(grad_ffn, down_part))[0].astype(low_type)
    grad_up_part = contract_rows(ffn_input, grad_pre)
    grad_normed = grad_second + contract_cols(grad_pre, up_part)
    grad_gain_one = jnp.sum(grad_normed * unit_one, axis=0)
    grad_bias_one = jnp.sum(grad_normed, axis=0)
    grad_first = norm_back(grad_normed, unit_one, inverse_one, gain_first)
    grad_branch = grad_first.astype(low_type)
    grad_out_full = contract_rows(token_view, grad_branch)
    part_out, part_up, part_down, part_gain_one, part_bias_one, part_gain_two, part_bias_two = (
        lax.psum_scatter(grad_out_full, BOTH, scatter_dimension=0, tiled=True),
        lax.psum_scatter(grad_up_part, BOTH, scatter_dimension=1, tiled=True),
        lax.psum_scatter(grad_down_part, BOTH, scatter_dimension=0, tiled=True),
        lax.psum_scatter(grad_gain_one, BOTH, scatter_dimension=0, tiled=True),
        lax.psum_scatter(grad_bias_one, BOTH, scatter_dimension=0, tiled=True),
        lax.psum_scatter(grad_gain_two, BOTH, scatter_dimension=0, tiled=True),
        lax.psum_scatter(grad_bias_two, BOTH, scatter_dimension=0, tiled=True),
    )
    grad_token_view = contract_cols(grad_branch, out_full).astype(low_type)
    grad_attended = lax.all_to_all(grad_token_view, HEAD, split_axis=1, concat_axis=0, tiled=True)
    grad_bins = grad_attended.reshape(shape_bins)
    grad_queries, grad_keys, grad_values = lax.map(
        lambda pieces: attend_back(pieces, factor),
        (queries, key_rows, value_rows, labels, row_tops, denominators, grad_bins),
    )
    grad_projected = jnp.concatenate(
        [
            grad_queries.reshape(group_rows, head_width),
            grad_keys.reshape(group_rows, head_width),
            grad_values.reshape(group_rows, head_width),
        ],
        axis=1,
    )
    grad_projection = contract_rows(whole_rows, grad_projected)
    part_query, part_key, part_value = (
        lax.psum_scatter(grad_projection[:, :head_width], DP, scatter_dimension=0, tiled=True),
        lax.psum_scatter(
            grad_projection[:, head_width : 2 * head_width], DP, scatter_dimension=0, tiled=True
        ),
        lax.psum_scatter(
            grad_projection[:, 2 * head_width :], DP, scatter_dimension=0, tiled=True
        ),
    )
    input_grad = (
        grad_first
        + lax.psum_scatter(
            contract_cols(grad_projected, projection).astype(jnp.bfloat16),
            HEAD,
            scatter_dimension=0,
            tiled=True,
        ).astype(F32)
    ).astype(low_type)
    return (
        output,
        input_grad,
        part_query,
        part_key,
        part_value,
        part_out,
        part_gain_one,
        part_bias_one,
        part_up,
        part_down,
        part_gain_two,
        part_bias_two,
    )


def solution(mesh):
    small = mesh.shape[DP] == 16 and mesh.shape[HEAD] == 2
    return jax.shard_map(
        layer_small if small else per_device,
        mesh=mesh,
        in_specs=(
            P(BOTH, None),
            P(DP, HEAD),
            P(DP, HEAD),
            P(DP, HEAD),
            P(BOTH, None),
            P(BOTH),
            P(BOTH),
            P(None, BOTH),
            P(BOTH, None),
            P(BOTH),
            P(BOTH),
            P(DP, None),
            P(DP, None),
            P(BOTH, None),
        ),
        out_specs=(
            P(BOTH, None),
            P(BOTH, None),
            P(DP, HEAD),
            P(DP, HEAD),
            P(DP, HEAD),
            P(BOTH, None),
            P(BOTH),
            P(BOTH),
            P(None, BOTH),
            P(BOTH, None),
            P(BOTH),
            P(BOTH),
        ),
        check_vma=False,
    )
```

```python
import functools
import math
import types

import jax
import jax.numpy as jnp
from jax import lax
from jax.experimental import pallas as pl
from jax.experimental.pallas import tpu as pltpu
from jax.sharding import PartitionSpec as P

HD = 64
BIN = 512
EPS = 1e-12
F32 = jnp.float32
BF = jnp.bfloat16
MESH = pl.DeviceIdType.MESH

MU, MV = 2, 1
ROWS = {"Q": 48, "O": 48, "U": 96, "D": 96}
COLS = {"Q": 1152, "O": 384, "U": 768, "D": 768}
APART = {"Q": 32, "O": 32, "U": 64, "D": 64}
PIECES = ("Q", "O", "U", "D")
PER_PIECE = ("G", "S1", "R1", "S2A", "R2A", "S3A", "R3A", "S2C", "R2C", "S3C", "R3C")
DP, HEAD = "dp", "head"
BOTH = (DP, HEAD)
SENT, RECEIVED = 52, 140


def mm(a, b, ca=1, cb=0):
    return lax.dot_general(a, b, (((ca,), (cb,)), ((), ())), preferred_element_type=F32)


def scratch_list():
    items = []
    for name, shape, dtype in MOVED_IN + MOVED_OUT:
        items.append((name, pltpu.VMEM(shape, dtype)))

    def add(name, shape, dtype):
        items.append((name, pltpu.VMEM(shape, dtype)))

    add("X", (512, 768), BF)
    add("WQ", (768, 1152), BF)
    add("WOP", (2, 768, 384), BF)
    add("WO", (768, 768), BF)
    add("WU", (1536, 768), BF)
    add("WD", (1536, 768), BF)
    for n in ("Q3", "K3", "V3", "ATT", "GA", "DQ", "DK", "DV"):
        add(n, (3, 512, 128), BF)
    add("ATTR", (3, 256, 128), BF)
    add("GAS", (3, 256, 128), BF)
    add("BIAS", (512, 512), F32)
    add("LIVE", (512, 128), F32)
    add("P32", (6, 512, 512), F32)
    add("PB", (512, 512), BF)
    add("DSB", (512, 512), BF)
    add("U1", (256, 768), F32)
    add("N1", (256, 768), F32)
    add("INV1", (256, 128), F32)
    add("FIN", (512, 768), BF)
    add("HID", (4, 512, 384), BF)
    add("GEL", (4, 512, 384), F32)
    add("SEC", (512, 768), F32)
    add("SECR", (256, 768), F32)
    add("GS", (256, 768), F32)
    add("GFB", (512, 768), BF)
    add("GB", (256, 768), BF)
    add("IGS", (256, 768), BF)
    add("IGR", (256, 768), BF)
    add("T", (768, 1152), F32)
    add("S0", (768, 384), BF)
    add("R0", (768, 384), BF)
    for p in PIECES:
        r, c, a = ROWS[p], COLS[p], APART[p]
        b = r - a
        sizes = (8 * r, 8 * r, 8 * r, 4 * a, 4 * a, 3 * a, 3 * a, 6 * b, 6 * b, b, b)
        for key, size in zip(PER_PIECE, sizes):
            add(key + p, (size, c), F32 if key == "G" else BF)
    add("VS", (96, 768), F32)
    add("VR", (96, 768), F32)
    items.append(("ss", pltpu.SemaphoreType.DMA((SENT,))))
    items.append(("rs", pltpu.SemaphoreType.DMA((RECEIVED,))))
    items.append(("ls", pltpu.SemaphoreType.DMA((1 + len(MOVED_IN) + len(MOVED_OUT),))))
    return items


IN_NAMES = ("tok", "wq", "wk", "wv", "wo", "ga", "ba", "wu", "wd", "gf", "bf", "len", "off", "og")
MOVED_IN = (
    ("wq", (48, 384), F32),
    ("wk", (48, 384), F32),
    ("wv", (48, 384), F32),
    ("ga", (24,), F32),
    ("ba", (24,), F32),
    ("gf", (24,), F32),
    ("bf", (24,), F32),
    ("tok", (256, 768), BF),
    ("wo", (24, 768), F32),
    ("wu", (96, 768), F32),
    ("wd", (96, 768), F32),
    ("og", (256, 768), BF),
)
MOVED_OUT = (
    ("out", (256, 768), BF),
    ("ig", (256, 768), BF),
    ("dwq", (48, 384), F32),
    ("dwk", (48, 384), F32),
    ("dwv", (48, 384), F32),
    ("dwo", (24, 768), F32),
    ("dga", (24,), F32),
    ("dba", (24,), F32),
    ("dwu", (96, 768), F32),
    ("dwd", (96, 768), F32),
    ("dgf", (24,), F32),
    ("dbf", (24,), F32),
)
OUT_NAMES = ("out", "ig", "dwq", "dwk", "dwv", "dwo", "dga", "dba", "dwu", "dwd", "dgf", "dbf")


def layer_kernel(*refs):
    ins = tuple(n if n in ("len", "off") else "far_" + n for n in IN_NAMES)
    outs = tuple("far_" + n for n in OUT_NAMES)
    names = ins + outs + tuple(n for n, _ in scratch_list())
    named = dict(zip(names, refs))
    r = types.SimpleNamespace(**named)
    for key in PER_PIECE:
        setattr(r, key, {p: named[key + p] for p in PIECES})
    me = lax.axis_index(DP)
    c = lax.axis_index(HEAD)
    x = lax.rem(me, 2)
    y = lax.rem(lax.div(me, 2), 2)
    z = lax.div(me, 4)
    u = x + c * (y - x)
    v = y + c * (x - y)
    ub = 1 + c
    vb = 2 - c
    zs = (z, z + 1 - 2 * lax.rem(z, 2), lax.rem(z + 2, 4), 3 - z)

    def chip(m):
        zm, du, dv = m // 4, (m // 2) % 2, m % 2
        uu = 1 - u if du else u
        vv = 1 - v if dv else v
        return 4 * zs[zm] + ub * uu + vb * vv

    ids = [chip(m) for m in range(16)]
    partner = (me, 1 - c)
    base256, base24, other24 = 256 * c, 24 * c, 24 * (1 - c)
    own_rows = pl.ds(pl.multiple_of(256 * c, 256), 256)
    oth_rows = pl.ds(pl.multiple_of(256 * (1 - c), 256), 256)

    in_copies, out_copies = {}, []
    for k, (n, _, _) in enumerate(MOVED_IN):
        in_copies[n] = pltpu.make_async_copy(named["far_" + n], named[n], r.ls.at[1 + k])
        in_copies[n].start()

    def arrived(*keys):
        for n in keys:
            in_copies[n].wait()

    def put(*keys):
        for n in keys:
            k = 1 + len(MOVED_IN) + OUT_NAMES.index(n)
            cp = pltpu.make_async_copy(named[n], named["far_" + n], r.ls.at[k])
            cp.start()
            out_copies.append(cp)

    peers = [partner] + [(ids[m], c) for m in (MU, MV, 4, 8, 12)]
    barrier = pltpu.get_barrier_semaphore()
    for dev in peers:
        pl.semaphore_signal(barrier, inc=1, device_id=dev, device_id_type=MESH)
    pl.semaphore_wait(barrier, len(peers))

    sends = []
    send_ids, recv_ids = {}, {}

    def sem_of(sems, ids_of, name):
        return sems.at[ids_of.setdefault(name, len(ids_of))]

    def send(key, src, dst, dev, out_group=None, in_group=None):
        out = out_group or ("one", len(sends))
        cp = pltpu.make_async_remote_copy(
            src_ref=src,
            dst_ref=dst,
            send_sem=sem_of(r.ss, send_ids, out),
            recv_sem=sem_of(r.rs, recv_ids, in_group or key),
            device_id=dev,
            device_id_type=MESH,
        )
        cp.start()
        sends.append((src, out, key))

    def wait_send(out, ref):
        pltpu.make_async_remote_copy(
            src_ref=ref,
            dst_ref=ref,
            send_sem=sem_of(r.ss, send_ids, out),
            recv_sem=r.rs.at[0],
            device_id=partner,
            device_id_type=MESH,
        ).wait_send()

    waited = set()

    def wait_sent(key):
        for src, out, k in sends:
            if k == key:
                wait_send(out, src)
                waited.add(out)

    def wait_recv(key, ref):
        pltpu.make_async_remote_copy(
            src_ref=ref,
            dst_ref=ref,
            send_sem=r.ss.at[0],
            recv_sem=sem_of(r.rs, recv_ids, key),
            device_id=partner,
            device_id_type=MESH,
        ).wait_recv()

    def wbuf(p):
        return {"Q": r.WQ, "O": r.WOP.at[c], "U": r.WU, "D": r.WD}[p]

    starts = {}
    for n_rows in (48, 96):
        for m in range(16):
            first = pl.multiple_of(ids[m] * n_rows, 16)
            third = pl.multiple_of(ids[m] * n_rows + 2 * n_rows // 3, 16)
            starts[n_rows, m] = (first, third)

    def wslice(p, part, m):
        a, rows = APART[p], ROWS[p]
        first, third = starts[rows, m]
        if part == "A":
            return wbuf(p).at[pl.ds(first, a), :]
        return wbuf(p).at[pl.ds(third, rows - a), :]

    def forward(p, part, m, f):
        ref = wslice(p, part, m)
        last = ("plane", p, m // 4) if f == MV else None
        send(("ag", p, part, m ^ f), ref, ref, (ids[f], c), ("ag", p, part), last)

    def got(p, part, m):
        wait_recv(("ag", p, part, m), wslice(p, part, m))

    def ag_own(p):
        forward(p, "C", 0, MU)
        for f in (4, 8, 12):
            forward(p, "A", 0, f)
        forward(p, "A", 0, MU)
        forward(p, "A", 0, MV)
        for f in (4, 8, 12):
            forward(p, "C", 0, f)
        forward(p, "C", 0, MV)

    def ag_steps(p):
        steps = []

        def step(part, m, flips):
            def run():
                got(p, part, m)
                for f in flips:
                    forward(p, part, m, f)

            steps.append(run)

        step("C", MU, (4, 8, 12, MV))
        step("A", MU, (MV,))
        for zz in (4, 8, 12):
            step("A", zz, (MU, MV))
        for zz in (4, 8, 12):
            step("C", zz, (MV,))
            step("C", zz + MU, (MV,))
        for zz in (4, 8, 12):
            step("A", zz + MU, (MV,))
        return steps

    def ag_plane(p, zm):
        wait_recv(("plane", p, zm), wbuf(p).at[pl.ds(0, 2 * ROWS[p]), :])

    def run(steps):
        for s in steps:
            s()

    flip_u, flip_v = ((ids[MU], c),), ((ids[MV], c),)
    line = tuple((ids[m], c) for m in (4, 8, 12))
    vec_peers = ((line, flip_v, flip_u, (partner,)), ((partner,), flip_v, flip_u, line))

    def vec_slots(k, s):
        first = 48 * k + 8 * (s + (2 if k == 0 and s else 0))
        return [pl.ds(first + 8 * j, 8) for j in range(len(vec_peers[k][s]))]

    def vec_send(k, s):
        for j, (slot, dev) in enumerate(zip(vec_slots(k, s), vec_peers[k][s])):
            send(("v", k, s, j), r.VS.at[pl.ds(48 * k + 8 * s, 8), :], r.VR.at[slot, :], dev)

    def vec_step(k, s):
        total = r.VS[pl.ds(48 * k + 8 * s, 8), :]
        for j, slot in enumerate(vec_slots(k, s)):
            wait_recv(("v", k, s, j), r.VR.at[slot, :])
            total = total + r.VR[slot, :]
        r.VS[pl.ds(48 * k + (8 * s + 8 if s < 3 else 40), 8), :] = total
        if s < 3:
            vec_send(k, s + 1)

    def rs1_send(p, zm):
        rows = 2 * ROWS[p]
        s = pl.ds(zm * rows, rows)
        send(("r1", p, zm), r.S1[p].at[s, :], r.R1[p].at[s, :], (ids[MV], c), ("S1", p))

    def rs_sum1(p, zm):
        rows, a = ROWS[p], APART[p]
        b = rows - a
        g, r1 = r.G[p], r.R1[p]
        s = pl.ds(zm * 2 * rows, 2 * rows)
        wait_recv(("r1", p, zm), r1.at[s, :])
        for du in (1, 0):
            o = (2 * zm + du) * rows
            top = g[o : o + a, :] + r1[o : o + a, :].astype(F32)
            low = g[o + a : o + rows, :] + r1[o + a : o + rows, :].astype(F32)
            if du == 1:
                q = pl.ds(zm * a, a)
                r.S2A[p][q, :] = top.astype(BF)
                send(("r2a", p, zm), r.S2A[p].at[q, :], r.R2A[p].at[q, :], (ids[MU], c), ("S2A", p))
            else:
                g[o : o + a, :] = top
            if zm:
                q = pl.ds(((zm - 1) * 2 + du) * b, b)
                r.S2C[p][q, :] = low.astype(BF)
            else:
                g[o + a : o + rows, :] = low
        if zm:
            q = pl.ds((zm - 1) * 2 * b, 2 * b)
            send(("r2c", p), r.S2C[p].at[q, :], r.R2C[p].at[q, :], (ids[4 * zm], c), ("S2C", p))

    def rs_sum2a(p, zm):
        rows, a = ROWS[p], APART[p]
        g, r2 = r.G[p], r.R2A[p]
        q = pl.ds(zm * a, a)
        wait_recv(("r2a", p, zm), r2.at[q, :])
        o = 2 * zm * rows
        val = g[o : o + a, :] + r2[q, :].astype(F32)
        if zm:
            k = pl.ds((zm - 1) * a, a)
            r.S3A[p][k, :] = val.astype(BF)
            send(("r3a", p), r.S3A[p].at[k, :], r.R3A[p].at[k, :], (ids[4 * zm], c), ("S3A", p))
        else:
            g[o : o + a, :] = val

    def rs_sum2c(p):
        rows, a = ROWS[p], APART[p]
        b = rows - a
        g, r2 = r.G[p], r.R2C[p]
        wait_recv(("r2c", p), r2)
        for du in (1, 0):
            o = du * rows + a
            val = g[o : o + b, :]
            for zm in (1, 2, 3):
                k = ((zm - 1) * 2 + du) * b
                val = val + r2[k : k + b, :].astype(F32)
            if du == 1:
                r.S3C[p][...] = val.astype(BF)
                send(("r3c", p), r.S3C[p], r.R3C[p], (ids[MU], c))
            else:
                g[o : o + b, :] = val

    def rs_final(p):
        rows, a = ROWS[p], APART[p]
        g = r.G[p]
        r3a, r3c = r.R3A[p], r.R3C[p]
        wait_recv(("r3a", p), r3a)
        val = g[0:a, :]
        for zm in (1, 2, 3):
            val = val + r3a[(zm - 1) * a : zm * a, :].astype(F32)
        g[0:a, :] = val
        wait_recv(("r3c", p), r3c)
        g[a:rows, :] = g[a:rows, :] + r3c[...].astype(F32)

    def block_row(zm, du, dv):
        uu = 1 - u if du else u
        vv = 1 - v if dv else v
        return ub * uu + vb * vv

    def stage(p, zm, src, base):
        rows, cols = ROWS[p], COLS[p]
        for du in (1, 0):
            k = (2 * zm + du) * rows
            far = pl.ds(pl.multiple_of(base + block_row(zm, du, 1) * rows, 8), rows)
            near = pl.ds(pl.multiple_of(base + block_row(zm, du, 0) * rows, 8), rows)
            r.S1[p][k : k + rows, :] = src[far, 0:cols].astype(BF)
            r.G[p][k : k + rows, :] = src[near, 0:cols]

    flat = 2 * me + c
    arrived("wq", "wk", "wv")
    r.WQ[pl.ds(pl.multiple_of(me * 48, 16), 48), 0:384] = r.wq[...].astype(BF)
    r.WQ[pl.ds(pl.multiple_of(me * 48, 16), 48), 384:768] = r.wk[...].astype(BF)
    r.WQ[pl.ds(pl.multiple_of(me * 48, 16), 48), 768:1152] = r.wv[...].astype(BF)
    ag_own("Q")
    arrived("tok")
    send("tok", r.tok, r.X.at[own_rows, :], partner)
    local = pltpu.make_async_copy(r.tok, r.X.at[own_rows, :], r.ls.at[0])
    local.start()
    arrived("ga", "ba", "gf", "bf")
    r.VS[0:8, :] = jnp.zeros((8, 768), F32)
    for k, n in enumerate(("ga", "ba", "gf", "bf")):
        r.VS[k : k + 1, 0:24] = getattr(r, n)[...].reshape(1, 24).astype(BF).astype(F32)
    r.VS[0:8, :] = pltpu.roll(r.VS[0:8, :], 24 * flat, 1)
    vec_send(0, 0)
    arrived("wo")
    wo = r.wo[...]
    r.WOP[c, pl.ds(pl.multiple_of(me * 48, 16), 48), :] = jnp.concatenate(
        [wo[:, 0:384], wo[:, 384:768]], axis=0
    ).astype(BF)
    arrived("wu", "wd", "og")
    r.WU[pl.ds(pl.multiple_of(me * 96, 16), 96), :] = r.wu[...].astype(BF)
    r.WD[pl.ds(pl.multiple_of(me * 96, 16), 96), :] = r.wd[...].astype(BF)

    q_steps, o_steps, u_steps, d_steps = (ag_steps(p) for p in PIECES)
    run(q_steps[:5])
    ag_own("O")
    run(o_steps[:1])

    col_pos = lax.broadcasted_iota(jnp.int32, (512, 128), 0)
    row_pos = lax.broadcasted_iota(jnp.int32, (8, 512), 1)
    col_lab = jnp.zeros((512, 128), jnp.int32)
    row_lab = jnp.zeros((8, 512), jnp.int32)
    for j in range(8):
        lo = r.off[0, j]
        hi = lo + r.len[0, j]
        col_lab = jnp.where((col_pos >= lo) & (col_pos < hi), j + 1, col_lab)
        row_lab = jnp.where((row_pos >= lo) & (row_pos < hi), j + 1, row_lab)
    r.LIVE[...] = jnp.where(col_lab > 0, 1.0, 0.0).astype(F32)
    row_lab = jnp.where(row_lab > 0, row_lab, -1)
    for t in range(4):
        q = slice(128 * t, 128 * t + 128)
        lab = jnp.concatenate([col_lab[q]] * 4, axis=1)
        same = lab == jnp.broadcast_to(row_lab[0:1], (128, 512))
        r.BIAS[q, :] = jnp.where(same, 0.0, -1e30).astype(F32)

    run(q_steps[5:])
    vec_step(0, 0)
    run(o_steps[1:5])
    ag_own("U")
    wait_recv("tok", r.X.at[own_rows, :])
    local.wait()
    for zm in range(4):
        ag_plane("Q", zm)

    for k, n in enumerate(("Q3", "K3", "V3")):
        full = mm(r.X[...], r.WQ[:, 384 * k : 384 * k + 384])
        full = full.astype(BF)
        if k == 0:
            full = full * BF(0.125)
        for i in range(3):
            getattr(r, n)[i] = full[:, 128 * i : 128 * i + 128]
    run(u_steps[:1])
    vec_step(0, 1)

    for i in range(3):
        r.ATT[i] = jnp.zeros((512, 128), BF)
    fw_hooks = [
        o_steps[5:8],
        o_steps[8:],
        [functools.partial(vec_step, 0, 2)] + u_steps[1:3],
        u_steps[3:5],
        u_steps[5:8],
        [functools.partial(ag_own, "D")] + u_steps[8:10],
    ]
    lane = lax.broadcasted_iota(jnp.int32, (1, 128), 1)

    def half(val, a):
        keep = (lane >= 64 * a) & (lane < 64 * a + 64)
        return jnp.where(keep, val, jnp.zeros_like(val))

    def at_index(h, hooks):
        for k, steps in enumerate(hooks):

            def go(steps=steps):
                run(steps)

            pl.when(h == k)(go)

    def fwd_head(h, carry):
        at_index(h, fw_hooks)
        i = lax.div(h, 2)
        a = lax.rem(h, 2)
        vals = half(r.V3[i], a)
        keys = half(r.K3[i], a)
        for t in range(4):
            q = slice(128 * t, 128 * t + 128)
            s = mm(r.Q3[i, q, :], keys, 1, 1) + r.BIAS[q, :]
            live = r.LIVE[q, 0:1]
            top = jnp.where(live > 0, jnp.max(s, axis=1, keepdims=True), 0.0)
            w = jnp.exp(s - top)
            total = jnp.sum(w, axis=1, keepdims=True) + (1.0 - live)
            prob = w * (1.0 / total)
            r.P32[h, q, :] = prob
            o = mm(prob.astype(BF), vals)
            r.ATT[i, q, :] = r.ATT[i, q, :] + o.astype(BF)
        return carry

    lax.fori_loop(0, 6, fwd_head, 0)

    send("att", r.ATT.at[:, oth_rows, :], r.ATTR, partner)
    for zm in range(4):
        ag_plane("O", zm)
    send("wop", r.WOP.at[c], r.WOP.at[c], partner)
    run(d_steps[:1] + u_steps[10:12])
    vec_step(0, 3)
    wait_recv("wop", r.WOP.at[1 - c])

    def build_out(i, carry):
        for k in range(2):
            blk = r.WOP[k, pl.ds(pl.multiple_of(48 * i, 16), 48), :].astype(F32)
            rows = jnp.concatenate([blk[0:24], blk[24:48]], axis=1)
            r.T[pl.ds(pl.multiple_of(48 * i + 24 * k, 8), 24), 0:768] = rows
        return carry

    lax.fori_loop(0, 16, build_out, 0)
    r.WO[...] = r.T[:, 0:768].astype(BF)
    wait_recv("att", r.ATTR)
    own_heads = pl.ds(pl.multiple_of(384 * c, 128), 384)
    oth_heads = pl.ds(pl.multiple_of(384 * (1 - c), 128), 384)

    def joined(ref, rows):
        return jnp.concatenate([ref[i, rows, :] for i in range(3)], axis=1)

    all256 = pl.ds(0, 256)
    branch = mm(joined(r.ATT, own_rows), r.WO[own_heads, :])
    branch = branch + mm(joined(r.ATTR, all256), r.WO[oth_heads, :])
    r.GS[...] = branch
    run(u_steps[12:] + d_steps[1:2])

    def norm(val):
        mean = jnp.mean(val, axis=1, keepdims=True)
        cen = val - mean
        inv = lax.rsqrt(jnp.mean(cen * cen, axis=1, keepdims=True) + EPS)
        return cen * inv, inv

    def ln1(t, carry):
        q = pl.ds(pl.multiple_of(64 * t, 64), 64)
        unit, inv = norm(r.tok[q, :].astype(F32) + r.GS[q, :])
        r.U1[q, :] = unit
        r.INV1[q, :] = jnp.broadcast_to(inv, (64, 128))
        one = unit * r.VS[40:41, :] + r.VS[41:42, :]
        r.N1[q, :] = one
        r.FIN[pl.ds(pl.multiple_of(base256 + 64 * t, 64), 64), :] = one.astype(BF)
        return carry

    lax.fori_loop(0, 4, ln1, 0)
    send("fin", r.FIN.at[own_rows, :], r.FIN.at[own_rows, :], partner)
    run(d_steps[2:5])
    wait_recv("fin", r.FIN.at[oth_rows, :])

    def plane_rows(zm):
        return pl.ds(pl.multiple_of(384 * zs[zm], 128), 384)

    def ffn_up(zm):
        for t in range(2):
            q = slice(256 * t, 256 * t + 256)
            pre = mm(r.FIN[q, :], r.WU[plane_rows(zm), :], 1, 1)
            r.GEL[zm, q, :] = pre

        def act(t, carry):
            q = pl.ds(pl.multiple_of(64 * t, 64), 64)
            pre = r.GEL[zm, q, :]
            cdf = 0.5 * (1.0 + lax.erf(pre * (2.0**-0.5)))
            pdf = jnp.exp(-0.5 * pre * pre) * (1.0 / math.sqrt(2.0 * math.pi))
            r.HID[zm, q, :] = (pre * cdf).astype(BF)
            r.GEL[zm, q, :] = cdf + pre * pdf
            return carry

        lax.fori_loop(0, 8, act, 0)

    d_groups = ([], d_steps[5:8], d_steps[8:11], d_steps[11:])
    for zm in range(4):
        ag_plane("U", zm)
        run(d_groups[zm])
        ffn_up(zm)
    for zm in range(4):
        ag_plane("D", zm)
        for rows in (oth_rows, own_rows):
            part = mm(r.HID[zm, rows, :], r.WD[plane_rows(zm), :])
            if zm:
                part = part + r.SEC[rows, :]
            r.SEC[rows, :] = part
            if zm == 3 and rows is oth_rows:
                for h in range(2):
                    part_rows = pl.ds(pl.multiple_of(256 * (1 - c) + 128 * h, 128), 128)
                    send(("sec", h), r.SEC.at[part_rows, :], r.SECR.at[pl.ds(128 * h, 128), :], partner)

    def ln2(t, sums):
        dg, db = sums
        q = pl.ds(pl.multiple_of(64 * t, 64), 64)
        qq = pl.ds(pl.multiple_of(base256 + 64 * t, 64), 64)
        unit, inv = norm(r.N1[q, :] + (r.SEC[qq, :] + r.SECR[q, :]))
        gain = r.VS[42:43, :]
        r.out[q, :] = (unit * gain + r.VS[43:44, :]).astype(BF)
        e = r.og[q, :].astype(F32)
        dg = dg + jnp.sum(e * unit, axis=0, keepdims=True)
        db = db + jnp.sum(e, axis=0, keepdims=True)
        eg = e * gain
        inner = jnp.mean(eg * unit, axis=1, keepdims=True)
        gs = inv * (eg - jnp.mean(eg, axis=1, keepdims=True) - unit * inner)
        r.GS[q, :] = gs
        r.GFB[qq, :] = gs.astype(BF)
        return dg, db

    zero = jnp.zeros((1, 768), F32)
    dg2, db2 = zero, zero
    for h in range(2):
        wait_recv(("sec", h), r.SECR.at[pl.ds(128 * h, 128), :])
        dg2, db2 = lax.fori_loop(2 * h, 2 * h + 2, ln2, (dg2, db2))
        part_rows = r.GFB.at[pl.ds(pl.multiple_of(base256 + 128 * h, 128), 128), :]
        send(("gfb", h), part_rows, part_rows, partner)
    put("out")
    r.T[0:384, 0:768] = mm(r.HID[3, own_rows, :], r.GFB[own_rows, :], 0, 0)
    for h in range(2):
        wait_recv(("gfb", h), r.GFB.at[pl.ds(pl.multiple_of(256 * (1 - c) + 128 * h, 128), 128), :])
    for h in range(2):
        wait_sent(("sec", h))

    for n_done, zm in enumerate((3, 2, 1, 0)):
        if zm == 3:
            r.T[0:384, 0:768] = r.T[0:384, 0:768] + mm(r.HID[3, oth_rows, :], r.GFB[oth_rows, :], 0, 0)
        else:
            r.T[0:384, 0:768] = mm(r.HID[zm], r.GFB[...], 0, 0)
        stage("D", zm, r.T, 0)
        if zm > 1:
            rs1_send("D", zm)
        for t in range(2):
            q = slice(256 * t, 256 * t + 256)
            gh = mm(r.GFB[q, :], r.WD[plane_rows(zm), :], 1, 1)
            r.HID[zm, q, :] = (gh * r.GEL[zm, q, :]).astype(BF)
        r.T[384:768, 0:768] = mm(r.HID[zm], r.FIN[...], 0, 0)
        stage("U", zm, r.T, 384)
        if zm > 1:
            rs1_send("U", zm)
        for rows in (oth_rows, own_rows):
            part = mm(r.HID[zm, rows, :], r.WU[plane_rows(zm), :])
            if n_done:
                part = part + r.SEC[rows, :]
            r.SEC[rows, :] = part
            if n_done == 3 and rows is oth_rows:
                send("gn", r.SEC.at[oth_rows, :], r.SECR, partner)
        if n_done == 2:
            rs_sum1("D", 3)
    rs_sum1("U", 3)
    rs1_send("D", 1)
    wait_recv("gn", r.SECR)

    def ln1_back(t, sums):
        dg, db = sums
        q = pl.ds(pl.multiple_of(64 * t, 64), 64)
        qq = pl.ds(pl.multiple_of(base256 + 64 * t, 64), 64)
        e = r.GS[q, :] + (r.SEC[qq, :] + r.SECR[q, :])
        unit = r.U1[q, :]
        inv = r.INV1[q, 0:1]
        dg = dg + jnp.sum(e * unit, axis=0, keepdims=True)
        db = db + jnp.sum(e, axis=0, keepdims=True)
        eg = e * r.VS[40:41, :]
        inner = jnp.mean(eg * unit, axis=1, keepdims=True)
        first = inv * (eg - jnp.mean(eg, axis=1, keepdims=True) - unit * inner)
        r.GS[q, :] = first
        r.GB[q, :] = first.astype(BF)
        return dg, db

    dg1, db1 = lax.fori_loop(0, 4, ln1_back, (zero, zero))
    r.VS[48:56, :] = jnp.zeros((8, 768), F32)
    for k, val in enumerate((dg1, db1, dg2, db2)):
        r.VS[48 + k : 49 + k, :] = val
    vec_send(1, 0)

    gview = mm(r.GB[...], r.WO[oth_heads, :], 1, 1).astype(BF)
    for i in range(3):
        r.GAS[i] = gview[:, 128 * i : 128 * i + 128]
    send("gas", r.GAS, r.GA.at[:, own_rows, :], partner)
    gview = mm(r.GB[...], r.WO[own_heads, :], 1, 1).astype(BF)
    for i in range(3):
        r.GA[i, own_rows, :] = gview[:, 128 * i : 128 * i + 128]
    vec_step(1, 0)
    rs_sum2a("D", 3)
    rs1_send("U", 1)
    r.T[own_heads, 0:768] = mm(joined(r.ATT, own_rows), r.GB[...], 0, 0)
    r.T[oth_heads, 0:768] = mm(joined(r.ATTR, all256), r.GB[...], 0, 0)

    def pair_out(i, carry):
        q = pl.ds(pl.multiple_of(48 * i, 16), 48)
        blk = r.T[pl.ds(pl.multiple_of(48 * i + other24, 8), 24), 0:768]
        r.S0[q, :] = jnp.concatenate([blk[:, 0:384], blk[:, 384:768]], axis=0).astype(BF)
        return carry

    lax.fori_loop(0, 16, pair_out, 0)
    send("s0", r.S0, r.R0, partner)
    rs_sum1("D", 2)
    rs_sum2a("U", 3)
    wait_recv("s0", r.R0)

    def out_block(m):
        i = ids[m]
        blk = r.T[pl.ds(pl.multiple_of(48 * i + base24, 8), 24), 0:768]
        blk = jnp.concatenate([blk[:, 0:384], blk[:, 384:768]], axis=0)
        return blk + r.R0[pl.ds(pl.multiple_of(48 * i, 16), 48), :].astype(F32)

    for zm in (3, 2, 1, 0):
        for du in (1, 0):
            k = (2 * zm + du) * 48
            r.S1["O"][k : k + 48, :] = out_block(4 * zm + 2 * du + 1).astype(BF)
            r.G["O"][k : k + 48, :] = out_block(4 * zm + 2 * du)
        if zm > 1:
            rs1_send("O", zm)

    wait_recv("gas", r.GA.at[:, oth_rows, :])
    for n in ("DQ", "DK", "DV"):
        for i in range(3):
            getattr(r, n)[i] = jnp.zeros((512, 128), BF)

    def s1(p, zm):
        return functools.partial(rs_sum1, p, zm)

    def s2a(p, zm):
        return functools.partial(rs_sum2a, p, zm)

    def s2c(p):
        return functools.partial(rs_sum2c, p)

    def vs(s):
        return functools.partial(vec_step, 1, s)

    bw_hooks = [
        [],
        [s1("U", 2)],
        [s2a("D", 2)],
        [],
        [s1("D", 1)],
        [s2a("U", 2), vs(1)],
    ]

    def bwd_head(h, carry):
        at_index(h, bw_hooks)
        i = lax.div(h, 2)
        a = lax.rem(h, 2)
        go = half(r.GA[i], a)
        for t in range(4):
            q = slice(128 * t, 128 * t + 128)
            prob = r.P32[h, q, :]
            dp = mm(go[q], r.V3[i], 1, 1)
            delta = jnp.sum(prob * dp, axis=1, keepdims=True)
            r.DSB[q, :] = (prob * (dp - delta)).astype(BF)
            r.PB[q, :] = prob.astype(BF)
        r.DV[i] = r.DV[i] + mm(r.PB[...], go, 0, 0).astype(BF)
        dq = mm(r.DSB[...], half(r.K3[i], a)) * 0.125
        r.DQ[i] = r.DQ[i] + dq.astype(BF)
        dk = mm(r.DSB[...], half(r.Q3[i], a), 0, 0)
        r.DK[i] = r.DK[i] + dk.astype(BF)
        return carry

    lax.fori_loop(0, 6, bwd_head, 0)

    all512 = pl.ds(0, 512)
    for k, n in enumerate(("DQ", "DK", "DV")):
        r.T[:, 384 * k : 384 * k + 384] = mm(r.X[...], joined(getattr(r, n), all512), 0, 0)
    for zm in (3, 2, 1, 0):
        stage("Q", zm, r.T, 192 * zs[zm])
        if zm > 1:
            rs1_send("Q", zm)

    def s0(p, zm):
        return functools.partial(rs1_send, p, zm)

    run([s1("U", 1), s2a("D", 1), vs(2), s0("Q", 1), s0("O", 1)])

    for rows in (oth_rows, own_rows):
        acc = mm(joined(r.DQ, rows), r.WQ[:, 0:384], 1, 1)
        acc = acc + mm(joined(r.DK, rows), r.WQ[:, 384:768], 1, 1)
        acc = acc + mm(joined(r.DV, rows), r.WQ[:, 768:1152], 1, 1)
        if rows is oth_rows:
            r.IGS[...] = acc.astype(BF)
            send("ig", r.IGS, r.IGR, partner)
            run([s1("O", 3), s1("O", 2), s2a("U", 1), s2a("O", 3), s0("D", 0)])
        else:
            r.GS[...] = r.GS[...] + acc
    wait_recv("ig", r.IGR)
    r.ig[...] = (r.GS[...] + r.IGR[...].astype(F32)).astype(BF)
    put("ig")

    run([s1("Q", 3), s2a("O", 2), s0("U", 0), s1("Q", 2), s2a("Q", 3), s0("Q", 0)])
    run([s1("Q", 1), s2a("Q", 2), s1("O", 1), s2a("Q", 1), s1("D", 0), s2a("O", 1), s2c("D")])
    run([s1("U", 0), s2c("U"), s2a("D", 0), s0("O", 0), s1("Q", 0), s2c("Q"), s2a("U", 0)])
    run([s2a("Q", 0), s1("O", 0), s2c("O"), s2a("O", 0)])
    rs_final("Q")
    r.dwq[...] = r.G["Q"][0:48, 0:384]
    r.dwk[...] = r.G["Q"][0:48, 384:768]
    r.dwv[...] = r.G["Q"][0:48, 768:1152]
    rs_final("D")
    r.dwd[...] = r.G["D"][0:96, :]
    put("dwq", "dwk", "dwv", "dwd")
    rs_final("U")
    r.dwu[...] = r.G["U"][0:96, :]
    rs_final("O")
    vec_step(1, 3)
    go = r.G["O"][0:48, :]
    r.dwo[...] = jnp.concatenate([go[0:24], go[24:48]], axis=1)
    back = pltpu.roll(r.VS[88:96, :], lax.rem(768 - 24 * flat, 768), 1)
    for k, n in enumerate(("dga", "dba", "dgf", "dbf")):
        getattr(r, n)[...] = back[k, 0:24]
    put("dwu", "dwo", "dga", "dba", "dgf", "dbf")

    for src, out, key in sends:
        if out in waited:
            continue
        waited.add(out)
        if out[0] == "one":
            ref = src
        elif out[0] == "ag":
            count = sum(o == out for _, o, _ in sends)
            n_rows = APART[out[1]] if out[2] == "A" else ROWS[out[1]] - APART[out[1]]
            ref = wbuf(out[1]).at[pl.ds(0, count * n_rows), :]
        else:
            ref = getattr(r, out[0])[out[1]]
        wait_send(out, ref)
    assert len(send_ids) == SENT and len(recv_ids) == RECEIVED, (len(send_ids), len(recv_ids))
    for cp in out_copies:
        cp.wait()


def hand_over(*refs):
    n = len(MOVED_OUT)
    srcs, dsts, bufs, sems = refs[:n], refs[n : 2 * n], refs[2 * n : 3 * n], refs[3 * n]
    reads = [pltpu.make_async_copy(srcs[k], bufs[k], sems.at[k]) for k in range(n)]
    writes = [pltpu.make_async_copy(bufs[k], dsts[k], sems.at[n + k]) for k in range(n)]
    for cp in reads:
        cp.start()
    for rd, wr in zip(reads, writes):
        rd.wait()
        wr.start()
    for cp in writes:
        cp.wait()


def layer_small(*args):
    shapes = tuple((shape, dtype) for _, shape, dtype in MOVED_OUT)
    smem = pl.BlockSpec(memory_space=pltpu.SMEM)
    anywhere = pl.BlockSpec(memory_space=pl.ANY)
    out_shape = tuple(jax.ShapeDtypeStruct(s, d) for s, d in shapes)
    up = IN_NAMES.index("wu")
    args = args[:up] + (args[up].T,) + args[up + 1 :]
    outs = pl.pallas_call(
        layer_kernel,
        out_shape=out_shape,
        in_specs=[smem if n in ("len", "off") else anywhere for n in IN_NAMES],
        out_specs=tuple(anywhere for _ in shapes),
        scratch_shapes=[s for _, s in scratch_list()],
        compiler_params=pltpu.CompilerParams(
            collective_id=0, has_side_effects=True, vmem_limit_bytes=67043328
        ),
    )(*args)
    outs = pl.pallas_call(
        hand_over,
        out_shape=out_shape,
        in_specs=[anywhere for _ in shapes],
        out_specs=tuple(anywhere for _ in shapes),
        scratch_shapes=[pltpu.VMEM(shape, dtype) for shape, dtype in shapes]
        + [pltpu.SemaphoreType.DMA((2 * len(shapes),))],
    )(*outs)
    up = OUT_NAMES.index("dwu")
    return outs[:up] + (outs[up].T,) + outs[up + 1 :]


def labels_of(lengths, offsets):
    position = jnp.arange(BIN, dtype=jnp.int32)[:, None]
    starts = offsets[None, :]
    inside = (position >= starts) & (position < starts + lengths[None, :])
    slot_order = jnp.arange(1, lengths.shape[0] + 1, dtype=jnp.int32)[None, :]
    return jnp.sum(jnp.where(inside, slot_order, 0), axis=1)


def layer_norm(operand, gain_vec, bias_vec):
    row_mean = jnp.mean(operand, axis=-1, keepdims=True)
    centered = operand - row_mean
    inverse = lax.rsqrt(jnp.mean(centered * centered, axis=-1, keepdims=True) + EPS)
    normed = centered * inverse
    return (normed * gain_vec + bias_vec, normed, inverse)


def norm_back(grad_rows, normed, inverse, gain_vec):
    scaled = grad_rows * gain_vec
    inner = jnp.mean(scaled * normed, axis=-1, keepdims=True)
    return inverse * (scaled - jnp.mean(scaled, axis=-1, keepdims=True) - normed * inner)


def gelu_exact(operand):
    return jax.nn.gelu(operand, approximate=False)


def contract_rows(left, right):
    return lax.dot_general(
        left, right, (((0,), (0,)), ((), ())), preferred_element_type=F32
    )


def contract_cols(left, right):
    return lax.dot_general(
        left, right, (((1,), (1,)), ((), ())), preferred_element_type=F32
    )


def score_block(queries, key_rows, labels_bin, factor):
    scores = (
        jnp.einsum("qhd,khd->hqk", queries, key_rows, preferred_element_type=F32) * factor
    )
    allowed = ((labels_bin[:, None] == labels_bin[None, :]) & (labels_bin[:, None] > 0))[None]
    live_rows = (labels_bin > 0)[None, :, None]
    return (scores, allowed, live_rows)


def masked_exp(scores, allowed, row_top):
    return jnp.where(allowed, jnp.exp(jnp.where(allowed, scores - row_top, 0.0)), 0.0)


def attend_bin(pieces, factor):
    queries, key_rows, value_rows, labels_bin = pieces
    scores, allowed, live_rows = score_block(queries, key_rows, labels_bin, factor)
    row_top = jnp.max(jnp.where(allowed, scores, -1e30), axis=2, keepdims=True)
    row_top = jnp.where(live_rows, row_top, 0.0)
    weights = masked_exp(scores, allowed, row_top)
    denominator = jnp.sum(weights, axis=2, keepdims=True) + jnp.where(live_rows, 0.0, 1.0)
    probability = (weights / denominator).astype(jnp.bfloat16)
    mixed_rows = jnp.einsum(
        "hqk,khd->qhd", probability, value_rows, preferred_element_type=F32
    )
    return (mixed_rows.astype(jnp.bfloat16), row_top, denominator)


def attend_back(pieces, factor):
    queries, key_rows, value_rows, labels_bin, row_top, denominator, grad_mixed = pieces
    scores, allowed, live_rows = score_block(queries, key_rows, labels_bin, factor)
    probability = masked_exp(scores, allowed, row_top) / denominator
    grad_values = jnp.einsum(
        "hqk,qhd->khd",
        probability.astype(jnp.bfloat16),
        grad_mixed,
        preferred_element_type=F32,
    )
    grad_probs = jnp.einsum(
        "qhd,khd->hqk", grad_mixed, value_rows, preferred_element_type=F32
    )
    row_delta = jnp.sum(probability * grad_probs, axis=2, keepdims=True)
    grad_scores = (probability * (grad_probs - row_delta)).astype(jnp.bfloat16)
    grad_queries = (
        jnp.einsum("hqk,khd->qhd", grad_scores, key_rows, preferred_element_type=F32)
        * factor
    )
    grad_keys = (
        jnp.einsum("hqk,qhd->khd", grad_scores, queries, preferred_element_type=F32)
        * factor
    )
    return (
        grad_queries.astype(jnp.bfloat16),
        grad_keys.astype(jnp.bfloat16),
        grad_values.astype(jnp.bfloat16),
    )


def per_device(
    tokens,
    w_query,
    w_key,
    w_value,
    w_out,
    gain_attn,
    bias_attn,
    w_up,
    w_down,
    gain_ffn,
    bias_ffn,
    seq_lengths,
    seq_offsets,
    out_grad,
):
    low_type = jnp.bfloat16
    bin_count = seq_lengths.shape[0]
    group_rows = bin_count * BIN
    head_width = w_query.shape[1]
    local_heads = head_width // HD
    factor = 1.0 / math.sqrt(HD)
    labels = jax.vmap(labels_of)(seq_lengths, seq_offsets)
    full_query, full_key, full_value = (
        lax.all_gather(w_query.astype(low_type), DP, axis=0, tiled=True),
        lax.all_gather(w_key.astype(low_type), DP, axis=0, tiled=True),
        lax.all_gather(w_value.astype(low_type), DP, axis=0, tiled=True),
    )
    projection = jnp.concatenate([full_query, full_key, full_value], axis=1)
    whole_rows = lax.all_gather(tokens, HEAD, axis=0, tiled=True)
    projected = jnp.dot(whole_rows, projection, preferred_element_type=F32).astype(low_type)
    shape_bins = (bin_count, BIN, local_heads, HD)
    queries = projected[:, :head_width].reshape(shape_bins)
    key_rows = projected[:, head_width : 2 * head_width].reshape(shape_bins)
    value_rows = projected[:, 2 * head_width :].reshape(shape_bins)
    mixed_bins, row_tops, denominators = lax.map(
        lambda pieces: attend_bin(pieces, factor), (queries, key_rows, value_rows, labels)
    )
    attended = mixed_bins.reshape(group_rows, head_width)
    out_full, up_part, down_part, gain_one, bias_one, gain_two, bias_two = (
        lax.all_gather(w_out.astype(low_type), BOTH, axis=0, tiled=True),
        lax.all_gather(w_up.astype(low_type), BOTH, axis=1, tiled=True),
        lax.all_gather(w_down.astype(low_type), BOTH, axis=0, tiled=True),
        lax.all_gather(gain_attn.astype(low_type), BOTH, axis=0, tiled=True),
        lax.all_gather(bias_attn.astype(low_type), BOTH, axis=0, tiled=True),
        lax.all_gather(gain_ffn.astype(low_type), BOTH, axis=0, tiled=True),
        lax.all_gather(bias_ffn.astype(low_type), BOTH, axis=0, tiled=True),
    )
    gain_first = gain_one.astype(F32)
    gain_second = gain_two.astype(F32)
    token_view = lax.all_to_all(attended, HEAD, split_axis=0, concat_axis=1, tiled=True)
    first_sum = tokens.astype(F32) + jnp.dot(
        token_view, out_full, preferred_element_type=F32
    )
    normed_one, unit_one, inverse_one = layer_norm(
        first_sum, gain_first, bias_one.astype(F32)
    )
    ffn_input = normed_one.astype(low_type)
    pre_act = jnp.dot(ffn_input, up_part, preferred_element_type=F32)
    activated, gelu_pull = jax.vjp(gelu_exact, pre_act)
    hidden = activated.astype(low_type)
    second_sum = normed_one + jnp.dot(hidden, down_part, preferred_element_type=F32)
    result, unit_two, inverse_two = layer_norm(
        second_sum, gain_second, bias_two.astype(F32)
    )
    output = result.astype(low_type)
    grad_result = out_grad.astype(F32)
    grad_gain_two = jnp.sum(grad_result * unit_two, axis=0)
    grad_bias_two = jnp.sum(grad_result, axis=0)
    grad_second = norm_back(grad_result, unit_two, inverse_two, gain_second)
    grad_ffn = grad_second.astype(low_type)
    grad_down_part = contract_rows(hidden, grad_ffn)
    grad_pre = gelu_pull(contract_cols(grad_ffn, down_part))[0].astype(low_type)
    grad_up_part = contract_rows(ffn_input, grad_pre)
    grad_normed = grad_second + contract_cols(grad_pre, up_part)
    grad_gain_one = jnp.sum(grad_normed * unit_one, axis=0)
    grad_bias_one = jnp.sum(grad_normed, axis=0)
    grad_first = norm_back(grad_normed, unit_one, inverse_one, gain_first)
    grad_branch = grad_first.astype(low_type)
    grad_out_full = contract_rows(token_view, grad_branch)
    part_out, part_up, part_down, part_gain_one, part_bias_one, part_gain_two, part_bias_two = (
        lax.psum_scatter(grad_out_full, BOTH, scatter_dimension=0, tiled=True),
        lax.psum_scatter(grad_up_part, BOTH, scatter_dimension=1, tiled=True),
        lax.psum_scatter(grad_down_part, BOTH, scatter_dimension=0, tiled=True),
        lax.psum_scatter(grad_gain_one, BOTH, scatter_dimension=0, tiled=True),
        lax.psum_scatter(grad_bias_one, BOTH, scatter_dimension=0, tiled=True),
        lax.psum_scatter(grad_gain_two, BOTH, scatter_dimension=0, tiled=True),
        lax.psum_scatter(grad_bias_two, BOTH, scatter_dimension=0, tiled=True),
    )
    grad_token_view = contract_cols(grad_branch, out_full).astype(low_type)
    grad_attended = lax.all_to_all(grad_token_view, HEAD, split_axis=1, concat_axis=0, tiled=True)
    grad_bins = grad_attended.reshape(shape_bins)
    grad_queries, grad_keys, grad_values = lax.map(
        lambda pieces: attend_back(pieces, factor),
        (queries, key_rows, value_rows, labels, row_tops, denominators, grad_bins),
    )
    grad_projected = jnp.concatenate(
        [
            grad_queries.reshape(group_rows, head_width),
            grad_keys.reshape(group_rows, head_width),
            grad_values.reshape(group_rows, head_width),
        ],
        axis=1,
    )
    grad_projection = contract_rows(whole_rows, grad_projected)
    part_query, part_key, part_value = (
        lax.psum_scatter(grad_projection[:, :head_width], DP, scatter_dimension=0, tiled=True),
        lax.psum_scatter(
            grad_projection[:, head_width : 2 * head_width], DP, scatter_dimension=0, tiled=True
        ),
        lax.psum_scatter(
            grad_projection[:, 2 * head_width :], DP, scatter_dimension=0, tiled=True
        ),
    )
    input_grad = (
        grad_first
        + lax.psum_scatter(
            contract_cols(grad_projected, projection).astype(jnp.bfloat16),
            HEAD,
            scatter_dimension=0,
            tiled=True,
        ).astype(F32)
    ).astype(low_type)
    return (
        output,
        input_grad,
        part_query,
        part_key,
        part_value,
        part_out,
        part_gain_one,
        part_bias_one,
        part_up,
        part_down,
        part_gain_two,
        part_bias_two,
    )


def solution(mesh):
    small = mesh.shape[DP] == 16 and mesh.shape[HEAD] == 2
    return jax.shard_map(
        layer_small if small else per_device,
        mesh=mesh,
        in_specs=(
            P(BOTH, None),
            P(DP, HEAD),
            P(DP, HEAD),
            P(DP, HEAD),
            P(BOTH, None),
            P(BOTH),
            P(BOTH),
            P(None, BOTH),
            P(BOTH, None),
            P(BOTH),
            P(BOTH),
            P(DP, None),
            P(DP, None),
            P(BOTH, None),
        ),
        out_specs=(
            P(BOTH, None),
            P(BOTH, None),
            P(DP, HEAD),
            P(DP, HEAD),
            P(DP, HEAD),
            P(BOTH, None),
            P(BOTH),
            P(BOTH),
            P(None, BOTH),
            P(BOTH, None),
            P(BOTH),
            P(BOTH),
        ),
        check_vma=False,
    )
```

```python
import functools
import math
import types

import jax
import jax.numpy as jnp
from jax import lax
from jax.experimental import pallas as pl
from jax.experimental.pallas import tpu as pltpu
from jax.sharding import PartitionSpec as P

HD = 64
BIN = 512
EPS = 1e-12
F32 = jnp.float32
BF = jnp.bfloat16
MESH = pl.DeviceIdType.MESH

MU, MV = 2, 1
ROWS = {"Q": 48, "O": 48, "U": 96, "D": 96}
COLS = {"Q": 1152, "O": 384, "U": 768, "D": 768}
APART = {"Q": 32, "O": 32, "U": 64, "D": 64}
PIECES = ("Q", "O", "U", "D")
PER_PIECE = ("G", "S1", "R1", "S2A", "R2A", "S3A", "R3A", "S2C", "R2C", "S3C", "R3C")
DP, HEAD = "dp", "head"
BOTH = (DP, HEAD)
SENT, RECEIVED = 52, 140


def mm(a, b, ca=1, cb=0):
    return lax.dot_general(a, b, (((ca,), (cb,)), ((), ())), preferred_element_type=F32)


def scratch_list():
    items = []
    for name, shape, dtype in MOVED_IN + MOVED_OUT:
        items.append((name, pltpu.VMEM(shape, dtype)))

    def add(name, shape, dtype):
        items.append((name, pltpu.VMEM(shape, dtype)))

    add("X", (512, 768), BF)
    add("WQ", (768, 1152), BF)
    add("WOP", (2, 768, 384), BF)
    add("WO", (768, 768), BF)
    add("WU", (1536, 768), BF)
    add("WD", (1536, 768), BF)
    for n in ("Q3", "K3", "V3", "ATT", "GA", "DQ", "DK", "DV"):
        add(n, (3, 512, 128), BF)
    add("ATTR", (3, 256, 128), BF)
    add("GAS", (3, 256, 128), BF)
    add("BIAS", (512, 512), F32)
    add("LIVE", (512, 128), F32)
    add("P32", (6, 512, 512), F32)
    add("PB", (512, 512), BF)
    add("DSB", (512, 512), BF)
    add("U1", (256, 768), F32)
    add("N1", (256, 768), F32)
    add("INV1", (256, 128), F32)
    add("FIN", (512, 768), BF)
    add("HID", (4, 512, 384), BF)
    add("GEL", (4, 512, 384), F32)
    add("SEC", (512, 768), F32)
    add("SECR", (256, 768), F32)
    add("GS", (256, 768), F32)
    add("GFB", (512, 768), BF)
    add("GB", (256, 768), BF)
    add("IGS", (256, 768), BF)
    add("IGR", (256, 768), BF)
    add("T", (768, 1152), F32)
    add("S0", (768, 384), BF)
    add("R0", (768, 384), BF)
    for p in PIECES:
        r, c, a = ROWS[p], COLS[p], APART[p]
        b = r - a
        sizes = (8 * r, 8 * r, 8 * r, 4 * a, 4 * a, 3 * a, 3 * a, 6 * b, 6 * b, b, b)
        for key, size in zip(PER_PIECE, sizes):
            add(key + p, (size, c), F32 if key == "G" else BF)
    add("VS", (96, 768), F32)
    add("VR", (96, 768), F32)
    items.append(("ss", pltpu.SemaphoreType.DMA((SENT,))))
    items.append(("rs", pltpu.SemaphoreType.DMA((RECEIVED,))))
    items.append(("ls", pltpu.SemaphoreType.DMA((1 + len(MOVED_IN) + len(MOVED_OUT),))))
    return items


IN_NAMES = ("tok", "wq", "wk", "wv", "wo", "ga", "ba", "wu", "wd", "gf", "bf", "len", "off", "og")
MOVED_IN = (
    ("wq", (48, 384), F32),
    ("wk", (48, 384), F32),
    ("wv", (48, 384), F32),
    ("ga", (24,), F32),
    ("ba", (24,), F32),
    ("gf", (24,), F32),
    ("bf", (24,), F32),
    ("tok", (256, 768), BF),
    ("wo", (24, 768), F32),
    ("wu", (96, 768), F32),
    ("wd", (96, 768), F32),
    ("og", (256, 768), BF),
)
MOVED_OUT = (
    ("out", (256, 768), BF),
    ("ig", (256, 768), BF),
    ("dwq", (48, 384), F32),
    ("dwk", (48, 384), F32),
    ("dwv", (48, 384), F32),
    ("dwo", (24, 768), F32),
    ("dga", (24,), F32),
    ("dba", (24,), F32),
    ("dwu", (96, 768), F32),
    ("dwd", (96, 768), F32),
    ("dgf", (24,), F32),
    ("dbf", (24,), F32),
)
OUT_NAMES = ("out", "ig", "dwq", "dwk", "dwv", "dwo", "dga", "dba", "dwu", "dwd", "dgf", "dbf")


def layer_kernel(*refs):
    ins = tuple(n if n in ("len", "off") else "far_" + n for n in IN_NAMES)
    outs = tuple("far_" + n for n in OUT_NAMES)
    names = ins + outs + tuple(n for n, _ in scratch_list())
    named = dict(zip(names, refs))
    r = types.SimpleNamespace(**named)
    for key in PER_PIECE:
        setattr(r, key, {p: named[key + p] for p in PIECES})
    me = lax.axis_index(DP)
    c = lax.axis_index(HEAD)
    x = lax.rem(me, 2)
    y = lax.rem(lax.div(me, 2), 2)
    z = lax.div(me, 4)
    u = x + c * (y - x)
    v = y + c * (x - y)
    ub = 1 + c
    vb = 2 - c
    zs = (z, z + 1 - 2 * lax.rem(z, 2), lax.rem(z + 2, 4), 3 - z)

    def chip(m):
        zm, du, dv = m // 4, (m // 2) % 2, m % 2
        uu = 1 - u if du else u
        vv = 1 - v if dv else v
        return 4 * zs[zm] + ub * uu + vb * vv

    ids = [chip(m) for m in range(16)]
    partner = (me, 1 - c)
    base256, base24, other24 = 256 * c, 24 * c, 24 * (1 - c)
    own_rows = pl.ds(pl.multiple_of(256 * c, 256), 256)
    oth_rows = pl.ds(pl.multiple_of(256 * (1 - c), 256), 256)

    in_copies, out_copies = {}, []
    for k, (n, _, _) in enumerate(MOVED_IN):
        in_copies[n] = pltpu.make_async_copy(named["far_" + n], named[n], r.ls.at[1 + k])
        in_copies[n].start()

    def arrived(*keys):
        for n in keys:
            in_copies[n].wait()

    def put(*keys):
        for n in keys:
            k = 1 + len(MOVED_IN) + OUT_NAMES.index(n)
            cp = pltpu.make_async_copy(named[n], named["far_" + n], r.ls.at[k])
            cp.start()
            out_copies.append(cp)

    peers = [partner] + [(ids[m], c) for m in (MU, MV, 4, 8, 12)]
    barrier = pltpu.get_barrier_semaphore()
    for dev in peers:
        pl.semaphore_signal(barrier, inc=1, device_id=dev, device_id_type=MESH)
    pl.semaphore_wait(barrier, len(peers))

    sends = []
    send_ids, recv_ids = {}, {}

    def sem_of(sems, ids_of, name):
        return sems.at[ids_of.setdefault(name, len(ids_of))]

    def send(key, src, dst, dev, out_group=None, in_group=None):
        out = out_group or ("one", len(sends))
        cp = pltpu.make_async_remote_copy(
            src_ref=src,
            dst_ref=dst,
            send_sem=sem_of(r.ss, send_ids, out),
            recv_sem=sem_of(r.rs, recv_ids, in_group or key),
            device_id=dev,
            device_id_type=MESH,
        )
        cp.start()
        sends.append((src, out, key))

    def wait_send(out, ref):
        pltpu.make_async_remote_copy(
            src_ref=ref,
            dst_ref=ref,
            send_sem=sem_of(r.ss, send_ids, out),
            recv_sem=r.rs.at[0],
            device_id=partner,
            device_id_type=MESH,
        ).wait_send()

    waited = set()

    def wait_sent(key):
        for src, out, k in sends:
            if k == key:
                wait_send(out, src)
                waited.add(out)

    def wait_recv(key, ref):
        pltpu.make_async_remote_copy(
            src_ref=ref,
            dst_ref=ref,
            send_sem=r.ss.at[0],
            recv_sem=sem_of(r.rs, recv_ids, key),
            device_id=partner,
            device_id_type=MESH,
        ).wait_recv()

    def wbuf(p):
        return {"Q": r.WQ, "O": r.WOP.at[c], "U": r.WU, "D": r.WD}[p]

    starts = {}
    for n_rows in (48, 96):
        for m in range(16):
            first = pl.multiple_of(ids[m] * n_rows, 16)
            third = pl.multiple_of(ids[m] * n_rows + 2 * n_rows // 3, 16)
            starts[n_rows, m] = (first, third)

    def wslice(p, part, m):
        a, rows = APART[p], ROWS[p]
        first, third = starts[rows, m]
        if part == "A":
            return wbuf(p).at[pl.ds(first, a), :]
        return wbuf(p).at[pl.ds(third, rows - a), :]

    def forward(p, part, m, f):
        ref = wslice(p, part, m)
        last = ("plane", p, m // 4) if f == MV else None
        send(("ag", p, part, m ^ f), ref, ref, (ids[f], c), ("ag", p, part), last)

    def got(p, part, m):
        wait_recv(("ag", p, part, m), wslice(p, part, m))

    def ag_own(p):
        forward(p, "C", 0, MU)
        for f in (4, 8, 12):
            forward(p, "A", 0, f)
        forward(p, "A", 0, MU)
        forward(p, "A", 0, MV)
        for f in (4, 8, 12):
            forward(p, "C", 0, f)
        forward(p, "C", 0, MV)

    def ag_steps(p):
        steps = []

        def step(part, m, flips):
            def run():
                got(p, part, m)
                for f in flips:
                    forward(p, part, m, f)

            steps.append(run)

        step("C", MU, (4, 8, 12, MV))
        step("A", MU, (MV,))
        for zz in (4, 8, 12):
            step("A", zz, (MU, MV))
        for zz in (4, 8, 12):
            step("C", zz, (MV,))
            step("C", zz + MU, (MV,))
        for zz in (4, 8, 12):
            step("A", zz + MU, (MV,))
        return steps

    def ag_plane(p, zm):
        wait_recv(("plane", p, zm), wbuf(p).at[pl.ds(0, 2 * ROWS[p]), :])

    def run(steps):
        for s in steps:
            s()

    flip_u, flip_v = ((ids[MU], c),), ((ids[MV], c),)
    line = tuple((ids[m], c) for m in (4, 8, 12))
    vec_peers = ((line, flip_v, flip_u, (partner,)), ((partner,), flip_v, flip_u, line))

    def vec_slots(k, s):
        first = 48 * k + 8 * (s + (2 if k == 0 and s else 0))
        return [pl.ds(first + 8 * j, 8) for j in range(len(vec_peers[k][s]))]

    def vec_send(k, s):
        for j, (slot, dev) in enumerate(zip(vec_slots(k, s), vec_peers[k][s])):
            send(("v", k, s, j), r.VS.at[pl.ds(48 * k + 8 * s, 8), :], r.VR.at[slot, :], dev)

    def vec_step(k, s):
        total = r.VS[pl.ds(48 * k + 8 * s, 8), :]
        for j, slot in enumerate(vec_slots(k, s)):
            wait_recv(("v", k, s, j), r.VR.at[slot, :])
            total = total + r.VR[slot, :]
        r.VS[pl.ds(48 * k + (8 * s + 8 if s < 3 else 40), 8), :] = total
        if s < 3:
            vec_send(k, s + 1)

    def rs1_send(p, zm):
        rows = 2 * ROWS[p]
        s = pl.ds(zm * rows, rows)
        send(("r1", p, zm), r.S1[p].at[s, :], r.R1[p].at[s, :], (ids[MV], c), ("S1", p))

    def rs_sum1(p, zm):
        rows, a = ROWS[p], APART[p]
        b = rows - a
        g, r1 = r.G[p], r.R1[p]
        s = pl.ds(zm * 2 * rows, 2 * rows)
        wait_recv(("r1", p, zm), r1.at[s, :])
        for du in (1, 0):
            o = (2 * zm + du) * rows
            top = g[o : o + a, :] + r1[o : o + a, :].astype(F32)
            low = g[o + a : o + rows, :] + r1[o + a : o + rows, :].astype(F32)
            if du == 1:
                q = pl.ds(zm * a, a)
                r.S2A[p][q, :] = top.astype(BF)
                send(("r2a", p, zm), r.S2A[p].at[q, :], r.R2A[p].at[q, :], (ids[MU], c), ("S2A", p))
            else:
                g[o : o + a, :] = top
            if zm:
                q = pl.ds(((zm - 1) * 2 + du) * b, b)
                r.S2C[p][q, :] = low.astype(BF)
            else:
                g[o + a : o + rows, :] = low
        if zm:
            q = pl.ds((zm - 1) * 2 * b, 2 * b)
            send(("r2c", p), r.S2C[p].at[q, :], r.R2C[p].at[q, :], (ids[4 * zm], c), ("S2C", p))

    def rs_sum2a(p, zm):
        rows, a = ROWS[p], APART[p]
        g, r2 = r.G[p], r.R2A[p]
        q = pl.ds(zm * a, a)
        wait_recv(("r2a", p, zm), r2.at[q, :])
        o = 2 * zm * rows
        val = g[o : o + a, :] + r2[q, :].astype(F32)
        if zm:
            k = pl.ds((zm - 1) * a, a)
            r.S3A[p][k, :] = val.astype(BF)
            send(("r3a", p), r.S3A[p].at[k, :], r.R3A[p].at[k, :], (ids[4 * zm], c), ("S3A", p))
        else:
            g[o : o + a, :] = val

    def rs_sum2c(p):
        rows, a = ROWS[p], APART[p]
        b = rows - a
        g, r2 = r.G[p], r.R2C[p]
        wait_recv(("r2c", p), r2)
        for du in (1, 0):
            o = du * rows + a
            val = g[o : o + b, :]
            for zm in (1, 2, 3):
                k = ((zm - 1) * 2 + du) * b
                val = val + r2[k : k + b, :].astype(F32)
            if du == 1:
                r.S3C[p][...] = val.astype(BF)
                send(("r3c", p), r.S3C[p], r.R3C[p], (ids[MU], c))
            else:
                g[o : o + b, :] = val

    def rs_final(p):
        rows, a = ROWS[p], APART[p]
        g = r.G[p]
        r3a, r3c = r.R3A[p], r.R3C[p]
        wait_recv(("r3a", p), r3a)
        val = g[0:a, :]
        for zm in (1, 2, 3):
            val = val + r3a[(zm - 1) * a : zm * a, :].astype(F32)
        g[0:a, :] = val
        wait_recv(("r3c", p), r3c)
        g[a:rows, :] = g[a:rows, :] + r3c[...].astype(F32)

    def block_row(zm, du, dv):
        uu = 1 - u if du else u
        vv = 1 - v if dv else v
        return ub * uu + vb * vv

    def stage(p, zm, src, base):
        rows, cols = ROWS[p], COLS[p]
        for du in (1, 0):
            k = (2 * zm + du) * rows
            far = pl.ds(pl.multiple_of(base + block_row(zm, du, 1) * rows, 8), rows)
            near = pl.ds(pl.multiple_of(base + block_row(zm, du, 0) * rows, 8), rows)
            r.S1[p][k : k + rows, :] = src[far, 0:cols].astype(BF)
            r.G[p][k : k + rows, :] = src[near, 0:cols]

    flat = 2 * me + c
    arrived("wq", "wk", "wv")
    r.WQ[pl.ds(pl.multiple_of(me * 48, 16), 48), 0:384] = r.wq[...].astype(BF)
    r.WQ[pl.ds(pl.multiple_of(me * 48, 16), 48), 384:768] = r.wk[...].astype(BF)
    r.WQ[pl.ds(pl.multiple_of(me * 48, 16), 48), 768:1152] = r.wv[...].astype(BF)
    ag_own("Q")
    arrived("tok")
    send("tok", r.tok, r.X.at[own_rows, :], partner)
    local = pltpu.make_async_copy(r.tok, r.X.at[own_rows, :], r.ls.at[0])
    local.start()
    arrived("ga", "ba", "gf", "bf")
    r.VS[0:8, :] = jnp.zeros((8, 768), F32)
    for k, n in enumerate(("ga", "ba", "gf", "bf")):
        r.VS[k : k + 1, 0:24] = getattr(r, n)[...].reshape(1, 24).astype(BF).astype(F32)
    r.VS[0:8, :] = pltpu.roll(r.VS[0:8, :], 24 * flat, 1)
    vec_send(0, 0)
    arrived("wo")
    wo = r.wo[...]
    r.WOP[c, pl.ds(pl.multiple_of(me * 48, 16), 48), :] = jnp.concatenate(
        [wo[:, 0:384], wo[:, 384:768]], axis=0
    ).astype(BF)
    arrived("wu", "wd", "og")
    r.WU[pl.ds(pl.multiple_of(me * 96, 16), 96), :] = r.wu[...].astype(BF)
    r.WD[pl.ds(pl.multiple_of(me * 96, 16), 96), :] = r.wd[...].astype(BF)

    q_steps, o_steps, u_steps, d_steps = (ag_steps(p) for p in PIECES)
    run(q_steps[:5])
    ag_own("O")
    run(o_steps[:1])

    col_pos = lax.broadcasted_iota(jnp.int32, (512, 128), 0)
    row_pos = lax.broadcasted_iota(jnp.int32, (8, 512), 1)
    col_lab = jnp.zeros((512, 128), jnp.int32)
    row_lab = jnp.zeros((8, 512), jnp.int32)
    for j in range(8):
        lo = r.off[0, j]
        hi = lo + r.len[0, j]
        col_lab = jnp.where((col_pos >= lo) & (col_pos < hi), j + 1, col_lab)
        row_lab = jnp.where((row_pos >= lo) & (row_pos < hi), j + 1, row_lab)
    r.LIVE[...] = jnp.where(col_lab > 0, 1.0, 0.0).astype(F32)
    row_lab = jnp.where(row_lab > 0, row_lab, -1)
    for t in range(4):
        q = slice(128 * t, 128 * t + 128)
        lab = jnp.concatenate([col_lab[q]] * 4, axis=1)
        same = lab == jnp.broadcast_to(row_lab[0:1], (128, 512))
        r.BIAS[q, :] = jnp.where(same, 0.0, -1e30).astype(F32)

    run(q_steps[5:])
    vec_step(0, 0)
    run(o_steps[1:5])
    ag_own("U")
    wait_recv("tok", r.X.at[own_rows, :])
    local.wait()
    for zm in range(4):
        ag_plane("Q", zm)

    for k, n in enumerate(("Q3", "K3", "V3")):
        full = mm(r.X[...], r.WQ[:, 384 * k : 384 * k + 384])
        full = full.astype(BF)
        if k == 0:
            full = full * BF(0.125)
        for i in range(3):
            getattr(r, n)[i] = full[:, 128 * i : 128 * i + 128]
    run(u_steps[:1])
    vec_step(0, 1)

    for i in range(3):
        r.ATT[i] = jnp.zeros((512, 128), BF)
    fw_hooks = [
        o_steps[5:8],
        o_steps[8:],
        [functools.partial(vec_step, 0, 2)] + u_steps[1:3],
        u_steps[3:5],
        u_steps[5:8],
        [functools.partial(ag_own, "D")] + u_steps[8:10],
    ]
    lane = lax.broadcasted_iota(jnp.int32, (1, 128), 1)

    def half(val, a):
        keep = (lane >= 64 * a) & (lane < 64 * a + 64)
        return jnp.where(keep, val, jnp.zeros_like(val))

    def at_index(h, hooks):
        for k, steps in enumerate(hooks):

            def go(steps=steps):
                run(steps)

            pl.when(h == k)(go)

    def fwd_head(h, carry):
        at_index(h, fw_hooks)
        i = lax.div(h, 2)
        a = lax.rem(h, 2)
        vals = half(r.V3[i], a)
        keys = half(r.K3[i], a)
        for t in range(4):
            q = slice(128 * t, 128 * t + 128)
            s = mm(r.Q3[i, q, :], keys, 1, 1) + r.BIAS[q, :]
            live = r.LIVE[q, 0:1]
            top = jnp.where(live > 0, jnp.max(s, axis=1, keepdims=True), 0.0)
            w = jnp.exp(s - top)
            total = jnp.sum(w, axis=1, keepdims=True) + (1.0 - live)
            prob = w * (1.0 / total)
            r.P32[h, q, :] = prob
            o = mm(prob.astype(BF), vals)
            r.ATT[i, q, :] = r.ATT[i, q, :] + o.astype(BF)
        return carry

    lax.fori_loop(0, 6, fwd_head, 0)

    send("att", r.ATT.at[:, oth_rows, :], r.ATTR, partner)
    for zm in range(4):
        ag_plane("O", zm)
    send("wop", r.WOP.at[c], r.WOP.at[c], partner)
    run(d_steps[:1] + u_steps[10:12])
    vec_step(0, 3)
    wait_recv("wop", r.WOP.at[1 - c])

    def build_out(i, carry):
        for k in range(2):
            blk = r.WOP[k, pl.ds(pl.multiple_of(48 * i, 16), 48), :].astype(F32)
            rows = jnp.concatenate([blk[0:24], blk[24:48]], axis=1)
            r.T[pl.ds(pl.multiple_of(48 * i + 24 * k, 8), 24), 0:768] = rows
        return carry

    lax.fori_loop(0, 16, build_out, 0)
    r.WO[...] = r.T[:, 0:768].astype(BF)
    wait_recv("att", r.ATTR)
    own_heads = pl.ds(pl.multiple_of(384 * c, 128), 384)
    oth_heads = pl.ds(pl.multiple_of(384 * (1 - c), 128), 384)

    def joined(ref, rows):
        return jnp.concatenate([ref[i, rows, :] for i in range(3)], axis=1)

    all256 = pl.ds(0, 256)
    branch = mm(joined(r.ATT, own_rows), r.WO[own_heads, :])
    branch = branch + mm(joined(r.ATTR, all256), r.WO[oth_heads, :])
    r.GS[...] = branch
    run(u_steps[12:] + d_steps[1:2])

    def norm(val):
        mean = jnp.mean(val, axis=1, keepdims=True)
        cen = val - mean
        inv = lax.rsqrt(jnp.mean(cen * cen, axis=1, keepdims=True) + EPS)
        return cen * inv, inv

    def ln1(t, carry):
        q = pl.ds(pl.multiple_of(64 * t, 64), 64)
        unit, inv = norm(r.tok[q, :].astype(F32) + r.GS[q, :])
        r.U1[q, :] = unit
        r.INV1[q, :] = jnp.broadcast_to(inv, (64, 128))
        one = unit * r.VS[40:41, :] + r.VS[41:42, :]
        r.N1[q, :] = one
        r.FIN[pl.ds(pl.multiple_of(base256 + 64 * t, 64), 64), :] = one.astype(BF)
        return carry

    lax.fori_loop(0, 4, ln1, 0)
    send("fin", r.FIN.at[own_rows, :], r.FIN.at[own_rows, :], partner)
    run(d_steps[2:5])
    wait_recv("fin", r.FIN.at[oth_rows, :])

    def plane_rows(zm):
        return pl.ds(pl.multiple_of(384 * zs[zm], 128), 384)

    def ffn_up(zm):
        for t in range(2):
            q = slice(256 * t, 256 * t + 256)
            pre = mm(r.FIN[q, :], r.WU[plane_rows(zm), :], 1, 1)
            r.GEL[zm, q, :] = pre

        def act(t, carry):
            q = pl.ds(pl.multiple_of(64 * t, 64), 64)
            pre = r.GEL[zm, q, :]
            cdf = 0.5 * (1.0 + lax.erf(pre * (2.0**-0.5)))
            pdf = jnp.exp(-0.5 * pre * pre) * (1.0 / math.sqrt(2.0 * math.pi))
            r.HID[zm, q, :] = (pre * cdf).astype(BF)
            r.GEL[zm, q, :] = cdf + pre * pdf
            return carry

        lax.fori_loop(0, 8, act, 0)

    d_groups = ([], d_steps[5:8], d_steps[8:11], d_steps[11:])
    for zm in range(4):
        ag_plane("U", zm)
        run(d_groups[zm])
        ffn_up(zm)
    for zm in range(4):
        ag_plane("D", zm)
        for rows in (oth_rows, own_rows):
            part = mm(r.HID[zm, rows, :], r.WD[plane_rows(zm), :])
            if zm:
                part = part + r.SEC[rows, :]
            r.SEC[rows, :] = part
            if zm == 3 and rows is oth_rows:
                for h in range(2):
                    part_rows = pl.ds(pl.multiple_of(256 * (1 - c) + 128 * h, 128), 128)
                    send(("sec", h), r.SEC.at[part_rows, :], r.SECR.at[pl.ds(128 * h, 128), :], partner)

    def ln2(t, sums):
        dg, db = sums
        q = pl.ds(pl.multiple_of(64 * t, 64), 64)
        qq = pl.ds(pl.multiple_of(base256 + 64 * t, 64), 64)
        unit, inv = norm(r.N1[q, :] + (r.SEC[qq, :] + r.SECR[q, :]))
        gain = r.VS[42:43, :]
        r.out[q, :] = (unit * gain + r.VS[43:44, :]).astype(BF)
        e = r.og[q, :].astype(F32)
        dg = dg + jnp.sum(e * unit, axis=0, keepdims=True)
        db = db + jnp.sum(e, axis=0, keepdims=True)
        eg = e * gain
        inner = jnp.mean(eg * unit, axis=1, keepdims=True)
        gs = inv * (eg - jnp.mean(eg, axis=1, keepdims=True) - unit * inner)
        r.GS[q, :] = gs
        r.GFB[qq, :] = gs.astype(BF)
        return dg, db

    zero = jnp.zeros((1, 768), F32)
    dg2, db2 = zero, zero
    for h in range(2):
        wait_recv(("sec", h), r.SECR.at[pl.ds(128 * h, 128), :])
        dg2, db2 = lax.fori_loop(2 * h, 2 * h + 2, ln2, (dg2, db2))
        part_rows = r.GFB.at[pl.ds(pl.multiple_of(base256 + 128 * h, 128), 128), :]
        send(("gfb", h), part_rows, part_rows, partner)
    put("out")
    r.T[0:384, 0:768] = mm(r.HID[3, own_rows, :], r.GFB[own_rows, :], 0, 0)
    for h in range(2):
        wait_recv(("gfb", h), r.GFB.at[pl.ds(pl.multiple_of(256 * (1 - c) + 128 * h, 128), 128), :])
    for h in range(2):
        wait_sent(("sec", h))

    for n_done, zm in enumerate((3, 2, 1, 0)):
        if zm == 3:
            r.T[0:384, 0:768] = r.T[0:384, 0:768] + mm(r.HID[3, oth_rows, :], r.GFB[oth_rows, :], 0, 0)
        else:
            r.T[0:384, 0:768] = mm(r.HID[zm], r.GFB[...], 0, 0)
        stage("D", zm, r.T, 0)
        if zm > 1:
            rs1_send("D", zm)
        for t in range(2):
            q = slice(256 * t, 256 * t + 256)
            gh = mm(r.GFB[q, :], r.WD[plane_rows(zm), :], 1, 1)
            r.HID[zm, q, :] = (gh * r.GEL[zm, q, :]).astype(BF)
        r.T[384:768, 0:768] = mm(r.HID[zm], r.FIN[...], 0, 0)
        stage("U", zm, r.T, 384)
        if zm > 1:
            rs1_send("U", zm)
        for rows in (oth_rows, own_rows):
            part = mm(r.HID[zm, rows, :], r.WU[plane_rows(zm), :])
            if n_done:
                part = part + r.SEC[rows, :]
            r.SEC[rows, :] = part
            if n_done == 3 and rows is oth_rows:
                send("gn", r.SEC.at[oth_rows, :], r.SECR, partner)
        if n_done == 2:
            rs_sum1("D", 3)
    rs1_send("D", 1)
    rs_sum1("U", 3)
    wait_recv("gn", r.SECR)

    def ln1_back(t, sums):
        dg, db = sums
        q = pl.ds(pl.multiple_of(64 * t, 64), 64)
        qq = pl.ds(pl.multiple_of(base256 + 64 * t, 64), 64)
        e = r.GS[q, :] + (r.SEC[qq, :] + r.SECR[q, :])
        unit = r.U1[q, :]
        inv = r.INV1[q, 0:1]
        dg = dg + jnp.sum(e * unit, axis=0, keepdims=True)
        db = db + jnp.sum(e, axis=0, keepdims=True)
        eg = e * r.VS[40:41, :]
        inner = jnp.mean(eg * unit, axis=1, keepdims=True)
        first = inv * (eg - jnp.mean(eg, axis=1, keepdims=True) - unit * inner)
        r.GS[q, :] = first
        r.GB[q, :] = first.astype(BF)
        return dg, db

    dg1, db1 = lax.fori_loop(0, 4, ln1_back, (zero, zero))
    r.VS[48:56, :] = jnp.zeros((8, 768), F32)
    for k, val in enumerate((dg1, db1, dg2, db2)):
        r.VS[48 + k : 49 + k, :] = val
    vec_send(1, 0)

    gview = mm(r.GB[...], r.WO[oth_heads, :], 1, 1).astype(BF)
    for i in range(3):
        r.GAS[i] = gview[:, 128 * i : 128 * i + 128]
    send("gas", r.GAS, r.GA.at[:, own_rows, :], partner)
    gview = mm(r.GB[...], r.WO[own_heads, :], 1, 1).astype(BF)
    for i in range(3):
        r.GA[i, own_rows, :] = gview[:, 128 * i : 128 * i + 128]
    vec_step(1, 0)
    rs_sum2a("D", 3)
    rs1_send("U", 1)
    r.T[own_heads, 0:768] = mm(joined(r.ATT, own_rows), r.GB[...], 0, 0)
    r.T[oth_heads, 0:768] = mm(joined(r.ATTR, all256), r.GB[...], 0, 0)

    def pair_out(i, carry):
        q = pl.ds(pl.multiple_of(48 * i, 16), 48)
        blk = r.T[pl.ds(pl.multiple_of(48 * i + other24, 8), 24), 0:768]
        r.S0[q, :] = jnp.concatenate([blk[:, 0:384], blk[:, 384:768]], axis=0).astype(BF)
        return carry

    lax.fori_loop(0, 16, pair_out, 0)
    send("s0", r.S0, r.R0, partner)
    rs_sum1("D", 2)
    rs_sum2a("U", 3)
    wait_recv("s0", r.R0)

    def out_block(m):
        i = ids[m]
        blk = r.T[pl.ds(pl.multiple_of(48 * i + base24, 8), 24), 0:768]
        blk = jnp.concatenate([blk[:, 0:384], blk[:, 384:768]], axis=0)
        return blk + r.R0[pl.ds(pl.multiple_of(48 * i, 16), 48), :].astype(F32)

    for zm in (3, 2, 1, 0):
        for du in (1, 0):
            k = (2 * zm + du) * 48
            r.S1["O"][k : k + 48, :] = out_block(4 * zm + 2 * du + 1).astype(BF)
            r.G["O"][k : k + 48, :] = out_block(4 * zm + 2 * du)
        if zm > 1:
            rs1_send("O", zm)

    wait_recv("gas", r.GA.at[:, oth_rows, :])
    for n in ("DQ", "DK", "DV"):
        for i in range(3):
            getattr(r, n)[i] = jnp.zeros((512, 128), BF)

    def s1(p, zm):
        return functools.partial(rs_sum1, p, zm)

    def s2a(p, zm):
        return functools.partial(rs_sum2a, p, zm)

    def s2c(p):
        return functools.partial(rs_sum2c, p)

    def vs(s):
        return functools.partial(vec_step, 1, s)

    bw_hooks = [
        [],
        [s1("U", 2)],
        [s2a("D", 2)],
        [],
        [s1("D", 1)],
        [s2a("U", 2), vs(1)],
    ]

    def bwd_head(h, carry):
        at_index(h, bw_hooks)
        i = lax.div(h, 2)
        a = lax.rem(h, 2)
        go = half(r.GA[i], a)
        for t in range(4):
            q = slice(128 * t, 128 * t + 128)
            prob = r.P32[h, q, :]
            dp = mm(go[q], r.V3[i], 1, 1)
            delta = jnp.sum(prob * dp, axis=1, keepdims=True)
            r.DSB[q, :] = (prob * (dp - delta)).astype(BF)
            r.PB[q, :] = prob.astype(BF)
        r.DV[i] = r.DV[i] + mm(r.PB[...], go, 0, 0).astype(BF)
        dq = mm(r.DSB[...], half(r.K3[i], a)) * 0.125
        r.DQ[i] = r.DQ[i] + dq.astype(BF)
        dk = mm(r.DSB[...], half(r.Q3[i], a), 0, 0)
        r.DK[i] = r.DK[i] + dk.astype(BF)
        return carry

    lax.fori_loop(0, 6, bwd_head, 0)

    all512 = pl.ds(0, 512)
    for k, n in enumerate(("DQ", "DK", "DV")):
        r.T[:, 384 * k : 384 * k + 384] = mm(r.X[...], joined(getattr(r, n), all512), 0, 0)
    for zm in (3, 2, 1, 0):
        stage("Q", zm, r.T, 192 * zs[zm])
        if zm > 1:
            rs1_send("Q", zm)

    def s0(p, zm):
        return functools.partial(rs1_send, p, zm)

    run([s1("U", 1), s2a("D", 1), vs(2), s0("Q", 1), s0("O", 1)])

    for rows in (oth_rows, own_rows):
        acc = mm(joined(r.DQ, rows), r.WQ[:, 0:384], 1, 1)
        acc = acc + mm(joined(r.DK, rows), r.WQ[:, 384:768], 1, 1)
        acc = acc + mm(joined(r.DV, rows), r.WQ[:, 768:1152], 1, 1)
        if rows is oth_rows:
            r.IGS[...] = acc.astype(BF)
            send("ig", r.IGS, r.IGR, partner)
            run([s1("O", 3), s1("O", 2), s2a("U", 1), s2a("O", 3), s0("D", 0)])
        else:
            r.GS[...] = r.GS[...] + acc
    wait_recv("ig", r.IGR)
    r.ig[...] = (r.GS[...] + r.IGR[...].astype(F32)).astype(BF)
    put("ig")

    run([s1("Q", 3), s2a("O", 2), s0("U", 0), s1("Q", 2), s2a("Q", 3), s0("Q", 0)])
    run([s1("Q", 1), s2a("Q", 2), s1("O", 1), s2a("Q", 1), s1("D", 0), s2a("O", 1), s2c("D")])
    run([s1("U", 0), s2c("U"), s2a("D", 0), s0("O", 0), s1("Q", 0), s2c("Q"), s2a("U", 0)])
    run([s2a("Q", 0), s1("O", 0), s2c("O"), s2a("O", 0)])
    rs_final("Q")
    r.dwq[...] = r.G["Q"][0:48, 0:384]
    r.dwk[...] = r.G["Q"][0:48, 384:768]
    r.dwv[...] = r.G["Q"][0:48, 768:1152]
    rs_final("D")
    r.dwd[...] = r.G["D"][0:96, :]
    put("dwq", "dwk", "dwv", "dwd")
    rs_final("U")
    r.dwu[...] = r.G["U"][0:96, :]
    rs_final("O")
    vec_step(1, 3)
    go = r.G["O"][0:48, :]
    r.dwo[...] = jnp.concatenate([go[0:24], go[24:48]], axis=1)
    back = pltpu.roll(r.VS[88:96, :], lax.rem(768 - 24 * flat, 768), 1)
    for k, n in enumerate(("dga", "dba", "dgf", "dbf")):
        getattr(r, n)[...] = back[k, 0:24]
    put("dwu", "dwo", "dga", "dba", "dgf", "dbf")

    for src, out, key in sends:
        if out in waited:
            continue
        waited.add(out)
        if out[0] == "one":
            ref = src
        elif out[0] == "ag":
            count = sum(o == out for _, o, _ in sends)
            n_rows = APART[out[1]] if out[2] == "A" else ROWS[out[1]] - APART[out[1]]
            ref = wbuf(out[1]).at[pl.ds(0, count * n_rows), :]
        else:
            ref = getattr(r, out[0])[out[1]]
        wait_send(out, ref)
    assert len(send_ids) == SENT and len(recv_ids) == RECEIVED, (len(send_ids), len(recv_ids))
    for cp in out_copies:
        cp.wait()


def hand_over(*refs):
    n = len(MOVED_OUT)
    srcs, dsts, bufs, sems = refs[:n], refs[n : 2 * n], refs[2 * n : 3 * n], refs[3 * n]
    reads = [pltpu.make_async_copy(srcs[k], bufs[k], sems.at[k]) for k in range(n)]
    writes = [pltpu.make_async_copy(bufs[k], dsts[k], sems.at[n + k]) for k in range(n)]
    for cp in reads:
        cp.start()
    for rd, wr in zip(reads, writes):
        rd.wait()
        wr.start()
    for cp in writes:
        cp.wait()


def layer_small(*args):
    shapes = tuple((shape, dtype) for _, shape, dtype in MOVED_OUT)
    smem = pl.BlockSpec(memory_space=pltpu.SMEM)
    anywhere = pl.BlockSpec(memory_space=pl.ANY)
    out_shape = tuple(jax.ShapeDtypeStruct(s, d) for s, d in shapes)
    up = IN_NAMES.index("wu")
    args = args[:up] + (args[up].T,) + args[up + 1 :]
    outs = pl.pallas_call(
        layer_kernel,
        out_shape=out_shape,
        in_specs=[smem if n in ("len", "off") else anywhere for n in IN_NAMES],
        out_specs=tuple(anywhere for _ in shapes),
        scratch_shapes=[s for _, s in scratch_list()],
        compiler_params=pltpu.CompilerParams(
            collective_id=0, has_side_effects=True, vmem_limit_bytes=67043328
        ),
    )(*args)
    outs = pl.pallas_call(
        hand_over,
        out_shape=out_shape,
        in_specs=[anywhere for _ in shapes],
        out_specs=tuple(anywhere for _ in shapes),
        scratch_shapes=[pltpu.VMEM(shape, dtype) for shape, dtype in shapes]
        + [pltpu.SemaphoreType.DMA((2 * len(shapes),))],
    )(*outs)
    up = OUT_NAMES.index("dwu")
    return outs[:up] + (outs[up].T,) + outs[up + 1 :]


def labels_of(lengths, offsets):
    position = jnp.arange(BIN, dtype=jnp.int32)[:, None]
    starts = offsets[None, :]
    inside = (position >= starts) & (position < starts + lengths[None, :])
    slot_order = jnp.arange(1, lengths.shape[0] + 1, dtype=jnp.int32)[None, :]
    return jnp.sum(jnp.where(inside, slot_order, 0), axis=1)


def layer_norm(operand, gain_vec, bias_vec):
    row_mean = jnp.mean(operand, axis=-1, keepdims=True)
    centered = operand - row_mean
    inverse = lax.rsqrt(jnp.mean(centered * centered, axis=-1, keepdims=True) + EPS)
    normed = centered * inverse
    return (normed * gain_vec + bias_vec, normed, inverse)


def norm_back(grad_rows, normed, inverse, gain_vec):
    scaled = grad_rows * gain_vec
    inner = jnp.mean(scaled * normed, axis=-1, keepdims=True)
    return inverse * (scaled - jnp.mean(scaled, axis=-1, keepdims=True) - normed * inner)


def gelu_exact(operand):
    return jax.nn.gelu(operand, approximate=False)


def contract_rows(left, right):
    return lax.dot_general(
        left, right, (((0,), (0,)), ((), ())), preferred_element_type=F32
    )


def contract_cols(left, right):
    return lax.dot_general(
        left, right, (((1,), (1,)), ((), ())), preferred_element_type=F32
    )


def score_block(queries, key_rows, labels_bin, factor):
    scores = (
        jnp.einsum("qhd,khd->hqk", queries, key_rows, preferred_element_type=F32) * factor
    )
    allowed = ((labels_bin[:, None] == labels_bin[None, :]) & (labels_bin[:, None] > 0))[None]
    live_rows = (labels_bin > 0)[None, :, None]
    return (scores, allowed, live_rows)


def masked_exp(scores, allowed, row_top):
    return jnp.where(allowed, jnp.exp(jnp.where(allowed, scores - row_top, 0.0)), 0.0)


def attend_bin(pieces, factor):
    queries, key_rows, value_rows, labels_bin = pieces
    scores, allowed, live_rows = score_block(queries, key_rows, labels_bin, factor)
    row_top = jnp.max(jnp.where(allowed, scores, -1e30), axis=2, keepdims=True)
    row_top = jnp.where(live_rows, row_top, 0.0)
    weights = masked_exp(scores, allowed, row_top)
    denominator = jnp.sum(weights, axis=2, keepdims=True) + jnp.where(live_rows, 0.0, 1.0)
    probability = (weights / denominator).astype(jnp.bfloat16)
    mixed_rows = jnp.einsum(
        "hqk,khd->qhd", probability, value_rows, preferred_element_type=F32
    )
    return (mixed_rows.astype(jnp.bfloat16), row_top, denominator)


def attend_back(pieces, factor):
    queries, key_rows, value_rows, labels_bin, row_top, denominator, grad_mixed = pieces
    scores, allowed, live_rows = score_block(queries, key_rows, labels_bin, factor)
    probability = masked_exp(scores, allowed, row_top) / denominator
    grad_values = jnp.einsum(
        "hqk,qhd->khd",
        probability.astype(jnp.bfloat16),
        grad_mixed,
        preferred_element_type=F32,
    )
    grad_probs = jnp.einsum(
        "qhd,khd->hqk", grad_mixed, value_rows, preferred_element_type=F32
    )
    row_delta = jnp.sum(probability * grad_probs, axis=2, keepdims=True)
    grad_scores = (probability * (grad_probs - row_delta)).astype(jnp.bfloat16)
    grad_queries = (
        jnp.einsum("hqk,khd->qhd", grad_scores, key_rows, preferred_element_type=F32)
        * factor
    )
    grad_keys = (
        jnp.einsum("hqk,qhd->khd", grad_scores, queries, preferred_element_type=F32)
        * factor
    )
    return (
        grad_queries.astype(jnp.bfloat16),
        grad_keys.astype(jnp.bfloat16),
        grad_values.astype(jnp.bfloat16),
    )


def per_device(
    tokens,
    w_query,
    w_key,
    w_value,
    w_out,
    gain_attn,
    bias_attn,
    w_up,
    w_down,
    gain_ffn,
    bias_ffn,
    seq_lengths,
    seq_offsets,
    out_grad,
):
    low_type = jnp.bfloat16
    bin_count = seq_lengths.shape[0]
    group_rows = bin_count * BIN
    head_width = w_query.shape[1]
    local_heads = head_width // HD
    factor = 1.0 / math.sqrt(HD)
    labels = jax.vmap(labels_of)(seq_lengths, seq_offsets)
    full_query, full_key, full_value = (
        lax.all_gather(w_query.astype(low_type), DP, axis=0, tiled=True),
        lax.all_gather(w_key.astype(low_type), DP, axis=0, tiled=True),
        lax.all_gather(w_value.astype(low_type), DP, axis=0, tiled=True),
    )
    projection = jnp.concatenate([full_query, full_key, full_value], axis=1)
    whole_rows = lax.all_gather(tokens, HEAD, axis=0, tiled=True)
    projected = jnp.dot(whole_rows, projection, preferred_element_type=F32).astype(low_type)
    shape_bins = (bin_count, BIN, local_heads, HD)
    queries = projected[:, :head_width].reshape(shape_bins)
    key_rows = projected[:, head_width : 2 * head_width].reshape(shape_bins)
    value_rows = projected[:, 2 * head_width :].reshape(shape_bins)
    mixed_bins, row_tops, denominators = lax.map(
        lambda pieces: attend_bin(pieces, factor), (queries, key_rows, value_rows, labels)
    )
    attended = mixed_bins.reshape(group_rows, head_width)
    out_full, up_part, down_part, gain_one, bias_one, gain_two, bias_two = (
        lax.all_gather(w_out.astype(low_type), BOTH, axis=0, tiled=True),
        lax.all_gather(w_up.astype(low_type), BOTH, axis=1, tiled=True),
        lax.all_gather(w_down.astype(low_type), BOTH, axis=0, tiled=True),
        lax.all_gather(gain_attn.astype(low_type), BOTH, axis=0, tiled=True),
        lax.all_gather(bias_attn.astype(low_type), BOTH, axis=0, tiled=True),
        lax.all_gather(gain_ffn.astype(low_type), BOTH, axis=0, tiled=True),
        lax.all_gather(bias_ffn.astype(low_type), BOTH, axis=0, tiled=True),
    )
    gain_first = gain_one.astype(F32)
    gain_second = gain_two.astype(F32)
    token_view = lax.all_to_all(attended, HEAD, split_axis=0, concat_axis=1, tiled=True)
    first_sum = tokens.astype(F32) + jnp.dot(
        token_view, out_full, preferred_element_type=F32
    )
    normed_one, unit_one, inverse_one = layer_norm(
        first_sum, gain_first, bias_one.astype(F32)
    )
    ffn_input = normed_one.astype(low_type)
    pre_act = jnp.dot(ffn_input, up_part, preferred_element_type=F32)
    activated, gelu_pull = jax.vjp(gelu_exact, pre_act)
    hidden = activated.astype(low_type)
    second_sum = normed_one + jnp.dot(hidden, down_part, preferred_element_type=F32)
    result, unit_two, inverse_two = layer_norm(
        second_sum, gain_second, bias_two.astype(F32)
    )
    output = result.astype(low_type)
    grad_result = out_grad.astype(F32)
    grad_gain_two = jnp.sum(grad_result * unit_two, axis=0)
    grad_bias_two = jnp.sum(grad_result, axis=0)
    grad_second = norm_back(grad_result, unit_two, inverse_two, gain_second)
    grad_ffn = grad_second.astype(low_type)
    grad_down_part = contract_rows(hidden, grad_ffn)
    grad_pre = gelu_pull(contract_cols(grad_ffn, down_part))[0].astype(low_type)
    grad_up_part = contract_rows(ffn_input, grad_pre)
    grad_normed = grad_second + contract_cols(grad_pre, up_part)
    grad_gain_one = jnp.sum(grad_normed * unit_one, axis=0)
    grad_bias_one = jnp.sum(grad_normed, axis=0)
    grad_first = norm_back(grad_normed, unit_one, inverse_one, gain_first)
    grad_branch = grad_first.astype(low_type)
    grad_out_full = contract_rows(token_view, grad_branch)
    part_out, part_up, part_down, part_gain_one, part_bias_one, part_gain_two, part_bias_two = (
        lax.psum_scatter(grad_out_full, BOTH, scatter_dimension=0, tiled=True),
        lax.psum_scatter(grad_up_part, BOTH, scatter_dimension=1, tiled=True),
        lax.psum_scatter(grad_down_part, BOTH, scatter_dimension=0, tiled=True),
        lax.psum_scatter(grad_gain_one, BOTH, scatter_dimension=0, tiled=True),
        lax.psum_scatter(grad_bias_one, BOTH, scatter_dimension=0, tiled=True),
        lax.psum_scatter(grad_gain_two, BOTH, scatter_dimension=0, tiled=True),
        lax.psum_scatter(grad_bias_two, BOTH, scatter_dimension=0, tiled=True),
    )
    grad_token_view = contract_cols(grad_branch, out_full).astype(low_type)
    grad_attended = lax.all_to_all(grad_token_view, HEAD, split_axis=1, concat_axis=0, tiled=True)
    grad_bins = grad_attended.reshape(shape_bins)
    grad_queries, grad_keys, grad_values = lax.map(
        lambda pieces: attend_back(pieces, factor),
        (queries, key_rows, value_rows, labels, row_tops, denominators, grad_bins),
    )
    grad_projected = jnp.concatenate(
        [
            grad_queries.reshape(group_rows, head_width),
            grad_keys.reshape(group_rows, head_width),
            grad_values.reshape(group_rows, head_width),
        ],
        axis=1,
    )
    grad_projection = contract_rows(whole_rows, grad_projected)
    part_query, part_key, part_value = (
        lax.psum_scatter(grad_projection[:, :head_width], DP, scatter_dimension=0, tiled=True),
        lax.psum_scatter(
            grad_projection[:, head_width : 2 * head_width], DP, scatter_dimension=0, tiled=True
        ),
        lax.psum_scatter(
            grad_projection[:, 2 * head_width :], DP, scatter_dimension=0, tiled=True
        ),
    )
    input_grad = (
        grad_first
        + lax.psum_scatter(
            contract_cols(grad_projected, projection).astype(jnp.bfloat16),
            HEAD,
            scatter_dimension=0,
            tiled=True,
        ).astype(F32)
    ).astype(low_type)
    return (
        output,
        input_grad,
        part_query,
        part_key,
        part_value,
        part_out,
        part_gain_one,
        part_bias_one,
        part_up,
        part_down,
        part_gain_two,
        part_bias_two,
    )


def solution(mesh):
    small = mesh.shape[DP] == 16 and mesh.shape[HEAD] == 2
    return jax.shard_map(
        layer_small if small else per_device,
        mesh=mesh,
        in_specs=(
            P(BOTH, None),
            P(DP, HEAD),
            P(DP, HEAD),
            P(DP, HEAD),
            P(BOTH, None),
            P(BOTH),
            P(BOTH),
            P(None, BOTH),
            P(BOTH, None),
            P(BOTH),
            P(BOTH),
            P(DP, None),
            P(DP, None),
            P(BOTH, None),
        ),
        out_specs=(
            P(BOTH, None),
            P(BOTH, None),
            P(DP, HEAD),
            P(DP, HEAD),
            P(DP, HEAD),
            P(BOTH, None),
            P(BOTH),
            P(BOTH),
            P(None, BOTH),
            P(BOTH, None),
            P(BOTH),
            P(BOTH),
        ),
        check_vma=False,
    )
```
